256 devices in a mesh: gx: 4 (over x), gy: 16 (over y_hi, z), gz: 4 (over y_lo, core).
Axes of the slice: x: 4, y: 4 (y_hi: 2, y_lo: 2; y = y_hi * 2 + y_lo), z: 8, core: 2. Of those that a mesh axis runs over, the one named last changes fastest.
Arguments:
- acoustic_iterate: float32 [2, 32, 512, 1024], P(None, 'gx', 'gy', 'gz'), may hold values from -6 to 6
- coarse_update: float32 [2, 16, 256, 512], P(None, 'gx', 'gy', 'gz'), may hold values from -6 to 6
- class_codes_volume: int32 [32, 512, 1024], P('gx', 'gy', 'gz'), may hold values from 0 to 3
- element_location: int32 [1024, 3], replicated, may hold values from 0 to 1023, as said below
- element_excitation: float32 [2, 1024], replicated, may hold values from -24 to 24
- class_wavespeed: float32 [4], replicated, may hold values from 1 to 2
- class_damping: float32 [4], replicated, may hold values from 0.2 to 1
- washout_fraction: float32 [4], replicated, may hold values from 0.005 to 0.05
- thermal_excess: float32 [16, 256, 512], P('gx', 'gy', 'gz'), may hold values from 12 to 22
- injury_integral: float32 [16, 256, 512], P('gx', 'gy', 'gz'), may hold values from 0.01 to 1
Outputs:
- pressure_out: float32 [2, 32, 512, 1024], P(None, 'gx', 'gy', 'gz')
- temperature_out: float32 [16, 256, 512], P('gx', 'gy', 'gz')
- log_dose: float32 [16, 256, 512], P('gx', 'gy', 'gz')
The draws below stay inside these ranges and needn't reach their ends.
Inputs may be any that keep to these rules, and one draw needn't show every extreme that they name: `element_location`: each row holds the first, second and third grid index of one element's cell, below 32, 512 and 1024 respectively; several elements may share a cell.
All inputs are finite; a program needn't handle non-finite values.
Results may differ from the reference program's by a relative error of at most 0.000035.
Values sent between devices are 32-bit elements; how exact they have to be, the bound alone decides.
No kernel may reach another device: no remote copies, remote signals or barrier semaphores. Data moves between devices by JAX's collectives and lax.ppermute only.
A program may use at most 128 MiB of HBM per device.

```python
import math
import jax
import jax.numpy as jnp
from jax import lax

ELEMS = 1024
LABELS = 4
SWEEPS = 2
STEPS = 4
MESH_POINTS_LEAD = 32
MESH_POINTS_MID = 512
MESH_POINTS_LAST = 1024


def draw_element_location(key, part):
    first_key, second_key, third_key = jax.random.split(key, 3)
    first = jax.random.randint(first_key, (ELEMS,), 0, MESH_POINTS_LEAD)
    second = jax.random.randint(second_key, (ELEMS,), 0, MESH_POINTS_MID)
    third = jax.random.randint(third_key, (ELEMS,), 0, MESH_POINTS_LAST)
    cells = jnp.stack([first, second, third], axis=1).astype(jnp.int32)
    cells = cells.at[0].set(jnp.zeros((3,), jnp.int32))
    corner = jnp.array([MESH_POINTS_LEAD - 1, MESH_POINTS_MID - 1, MESH_POINTS_LAST - 1], jnp.int32)
    cells = cells.at[ELEMS - 1].set(corner)
    return cells


def set_ends(values, key, smallest, top_value):
    index_at = [jax.random.randint(jax.random.fold_in(key, axis), (), 0, length) for axis, length in enumerate(values.shape)]
    main_axis = values.shape.index(max(values.shape))
    beside = index_at[:main_axis] + [(index_at[main_axis] + 1) % values.shape[main_axis]] + index_at[main_axis + 1:]
    return values.at[tuple(index_at)].set(smallest).at[tuple(beside)].set(top_value)


def block_levels(own_key, dims, pieces, smallest, largest):
    def one(axis_at, blocks):
        draws = jax.random.uniform(jax.random.fold_in(jax.random.fold_in(own_key, 6), axis_at), (blocks,), jnp.float32, smallest / len(pieces), largest / len(pieces))
        return jnp.repeat(jnp.exp(draws), dims[axis_at] // blocks).reshape((-1,) + (1,) * (len(dims) - axis_at - 1))

    factor_of = one(*pieces[0])
    for cut in pieces[1:]:
        factor_of = factor_of * one(*cut)
    return factor_of


def normal_values(key, extent, deviation, reach, shards=(), kind=jnp.bfloat16):
    entries = jax.random.normal(key, extent, jnp.float32) * deviation
    if len(shards) > 0:
        entries = block_levels(key, extent, shards, -0.22, 0.18) * entries
    return jnp.clip(entries, min=-reach, max=reach).astype(kind)


def setup_inputs(seed: int = 0) -> dict:
    key_list = jax.random.split(jax.random.key(seed), 11)
    acoustic_iterate = normal_values(key_list[0], (2, MESH_POINTS_LEAD, MESH_POINTS_MID, MESH_POINTS_LAST), 1.0, 6.0, ((1, 4), (2, 16), (3, 4)), jnp.float32)
    coarse_update = normal_values(key_list[1], (2, MESH_POINTS_LEAD // 2, MESH_POINTS_MID // 2, MESH_POINTS_LAST // 2), 1.0, 6.0, ((1, 4), (2, 16), (3, 4)), jnp.float32)
    class_codes_volume = set_ends(jax.random.randint(key_list[2], (MESH_POINTS_LEAD, MESH_POINTS_MID, MESH_POINTS_LAST), 0, LABELS), jax.random.fold_in(key_list[2], 1), 0, LABELS - 1).astype(jnp.int32)
    element_location = draw_element_location(jax.random.fold_in(key_list[10], 71), 0)
    element_excitation = normal_values(key_list[4], (2, ELEMS), 4.0, 24.0, (), jnp.float32)
    class_wavespeed = jnp.clip(jax.random.uniform(key_list[5], (LABELS,), jnp.float32, 1.0, 2.0), 1.0, 2.0)
    class_damping = jnp.clip(jax.random.uniform(key_list[6], (LABELS,), jnp.float32, 0.2, 1.0), 0.2, 1.0)
    washout_fraction = jnp.clip(jax.random.uniform(key_list[7], (LABELS,), jnp.float32, 0.005, 0.05), 0.005, 0.05)
    thermal_excess = jnp.clip(12.0 + 10.0 * jax.random.uniform(key_list[8], (MESH_POINTS_LEAD // 2, MESH_POINTS_MID // 2, MESH_POINTS_LAST // 2), jnp.float32) ** block_levels(key_list[8], (MESH_POINTS_LEAD // 2, MESH_POINTS_MID // 2, MESH_POINTS_LAST // 2), ((0, 4), (1, 16), (2, 4)), -0.2, 0.2), 12.0, 22.0)
    injury_integral = jnp.clip(jnp.exp(math.log(1.0) - 4.6051702 * jax.random.uniform(key_list[9], (MESH_POINTS_LEAD // 2, MESH_POINTS_MID // 2, MESH_POINTS_LAST // 2), jnp.float32) ** block_levels(key_list[9], (MESH_POINTS_LEAD // 2, MESH_POINTS_MID // 2, MESH_POINTS_LAST // 2), ((0, 4), (1, 16), (2, 4)), -0.2, 0.2)), 0.01, 1.0)
    return dict(acoustic_iterate=acoustic_iterate, coarse_update=coarse_update, class_codes_volume=class_codes_volume, element_location=element_location, element_excitation=element_excitation, class_wavespeed=class_wavespeed, class_damping=class_damping, washout_fraction=washout_fraction, thermal_excess=thermal_excess, injury_integral=injury_integral)


RELAXATION = 0.8
DAMPING_SHIFT = 0.5
DIFFUSION = 0.15
HEATING = 0.25
LN_PREFACTOR = 226.78
ENERGY_BARRIER = 75535.0
CORE_WARMTH = 310.15


def lookup(class_codes_volume, table):
    total = jnp.zeros(class_codes_volume.shape, table.dtype)
    for tissue in range(table.shape[0]):
        total = total + (class_codes_volume == tissue).astype(table.dtype) * table[tissue]
    return total


def neighbours(bordered_volume):
    total = bordered_volume[:, 2:, 1:-1, 1:-1] + bordered_volume[:, :-2, 1:-1, 1:-1]
    total = total + bordered_volume[:, 1:-1, 2:, 1:-1] + bordered_volume[:, 1:-1, :-2, 1:-1]
    return total + bordered_volume[:, 1:-1, 1:-1, 2:] + bordered_volume[:, 1:-1, 1:-1, :-2]


def jacobi(bordered_volume, diag_real, diag_imag, gain_real, gain_imag, source):
    wave_state = bordered_volume[:, 1:-1, 1:-1, 1:-1]
    beside_all = neighbours(bordered_volume)
    apply_real = diag_real * wave_state[0] - diag_imag * wave_state[1] - beside_all[0]
    apply_imag = diag_real * wave_state[1] + diag_imag * wave_state[0] - beside_all[1]
    resid_real = source[0] - apply_real
    resid_imag = source[1] - apply_imag
    new_real = wave_state[0] + gain_real * resid_real + gain_imag * resid_imag
    new_imag = wave_state[1] + gain_real * resid_imag - gain_imag * resid_real
    return jnp.stack([new_real, new_imag])


def prolong_axis(bordered_volume, axis):
    length = bordered_volume.shape[axis] - 2
    center = lax.slice_in_dim(bordered_volume, 1, length + 1, axis=axis)
    lower = lax.slice_in_dim(bordered_volume, 0, length, axis=axis)
    upper = lax.slice_in_dim(bordered_volume, 2, length + 2, axis=axis)
    even = 0.75 * center + 0.25 * lower
    odd = 0.75 * center + 0.25 * upper
    paired = jnp.stack([even, odd], axis=axis + 1)
    new_shape = list(center.shape)
    new_shape[axis] = 2 * length
    return paired.reshape(new_shape)


def prolong(bordered_volume):
    result = bordered_volume
    for axis in (1, 2, 3):
        result = prolong_axis(result, axis)
    return result


def restrict(fields):
    count, size_a, size_b, size_c = fields.shape
    blocks = fields.reshape(count, size_a // 2, 2, size_b // 2, 2, size_c // 2, 2)
    return jnp.sum(blocks, axis=(2, 4, 6)) * 0.125


def thermal_advance(bordered_volume, perf_coarse, power_coarse):
    centre = bordered_volume[1:-1, 1:-1, 1:-1]
    beside_all = neighbours(bordered_volume[None])[0]
    return centre + DIFFUSION * (beside_all - 6.0 * centre) - perf_coarse * centre + HEATING * power_coarse


def injury_kinetics(warming_excess):
    return jnp.exp(LN_PREFACTOR - ENERGY_BARRIER / (CORE_WARMTH + warming_excess))


def reference(acoustic_iterate, coarse_update, class_codes_volume, element_location, element_excitation, class_wavespeed, class_damping, washout_fraction, thermal_excess, injury_integral):
    speed_cells = lookup(class_codes_volume, class_wavespeed)
    atten_cells = lookup(class_codes_volume, class_damping)
    perf_cells = lookup(class_codes_volume, washout_fraction)
    wave = 1.0 / (speed_cells * speed_cells)
    diag_real = 6.0 - wave
    diag_imag = DAMPING_SHIFT * wave + atten_cells
    modulus = diag_real * diag_real + diag_imag * diag_imag
    gain_real = RELAXATION * diag_real / modulus
    gain_imag = RELAXATION * diag_imag / modulus
    source = jnp.zeros(acoustic_iterate.shape, acoustic_iterate.dtype)
    source = source.at[:, element_location[:, 0], element_location[:, 1], element_location[:, 2]].add(element_excitation)
    coarse = jnp.pad(coarse_update, ((0, 0), (1, 1), (1, 1), (1, 1)))
    wave_state = acoustic_iterate + prolong(coarse)
    for sweep_index in range(SWEEPS):
        bordered_volume = jnp.pad(wave_state, ((0, 0), (1, 1), (1, 1), (1, 1)))
        wave_state = jacobi(bordered_volume, diag_real, diag_imag, gain_real, gain_imag, source)
    power = atten_cells * (wave_state[0] * wave_state[0] + wave_state[1] * wave_state[1])
    coarsened_volumes = restrict(jnp.stack([power, perf_cells]))
    warming_excess = thermal_excess
    injury_gain = injury_integral
    for step_index in range(STEPS):
        warming_excess = thermal_advance(jnp.pad(warming_excess, 1), coarsened_volumes[1], coarsened_volumes[0])
        injury_gain = injury_gain + injury_kinetics(warming_excess)
    return wave_state, warming_excess, jnp.log(injury_gain)
```

```python
import jax
import jax.numpy as jnp
from jax import lax
from jax.experimental import pallas as pl
from jax.experimental.pallas import tpu as pltpu
from jax.sharding import PartitionSpec as P

F32 = jnp.float32
BF16 = jnp.bfloat16

RELAXATION = 0.8
DAMPING_SHIFT = 0.5
DIFFUSION = 0.15
HEATING = 0.25
LN_PREFACTOR = 226.78
ENERGY_BARRIER = 75535.0
CORE_WARMTH = 310.15

FX, CX, LX, TX, QX = 12, 10, 8, 12, 10
XB_CODE, XB_COARSE, XB_THERM, XB = 128, 160, 192, 256
YB_CODE, YB_COARSE, YB_THERM, YB = 192, 272, 336, 384
WIDE = 2 * FX * 48 + CX * 48
N_CODE = 2 * FX * 48
N_COARSE, N_THETA, N_PERF, NARROW = 0, 512, 800, 1056
GROUPS = 16
ZB = (WIDE + NARROW) // GROUPS


def vmem():
    return pl.BlockSpec(memory_space=pltpu.VMEM)


def smem():
    return pl.BlockSpec(memory_space=pltpu.SMEM)


def exchange(up, down, axis):
    n = lax.axis_size(axis)
    ahead = [(i, (i + 1) % n) for i in range(n)]
    back = [(j, i) for i, j in ahead]
    return lax.ppermute(up, axis, ahead), lax.ppermute(down, axis, back)


def exact_dot(values, weights):
    high = values.astype(BF16)
    rest = values - high.astype(F32)
    mid = rest.astype(BF16)
    low = (rest - mid.astype(F32)).astype(BF16)
    total = jnp.dot(high, weights, preferred_element_type=F32)
    total = total + jnp.dot(mid, weights, preferred_element_type=F32)
    return total + jnp.dot(low, weights, preferred_element_type=F32)


def iota(shape, dim):
    return lax.broadcasted_iota(jnp.int32, shape, dim)


def pick(codes, entries):
    value = jnp.where(codes == 0.0, entries[0], entries[1])
    value = jnp.where(codes == 2.0, entries[2], value)
    return jnp.where(codes == 3.0, entries[3], value)


def pack_x(wash, it, co, codes, theta, up, down, perf, pool):
    lane, col = iota((256, 128), 0), iota((256, 128), 1)
    pairs = jnp.where(lane // 2 == col, 1.0, 0.0).astype(BF16)
    entries = [wash[k] for k in range(4)]
    for i in range(4):
        both = pick(codes[2 * i].astype(F32), entries) + pick(codes[2 * i + 1].astype(F32), entries)
        for half in range(2):
            pool[half, i * 32 : i * 32 + 32, :] = both[:, half * 128 : half * 128 + 128]
    rows = jnp.concatenate([pool[h, pl.ds(0, 64, 2), :] + pool[h, pl.ds(1, 64, 2), :] for h in range(2)], axis=1)
    washed = exact_dot(rows, pairs) * 0.125
    for i in range(4):
        perf[i] = washed[i * 16 : i * 16 + 16]
    for ref, fine, coarse in ((up, 6, 2), (down, 0, 0)):
        for c in range(2):
            for k in range(2):
                ref[pl.ds((c * 2 + k) * 32, 32), :] = it[c, fine + k]
        ref[pl.ds(XB_CODE, 32), :] = codes[7 if fine else 0].astype(F32)
        for k in range(2):
            for c in range(2):
                ref[pl.ds(XB_COARSE + 16 * k, 16), pl.ds(128 * c, 128)] = co[c, coarse + k]
        for i in range(4):
            ref[pl.ds(XB_THERM + 16 * i, 16), pl.ds(0, 128)] = theta[i]
            ref[pl.ds(XB_THERM + 16 * i, 16), pl.ds(128, 128)] = washed[i * 16 : i * 16 + 16]


class Columns:
    def __init__(self, it, co, codes, theta, perf, before, after):
        self.it, self.co, self.codes, self.theta, self.perf = it, co, codes, theta, perf
        self.before, self.after = before, after

    def iterate(self, c, f, rows):
        at, n = rows
        if 2 <= f < 10:
            return self.it[c, f - 2, pl.ds(at, n), :]
        ref, k = (self.before, f) if f < 2 else (self.after, f - 10)
        return ref[pl.ds((c * 2 + k) * 32 + at, n), :]

    def code(self, f, rows):
        at, n = rows
        if 1 <= f < 9:
            return self.codes[f - 1, pl.ds(at, n), :].astype(F32)
        return (self.before if f < 1 else self.after)[pl.ds(XB_CODE + at, n), :]

    def coarse(self, c, f, rows):
        at, n = rows
        if 2 <= f < 6:
            return self.co[c, f - 2, pl.ds(at, n), :]
        ref, k = (self.before, f) if f < 2 else (self.after, f - 6)
        return ref[pl.ds(XB_COARSE + 16 * k + at, n), pl.ds(128 * c, 128)]

    def warm(self, f, rows):
        at, n = rows
        if 4 <= f < 8:
            return self.theta[f - 4, pl.ds(at, n), :]
        ref, k = (self.before, f) if f < 4 else (self.after, f - 8)
        return ref[pl.ds(XB_THERM + 16 * k + at, n), pl.ds(0, 128)]

    def wash(self, f, rows):
        at, n = rows
        if 3 <= f < 7:
            return self.perf[f - 3, pl.ds(at, n), :]
        ref, k = (self.before, f + 1) if f < 3 else (self.after, f - 7)
        return ref[pl.ds(XB_THERM + 16 * k + at, n), pl.ds(128, 128)]


def pack_y(it, co, codes, theta, perf, before, after, up, down):
    block = Columns(it, co, codes, theta, perf, before, after)
    for ref, last in ((up, True), (down, False)):
        fine, coarse, warm = ((24, 8), (8, 8), (12, 4)) if last else ((0, 8), (0, 8), (0, 4))
        for c in range(2):
            for f in range(FX):
                ref[pl.ds((c * FX + f) * 8, 8), :] = block.iterate(c, f, fine)
        for f in range(CX):
            ref[pl.ds(YB_CODE + f * 8, 8), :] = block.code(f, fine)
        for f in range(LX):
            for c in range(2):
                ref[pl.ds(YB_COARSE + f * 8, 8), pl.ds(128 * c, 128)] = block.coarse(c, f, coarse)
        for f in range(TX):
            ref[pl.ds(YB_THERM + f * 4, 4), pl.ds(0, 128)] = block.warm(f, warm)
            wash = block.wash(f - 1, warm) if 1 <= f < 11 else jnp.zeros((4, 128), F32)
            ref[pl.ds(YB_THERM + f * 4, 4), pl.ds(128, 128)] = wash


def rows_of(wide, narrow, start, count, half):
    parts = []
    if start < WIDE:
        n = min(count, WIDE - start)
        parts.append(wide[pl.ds(start, n), pl.ds(128 * half, 128)])
        start, count = start + n, count - n
    if count:
        parts.append(narrow[pl.ds(start - WIDE, count), :])
    return parts[0] if len(parts) == 1 else jnp.concatenate(parts, axis=0)


def pack_z(it, co, codes, theta, perf, before, after, below, above, wide, narrow, up, down):
    block = Columns(it, co, codes, theta, perf, before, after)
    for c in range(2):
        for f in range(FX):
            at, k = (c * FX + f) * 48, (c * FX + f) * 8
            wide[pl.ds(at, 32), :] = block.iterate(c, f, (0, 32))
            wide[pl.ds(at + 32, 8), :] = above[pl.ds(k, 8), :]
            wide[pl.ds(at + 40, 8), :] = below[pl.ds(k, 8), :]
    for f in range(CX):
        at, k = N_CODE + f * 48, YB_CODE + f * 8
        wide[pl.ds(at, 32), :] = block.code(f, (0, 32))
        wide[pl.ds(at + 32, 8), :] = above[pl.ds(k, 8), :]
        wide[pl.ds(at + 40, 8), :] = below[pl.ds(k, 8), :]
    row = iota((8, 128), 0)
    for c in range(2):
        for f in range(LX):
            at, k, half = N_COARSE + (c * LX + f) * 32, YB_COARSE + f * 8, pl.ds(128 * c, 128)
            over, under = above[pl.ds(k, 8), half], below[pl.ds(k, 8), half]
            narrow[pl.ds(at, 16), :] = block.coarse(c, f, (0, 16))
            narrow[pl.ds(at + 16, 8), :] = jnp.where(row < 4, over, under)
            far = jnp.where(row == 1, jnp.broadcast_to(over[4:5], (8, 128)), 0.0)
            narrow[pl.ds(at + 24, 8), :] = jnp.where(row == 0, jnp.broadcast_to(under[3:4], (8, 128)), far)
    for f in range(TX):
        at, k = N_THETA + f * 24, YB_THERM + f * 4
        narrow[pl.ds(at, 16), :] = block.warm(f, (0, 16))
        narrow[pl.ds(at + 16, 4), :] = above[pl.ds(k, 4), pl.ds(0, 128)]
        narrow[pl.ds(at + 20, 4), :] = below[pl.ds(k, 4), pl.ds(0, 128)]
    for f in range(QX):
        at, k = N_PERF + f * 24, YB_THERM + (f + 1) * 4
        narrow[pl.ds(at, 16), :] = block.wash(f, (0, 16))
        narrow[pl.ds(at + 16, 4), :] = above[pl.ds(k, 4), pl.ds(128, 128)]
        narrow[pl.ds(at + 20, 4), :] = below[pl.ds(k, 4), pl.ds(128, 128)]
    narrow[pl.ds(N_PERF + QX * 24, NARROW - N_PERF - QX * 24), :] = jnp.zeros((NARROW - N_PERF - QX * 24, 128), F32)
    lane = iota((ZB, 128), 1) // 8
    for ref, half, shift in ((up, 1, 8), (down, 0, 0)):
        packed = None
        for g in range(GROUPS):
            part = rows_of(wide, narrow, g * ZB, ZB, half)
            turn = (8 * g + shift) % 128
            part = pltpu.roll(part, turn, 1) if turn else part
            packed = part if packed is None else jnp.where(lane == g, part, packed)
        ref[...] = packed


def sources(coord, loc_s, exc_s, loc, field, spread, gather):
    field[...] = jnp.zeros(field.shape, F32)
    first = loc[0:1, :] - coord[0] * 8
    second = loc[1:2, :] - coord[1] * 32
    third = loc[2:3, :] - coord[2] * 256
    near = (first >= -1) & (first < 9) & (second >= -7) & (second < 39) & (third >= -7) & (third < 263)
    order = iota((1, 1024), 1)
    lane = iota((1, 384), 1)

    def place(state):
        e, keys = state
        x = loc_s[0, e] - coord[0] * 8 + 1
        y = loc_s[1, e] - coord[1] * 32
        z = loc_s[2, e] - coord[2] * 256
        y = jnp.where(y < 0, y + 48, y)
        z = jnp.where(z < 0, z + 384, z)
        for c in range(2):
            field[c, x, pl.ds(y, 1), :] += jnp.where(lane == z, exc_s[c, e], 0.0)
        keys = jnp.where(order == e, 1024, keys)
        return jnp.min(keys), keys

    keys = jnp.where(near, order, 1024)
    lax.while_loop(lambda state: state[0] < 1024, place, (jnp.min(keys), keys))

    k, f = iota((256, 384), 0), iota((256, 384), 1)
    cell = jnp.where(f < 320, f, f - 384)
    centre = cell >> 1
    beside = centre + jnp.where((cell & 1) == 1, 1, -1)
    weight = jnp.where(k == (centre & 255), 0.75, jnp.where(k == (beside & 255), 0.25, 0.0))
    spread[...] = weight.astype(BF16)
    f, k = iota((384, 256), 0), iota((384, 256), 1)
    cell = jnp.where(f < 320, f, f - 384)
    gather[...] = jnp.where(k == ((cell >> 1) & 255), 1.0, 0.0).astype(BF16)


def smooth(coord, wave_t, damp_t, wide, narrow, left, right, source, spread, gather,
           out, power, up, down, tiles, halo, grown, fine, first, second, gain_r, gain_i, pool):
    lane = iota((ZB, 128), 1)
    for g in range(GROUPS):
        turn = (128 - 8 * g) % 128
        after = pltpu.roll(right[...], turn, 1) if turn else right[...]
        turn = (120 - 8 * g) % 128
        before = pltpu.roll(left[...], turn, 1) if turn else left[...]
        halo[pl.ds(g * ZB, ZB), :] = jnp.where(lane < 8, after, jnp.where(lane >= 120, before, 0.0))
    tiles[...] = halo[pl.ds(WIDE + N_THETA, NARROW - N_THETA), :]

    def flag(test):
        return jnp.where(test, 1.0, 0.0)

    x_before, x_after = flag(coord[0] > 0), flag(coord[0] < 3)
    y_before, y_after = flag(coord[1] > 0), flag(coord[1] < 15)
    z_before, z_after = flag(coord[2] > 0), flag(coord[2] < 3)

    row, col = iota((32, 256), 0), iota((32, 256), 1)
    y_ok = jnp.where(row < 16, 1.0, jnp.where((row < 20) | (row == 25), y_after, y_before))
    z_ok = jnp.where(col < 128, 1.0, jnp.where(col < 192, z_after, z_before))
    inside = y_ok * z_ok
    row = iota((24, 256), 0)
    for c in range(2):
        for f in range(LX):
            at = N_COARSE + (c * LX + f) * 32
            cells = jnp.concatenate([narrow[pl.ds(at, 32), :], halo[pl.ds(WIDE + at, 32), :]], axis=1)
            x_ok = x_before if f < 2 else x_after if f >= 6 else None
            cells = cells * (inside if x_ok is None else inside * x_ok)
            centre = cells[0:24]
            lower = jnp.where(row == 20, jnp.broadcast_to(cells[24:25], (24, 256)), pltpu.roll(centre, 1, 0))
            upper = jnp.where(row == 19, jnp.broadcast_to(cells[25:26], (24, 256)), pltpu.roll(centre, 23, 0))
            even = 0.75 * centre + 0.25 * lower
            odd = 0.75 * centre + 0.25 * upper
            for half in range(2):
                to = (c * LX + f) * 48
                grown[half, pl.ds(to, 24, 2), :] = even[:, half * 128 : half * 128 + 128]
                grown[half, pl.ds(to + 1, 24, 2), :] = odd[:, half * 128 : half * 128 + 128]
    fine[...] = exact_dot(jnp.concatenate([grown[0], grown[1]], axis=1), spread[...])

    row, col = iota((48, 384), 0), iota((48, 384), 1)
    y_ok = jnp.where(row < 32, 1.0, jnp.where(row < 40, y_after, y_before))
    z_ok = jnp.where(col < 256, 1.0, jnp.where(col < 320, z_after, z_before))
    inside = y_ok * z_ok
    for c in range(2):
        for f in range(FX):
            at = (c * FX + f) * 48
            start = jnp.concatenate([wide[pl.ds(at, 48), :], halo[pl.ds(at, 48), :]], axis=1)
            near = c * LX + f // 2 + 1
            far = near + (1 if f % 2 else -1)
            grow = 0.75 * fine[pl.ds(near * 48, 48), :] + 0.25 * fine[pl.ds(far * 48, 48), :]
            x_ok = x_before if f < 2 else x_after if f >= 10 else None
            first[c, f] = (start + grow) * (inside if x_ok is None else inside * x_ok)

    gains_r, gains_i, damps = [], [], []
    for t in range(4):
        speed = jnp.full((8, 128), wave_t[t], F32)
        damp = jnp.full((8, 128), damp_t[t], F32)
        wave = 1.0 / (speed * speed)
        diag_r = 6.0 - wave
        diag_i = DAMPING_SHIFT * wave + damp
        modulus = diag_r * diag_r + diag_i * diag_i
        gains_r.append((RELAXATION * diag_r / modulus)[0:1, 0:1])
        gains_i.append((RELAXATION * diag_i / modulus)[0:1, 0:1])
        damps.append(damp_t[t])

    def step(cells, at, drive_r, drive_i, g_r, g_i):
        sums = []
        for c, drive in ((0, drive_r), (1, drive_i)):
            mid = cells[c, at]
            total = cells[c, at - 1] + cells[c, at + 1] + drive
            total = total + pltpu.roll(mid, 1, 0) + pltpu.roll(mid, 47, 0)
            sums.append((mid, total + pltpu.roll(mid, 1, 1) + pltpu.roll(mid, 383, 1)))
        (mid_r, sum_r), (mid_i, sum_i) = sums
        keep = 1.0 - RELAXATION
        return keep * mid_r + (g_r * sum_r + g_i * sum_i), keep * mid_i + (g_r * sum_i - g_i * sum_r)

    def classes(f):
        at = N_CODE + f * 48
        return jnp.concatenate([wide[pl.ds(at, 48), :], halo[pl.ds(at, 48), :]], axis=1)

    for f in range(CX):
        codes = classes(f)
        x_ok = x_before if f < 1 else x_after if f >= 9 else None
        ok = inside if x_ok is None else inside * x_ok
        g_r = pick(codes, gains_r) * ok
        g_i = pick(codes, gains_i) * ok
        gain_r[f], gain_i[f] = g_r, g_i
        second[0, f], second[1, f] = step(first, f + 1, source[0, f], source[1, f], g_r, g_i)

    for i in range(4):
        heat = None
        for f in (2 * i, 2 * i + 1):
            new_r, new_i = step(second, f + 1, source[0, f + 1], source[1, f + 1], gain_r[f + 1], gain_i[f + 1])
            out[0, f] = new_r[0:32, 0:256]
            out[1, f] = new_i[0:32, 0:256]
            layer = pick(classes(f + 1), damps) * (new_r * new_r + new_i * new_i)
            heat = layer if heat is None else heat + layer
        for third in range(3):
            pool[third, pl.ds(i * 48, 48), :] = heat[:, third * 128 : third * 128 + 128]
    sums = jnp.concatenate([pool[t, pl.ds(0, 96, 2), :] + pool[t, pl.ds(1, 96, 2), :] for t in range(3)], axis=1)
    sums = exact_dot(sums, gather[...]) * 0.125
    for i in range(4):
        power[i] = sums[i * 24 : i * 24 + 24]
        if i >= 1:
            up[i - 1] = sums[i * 24 : i * 24 + 24]
        if i < 3:
            down[i] = sums[i * 24 : i * 24 + 24]


def bioheat(coord, narrow, tiles, power, before, after, injury, warm_out, dose_out, now, later):
    def flag(test):
        return jnp.where(test, 1.0, 0.0)

    x_before, x_after = flag(coord[0] > 0), flag(coord[0] < 3)
    row, col = iota((24, 256), 0), iota((24, 256), 1)
    y_ok = jnp.where(row < 16, 1.0, jnp.where(row < 20, flag(coord[1] < 15), flag(coord[1] > 0)))
    z_ok = jnp.where(col < 128, 1.0, jnp.where(col < 192, flag(coord[2] < 3), flag(coord[2] > 0)))
    inside = y_ok * z_ok
    edge = [inside * (x_before if f < 4 else x_after) if not 4 <= f < 8 else inside for f in range(TX)]

    def extended(base, f):
        at = base + f * 24
        return jnp.concatenate([narrow[pl.ds(at, 24), :], tiles[pl.ds(at - N_THETA, 24), :]], axis=1)

    for f in range(TX):
        now[f] = extended(N_THETA, f) * edge[f]
    dose = [injury[i] for i in range(4)]
    state, other = now, later
    for turn in range(4):
        for f in range(1 + turn, TX - 1 - turn):
            mid = state[f]
            beside = state[f - 1] + state[f + 1]
            beside = beside + pltpu.roll(mid, 1, 0) + pltpu.roll(mid, 23, 0)
            beside = beside + pltpu.roll(mid, 1, 1) + pltpu.roll(mid, 255, 1)
            heat = power[f - 4] if 4 <= f < 8 else before[f - 1] if f < 4 else after[f - 8]
            wash = extended(N_PERF, f - 1)
            new = mid + DIFFUSION * (beside - 6.0 * mid) - wash * mid + HEATING * heat
            other[f] = new * edge[f]
            if 4 <= f < 8:
                own = new[0:16, 0:128]
                dose[f - 4] = dose[f - 4] + jnp.exp(LN_PREFACTOR - ENERGY_BARRIER / (CORE_WARMTH + own))
                if turn == 3:
                    warm_out[f - 4] = own
        state, other = other, state
    for i in range(4):
        dose_out[i] = jnp.log(dose[i])


def shaped(*shape, dtype=F32):
    return jax.ShapeDtypeStruct(shape, dtype)


def call(kernel, name, in_specs, outs, scratch=(), cost=2000):
    return pl.pallas_call(
        kernel,
        name=name,
        out_shape=tuple(outs),
        in_specs=in_specs,
        out_specs=tuple(vmem() for _ in outs),
        scratch_shapes=list(scratch),
        cost_estimate=pl.CostEstimate(flops=cost * 1000, bytes_accessed=cost * 1000, transcendentals=0),
        compiler_params=pltpu.CompilerParams(vmem_limit_bytes=24 * 1024 * 1024),
    )


def on_device(
    acoustic_iterate,
    coarse_update,
    class_codes_volume,
    element_location,
    element_excitation,
    class_wavespeed,
    class_damping,
    washout_fraction,
    thermal_excess,
    injury_integral,
):
    it, co, codes, theta = acoustic_iterate, coarse_update, class_codes_volume, thermal_excess
    coord = jnp.stack([lax.axis_index("gx"), lax.axis_index("gy"), lax.axis_index("gz")]).astype(jnp.int32)
    loc = element_location.T

    up, down, perf = call(
        pack_x, "pack_x", [smem()] + [vmem()] * 4,
        [shaped(XB, 256), shaped(XB, 256), shaped(4, 16, 128)],
        [pltpu.VMEM((2, 128, 128), F32)],
    )(washout_fraction, it, co, codes, theta)
    before, after = exchange(up, down, "gx")

    field, spread, gather = call(
        sources, "sources", [smem(), smem(), smem(), vmem()],
        [shaped(2, CX, 48, 384), shaped(256, 384, dtype=BF16), shaped(384, 256, dtype=BF16)], cost=8000,
    )(coord, loc, element_excitation, loc)

    up, down = call(pack_y, "pack_y", [vmem()] * 7, [shaped(YB, 256), shaped(YB, 256)])(
        it, co, codes, theta, perf, before, after
    )
    below, above = exchange(up, down, "gy")

    wide, narrow, up, down = call(
        pack_z, "pack_z", [vmem()] * 9,
        [shaped(WIDE, 256), shaped(NARROW, 128), shaped(ZB, 128), shaped(ZB, 128)],
    )(it, co, codes, theta, perf, before, after, below, above)
    left, right = exchange(up, down, "gz")

    pressure, power, up, down, tiles = call(
        smooth, "smooth", [smem()] * 3 + [vmem()] * 7,
        [
            shaped(2, 8, 32, 256),
            shaped(4, 24, 256),
            shaped(3, 24, 256),
            shaped(3, 24, 256),
            shaped(NARROW - N_THETA, 128),
        ],
        [
            pltpu.VMEM((WIDE + NARROW, 128), F32),
            pltpu.VMEM((2, 2 * LX * 48, 128), F32),
            pltpu.VMEM((2 * LX * 48, 384), F32),
            pltpu.VMEM((2, FX, 48, 384), F32),
            pltpu.VMEM((2, CX, 48, 384), F32),
            pltpu.VMEM((CX, 48, 384), F32),
            pltpu.VMEM((CX, 48, 384), F32),
            pltpu.VMEM((3, 192, 128), F32),
        ],
    )(coord, class_wavespeed, class_damping, wide, narrow, left, right, field, spread, gather)
    before, after = exchange(up, down, "gx")

    warmth, dose = call(
        bioheat, "bioheat", [smem()] + [vmem()] * 6,
        [shaped(4, 16, 128), shaped(4, 16, 128)],
        [pltpu.VMEM((TX, 24, 256), F32), pltpu.VMEM((TX, 24, 256), F32)],
    )(coord, narrow, tiles, power, before, after, injury_integral)
    return pressure, warmth, dose


def solution(mesh):
    placed = (
        P(None, "gx", "gy", "gz"),
        P(None, "gx", "gy", "gz"),
        P("gx", "gy", "gz"),
        P(),
        P(),
        P(),
        P(),
        P(),
        P("gx", "gy", "gz"),
        P("gx", "gy", "gz"),
    )
    return jax.shard_map(
        on_device,
        mesh=mesh,
        in_specs=placed,
        out_specs=(P(None, "gx", "gy", "gz"), P("gx", "gy", "gz"), P("gx", "gy", "gz")),
        check_vma=False,
    )
```

```python
import jax
import jax.numpy as jnp
from jax import lax
from jax.experimental import pallas as pl
from jax.experimental.pallas import tpu as pltpu
from jax.sharding import PartitionSpec as P

F32 = jnp.float32
BF16 = jnp.bfloat16

RELAXATION = 0.8
DAMPING_SHIFT = 0.5
DIFFUSION = 0.15
HEATING = 0.25
LN_PREFACTOR = 226.78
ENERGY_BARRIER = 75535.0
CORE_WARMTH = 310.15

FX, CX, LX, TX, QX = 12, 10, 8, 12, 10
XB_CODE, XB_COARSE, XB_THERM, XB = 128, 160, 192, 256
YB_CODE, YB_COARSE, YB_THERM, YB = 192, 272, 336, 384
WIDE = 2 * FX * 48 + CX * 48
N_CODE = 2 * FX * 48
N_COARSE, N_THETA, N_PERF, NARROW = 0, 512, 800, 1056
GROUPS = 16
ZB = (WIDE + NARROW) // GROUPS


def vmem():
    return pl.BlockSpec(memory_space=pltpu.VMEM)


def hbm():
    return pl.BlockSpec(memory_space=pltpu.HBM)


def smem():
    return pl.BlockSpec(memory_space=pltpu.SMEM)


def exchange(up, down, axis):
    n = lax.axis_size(axis)
    ahead = [(i, (i + 1) % n) for i in range(n)]
    back = [(j, i) for i, j in ahead]
    return lax.ppermute(up, axis, ahead), lax.ppermute(down, axis, back)


def exact_dot(values, weights):
    high = values.astype(BF16)
    rest = values - high.astype(F32)
    mid = rest.astype(BF16)
    low = (rest - mid.astype(F32)).astype(BF16)
    total = jnp.dot(high, weights, preferred_element_type=F32)
    total = total + jnp.dot(mid, weights, preferred_element_type=F32)
    return total + jnp.dot(low, weights, preferred_element_type=F32)


def iota(shape, dim):
    return lax.broadcasted_iota(jnp.int32, shape, dim)


def pick(codes, entries):
    value = jnp.where(codes == 0.0, entries[0], entries[1])
    value = jnp.where(codes == 2.0, entries[2], value)
    return jnp.where(codes == 3.0, entries[3], value)


def pack_x(wash_h, it_h, co_h, codes_h, theta_h, up, down, perf, it, co, codes, theta, pool, wash, sems):
    loads = [
        pltpu.make_async_copy(src, dst, sems.at[k])
        for k, (src, dst) in enumerate(
            ((codes_h, codes), (it_h, it), (wash_h, wash), (co_h, co), (theta_h, theta))
        )
    ]
    for load in loads:
        load.start()
    lane, col = iota((256, 128), 0), iota((256, 128), 1)
    pairs = jnp.where(lane // 2 == col, 1.0, 0.0).astype(BF16)
    for load in loads:
        load.wait()
    entries = [wash[k] for k in range(4)]
    for i in range(4):
        both = pick(codes[2 * i].astype(F32), entries) + pick(codes[2 * i + 1].astype(F32), entries)
        for half in range(2):
            pool[half, i * 32 : i * 32 + 32, :] = both[:, half * 128 : half * 128 + 128]
    rows = jnp.concatenate([pool[h, pl.ds(0, 64, 2), :] + pool[h, pl.ds(1, 64, 2), :] for h in range(2)], axis=1)
    washed = exact_dot(rows, pairs) * 0.125
    for i in range(4):
        perf[i] = washed[i * 16 : i * 16 + 16]
    for ref, fine, coarse in ((up, 6, 2), (down, 0, 0)):
        for c in range(2):
            for k in range(2):
                ref[pl.ds((c * 2 + k) * 32, 32), :] = it[c, fine + k]
        ref[pl.ds(XB_CODE, 32), :] = codes[7 if fine else 0].astype(F32)
        for k in range(2):
            for c in range(2):
                ref[pl.ds(XB_COARSE + 16 * k, 16), pl.ds(128 * c, 128)] = co[c, coarse + k]
        for i in range(4):
            ref[pl.ds(XB_THERM + 16 * i, 16), pl.ds(0, 128)] = theta[i]
            ref[pl.ds(XB_THERM + 16 * i, 16), pl.ds(128, 128)] = washed[i * 16 : i * 16 + 16]


class Columns:
    def __init__(self, it, co, codes, theta, perf, before, after):
        self.it, self.co, self.codes, self.theta, self.perf = it, co, codes, theta, perf
        self.before, self.after = before, after

    def iterate(self, c, f, rows):
        at, n = rows
        if 2 <= f < 10:
            return self.it[c, f - 2, pl.ds(at, n), :]
        ref, k = (self.before, f) if f < 2 else (self.after, f - 10)
        return ref[pl.ds((c * 2 + k) * 32 + at, n), :]

    def code(self, f, rows):
        at, n = rows
        if 1 <= f < 9:
            return self.codes[f - 1, pl.ds(at, n), :].astype(F32)
        return (self.before if f < 1 else self.after)[pl.ds(XB_CODE + at, n), :]

    def coarse(self, c, f, rows):
        at, n = rows
        if 2 <= f < 6:
            return self.co[c, f - 2, pl.ds(at, n), :]
        ref, k = (self.before, f) if f < 2 else (self.after, f - 6)
        return ref[pl.ds(XB_COARSE + 16 * k + at, n), pl.ds(128 * c, 128)]

    def warm(self, f, rows):
        at, n = rows
        if 4 <= f < 8:
            return self.theta[f - 4, pl.ds(at, n), :]
        ref, k = (self.before, f) if f < 4 else (self.after, f - 8)
        return ref[pl.ds(XB_THERM + 16 * k + at, n), pl.ds(0, 128)]

    def wash(self, f, rows):
        at, n = rows
        if 3 <= f < 7:
            return self.perf[f - 3, pl.ds(at, n), :]
        ref, k = (self.before, f + 1) if f < 3 else (self.after, f - 7)
        return ref[pl.ds(XB_THERM + 16 * k + at, n), pl.ds(128, 128)]


def pack_y(it, co, codes, theta, perf, before, after, after_this, up, down):
    block = Columns(it, co, codes, theta, perf, before, after)
    for ref, last in ((up, True), (down, False)):
        fine, coarse, warm = ((24, 8), (8, 8), (12, 4)) if last else ((0, 8), (0, 8), (0, 4))
        for c in range(2):
            for f in range(FX):
                ref[pl.ds((c * FX + f) * 8, 8), :] = block.iterate(c, f, fine)
        for f in range(CX):
            ref[pl.ds(YB_CODE + f * 8, 8), :] = block.code(f, fine)
        for f in range(LX):
            for c in range(2):
                ref[pl.ds(YB_COARSE + f * 8, 8), pl.ds(128 * c, 128)] = block.coarse(c, f, coarse)
        for f in range(TX):
            ref[pl.ds(YB_THERM + f * 4, 4), pl.ds(0, 128)] = block.warm(f, warm)
            wash = block.wash(f - 1, warm) if 1 <= f < 11 else jnp.zeros((4, 128), F32)
            ref[pl.ds(YB_THERM + f * 4, 4), pl.ds(128, 128)] = wash


def rows_of(wide, narrow, start, count, half):
    parts = []
    if start < WIDE:
        n = min(count, WIDE - start)
        parts.append(wide[pl.ds(start, n), pl.ds(128 * half, 128)])
        start, count = start + n, count - n
    if count:
        parts.append(narrow[pl.ds(start - WIDE, count), :])
    return parts[0] if len(parts) == 1 else jnp.concatenate(parts, axis=0)


def pack_z(it, co, codes, theta, perf, before, after, below, above, wide, narrow, up, down):
    block = Columns(it, co, codes, theta, perf, before, after)
    for c in range(2):
        for f in range(FX):
            at, k = (c * FX + f) * 48, (c * FX + f) * 8
            wide[pl.ds(at, 32), :] = block.iterate(c, f, (0, 32))
            wide[pl.ds(at + 32, 8), :] = above[pl.ds(k, 8), :]
            wide[pl.ds(at + 40, 8), :] = below[pl.ds(k, 8), :]
    for f in range(CX):
        at, k = N_CODE + f * 48, YB_CODE + f * 8
        wide[pl.ds(at, 32), :] = block.code(f, (0, 32))
        wide[pl.ds(at + 32, 8), :] = above[pl.ds(k, 8), :]
        wide[pl.ds(at + 40, 8), :] = below[pl.ds(k, 8), :]
    row = iota((8, 128), 0)
    for c in range(2):
        for f in range(LX):
            at, k, half = N_COARSE + (c * LX + f) * 32, YB_COARSE + f * 8, pl.ds(128 * c, 128)
            over, under = above[pl.ds(k, 8), half], below[pl.ds(k, 8), half]
            narrow[pl.ds(at, 16), :] = block.coarse(c, f, (0, 16))
            narrow[pl.ds(at + 16, 8), :] = jnp.where(row < 4, over, under)
            far = jnp.where(row == 1, jnp.broadcast_to(over[4:5], (8, 128)), 0.0)
            narrow[pl.ds(at + 24, 8), :] = jnp.where(row == 0, jnp.broadcast_to(under[3:4], (8, 128)), far)
    for f in range(TX):
        at, k = N_THETA + f * 24, YB_THERM + f * 4
        narrow[pl.ds(at, 16), :] = block.warm(f, (0, 16))
        narrow[pl.ds(at + 16, 4), :] = above[pl.ds(k, 4), pl.ds(0, 128)]
        narrow[pl.ds(at + 20, 4), :] = below[pl.ds(k, 4), pl.ds(0, 128)]
    for f in range(QX):
        at, k = N_PERF + f * 24, YB_THERM + (f + 1) * 4
        narrow[pl.ds(at, 16), :] = block.wash(f, (0, 16))
        narrow[pl.ds(at + 16, 4), :] = above[pl.ds(k, 4), pl.ds(128, 128)]
        narrow[pl.ds(at + 20, 4), :] = below[pl.ds(k, 4), pl.ds(128, 128)]
    narrow[pl.ds(N_PERF + QX * 24, NARROW - N_PERF - QX * 24), :] = jnp.zeros((NARROW - N_PERF - QX * 24, 128), F32)
    lane = iota((ZB, 128), 1) // 8
    for ref, half, shift in ((up, 1, 8), (down, 0, 0)):
        packed = None
        for g in range(GROUPS):
            part = rows_of(wide, narrow, g * ZB, ZB, half)
            turn = (8 * g + shift) % 128
            part = pltpu.roll(part, turn, 1) if turn else part
            packed = part if packed is None else jnp.where(lane == g, part, packed)
        ref[...] = packed


def sources(coord, loc_s, exc_s, loc, after_this, field, spread, gather):
    field[...] = jnp.zeros(field.shape, F32)
    first = loc[0:1, :] - coord[0] * 8
    second = loc[1:2, :] - coord[1] * 32
    third = loc[2:3, :] - coord[2] * 256
    near = (first >= -1) & (first < 9) & (second >= -7) & (second < 39) & (third >= -7) & (third < 263)
    order = iota((1, 1024), 1)
    lane = iota((1, 384), 1)

    def place(state):
        e, keys = state
        x = loc_s[0, e] - coord[0] * 8 + 1
        y = loc_s[1, e] - coord[1] * 32
        z = loc_s[2, e] - coord[2] * 256
        y = jnp.where(y < 0, y + 48, y)
        z = jnp.where(z < 0, z + 384, z)
        for c in range(2):
            field[c, x, pl.ds(y, 1), :] += jnp.where(lane == z, exc_s[c, e], 0.0)
        keys = jnp.where(order == e, 1024, keys)
        return jnp.min(keys), keys

    keys = jnp.where(near, order, 1024)
    lax.while_loop(lambda state: state[0] < 1024, place, (jnp.min(keys), keys))

    k, f = iota((256, 384), 0), iota((256, 384), 1)
    cell = jnp.where(f < 320, f, f - 384)
    centre = cell >> 1
    beside = centre + jnp.where((cell & 1) == 1, 1, -1)
    weight = jnp.where(k == (centre & 255), 0.75, jnp.where(k == (beside & 255), 0.25, 0.0))
    spread[...] = weight.astype(BF16)
    f, k = iota((384, 256), 0), iota((384, 256), 1)
    cell = jnp.where(f < 320, f, f - 384)
    gather[...] = jnp.where(k == ((cell >> 1) & 255), 1.0, 0.0).astype(BF16)


def smooth(coord, wave_t, damp_t, wide, narrow, left, right, source, spread, gather,
           out, power, up, down, tiles, halo, grown, fine, first, second, gain_r, gain_i, pool):
    lane = iota((ZB, 128), 1)
    for g in range(GROUPS):
        turn = (128 - 8 * g) % 128
        after = pltpu.roll(right[...], turn, 1) if turn else right[...]
        turn = (120 - 8 * g) % 128
        before = pltpu.roll(left[...], turn, 1) if turn else left[...]
        halo[pl.ds(g * ZB, ZB), :] = jnp.where(lane < 8, after, jnp.where(lane >= 120, before, 0.0))
    tiles[...] = halo[pl.ds(WIDE + N_THETA, NARROW - N_THETA), :]

    def flag(test):
        return jnp.where(test, 1.0, 0.0)

    x_before, x_after = flag(coord[0] > 0), flag(coord[0] < 3)
    y_before, y_after = flag(coord[1] > 0), flag(coord[1] < 15)
    z_before, z_after = flag(coord[2] > 0), flag(coord[2] < 3)

    row, col = iota((32, 256), 0), iota((32, 256), 1)
    y_ok = jnp.where(row < 16, 1.0, jnp.where((row < 20) | (row == 25), y_after, y_before))
    z_ok = jnp.where(col < 128, 1.0, jnp.where(col < 192, z_after, z_before))
    inside = y_ok * z_ok
    row = iota((24, 256), 0)
    for c in range(2):
        for f in range(LX):
            at = N_COARSE + (c * LX + f) * 32
            cells = jnp.concatenate([narrow[pl.ds(at, 32), :], halo[pl.ds(WIDE + at, 32), :]], axis=1)
            x_ok = x_before if f < 2 else x_after if f >= 6 else None
            cells = cells * (inside if x_ok is None else inside * x_ok)
            centre = cells[0:24]
            lower = jnp.where(row == 20, jnp.broadcast_to(cells[24:25], (24, 256)), pltpu.roll(centre, 1, 0))
            upper = jnp.where(row == 19, jnp.broadcast_to(cells[25:26], (24, 256)), pltpu.roll(centre, 23, 0))
            even = 0.75 * centre + 0.25 * lower
            odd = 0.75 * centre + 0.25 * upper
            for half in range(2):
                to = (c * LX + f) * 48
                grown[half, pl.ds(to, 24, 2), :] = even[:, half * 128 : half * 128 + 128]
                grown[half, pl.ds(to + 1, 24, 2), :] = odd[:, half * 128 : half * 128 + 128]
    fine[...] = exact_dot(jnp.concatenate([grown[0], grown[1]], axis=1), spread[...])

    row, col = iota((48, 384), 0), iota((48, 384), 1)
    y_ok = jnp.where(row < 32, 1.0, jnp.where(row < 40, y_after, y_before))
    z_ok = jnp.where(col < 256, 1.0, jnp.where(col < 320, z_after, z_before))
    inside = y_ok * z_ok
    for c in range(2):
        for f in range(FX):
            at = (c * FX + f) * 48
            start = jnp.concatenate([wide[pl.ds(at, 48), :], halo[pl.ds(at, 48), :]], axis=1)
            near = c * LX + f // 2 + 1
            far = near + (1 if f % 2 else -1)
            grow = 0.75 * fine[pl.ds(near * 48, 48), :] + 0.25 * fine[pl.ds(far * 48, 48), :]
            x_ok = x_before if f < 2 else x_after if f >= 10 else None
            first[c, f] = (start + grow) * (inside if x_ok is None else inside * x_ok)

    gains_r, gains_i, damps = [], [], []
    for t in range(4):
        speed = jnp.full((8, 128), wave_t[t], F32)
        damp = jnp.full((8, 128), damp_t[t], F32)
        wave = 1.0 / (speed * speed)
        diag_r = 6.0 - wave
        diag_i = DAMPING_SHIFT * wave + damp
        modulus = diag_r * diag_r + diag_i * diag_i
        gains_r.append((RELAXATION * diag_r / modulus)[0:1, 0:1])
        gains_i.append((RELAXATION * diag_i / modulus)[0:1, 0:1])
        damps.append(damp_t[t])

    def step(cells, at, drive_r, drive_i, g_r, g_i):
        sums = []
        for c, drive in ((0, drive_r), (1, drive_i)):
            mid = cells[c, at]
            total = cells[c, at - 1] + cells[c, at + 1] + drive
            total = total + pltpu.roll(mid, 1, 0) + pltpu.roll(mid, 47, 0)
            sums.append((mid, total + pltpu.roll(mid, 1, 1) + pltpu.roll(mid, 383, 1)))
        (mid_r, sum_r), (mid_i, sum_i) = sums
        keep = 1.0 - RELAXATION
        return keep * mid_r + (g_r * sum_r + g_i * sum_i), keep * mid_i + (g_r * sum_i - g_i * sum_r)

    def classes(f):
        at = N_CODE + f * 48
        return jnp.concatenate([wide[pl.ds(at, 48), :], halo[pl.ds(at, 48), :]], axis=1)

    for f in range(CX):
        codes = classes(f)
        x_ok = x_before if f < 1 else x_after if f >= 9 else None
        ok = inside if x_ok is None else inside * x_ok
        g_r = pick(codes, gains_r) * ok
        g_i = pick(codes, gains_i) * ok
        gain_r[f], gain_i[f] = g_r, g_i
        second[0, f], second[1, f] = step(first, f + 1, source[0, f], source[1, f], g_r, g_i)

    for i in range(4):
        heat = None
        for f in (2 * i, 2 * i + 1):
            new_r, new_i = step(second, f + 1, source[0, f + 1], source[1, f + 1], gain_r[f + 1], gain_i[f + 1])
            out[0, f] = new_r[0:32, 0:256]
            out[1, f] = new_i[0:32, 0:256]
            layer = pick(classes(f + 1), damps) * (new_r * new_r + new_i * new_i)
            heat = layer if heat is None else heat + layer
        for third in range(3):
            pool[third, pl.ds(i * 48, 48), :] = heat[:, third * 128 : third * 128 + 128]
    sums = jnp.concatenate([pool[t, pl.ds(0, 96, 2), :] + pool[t, pl.ds(1, 96, 2), :] for t in range(3)], axis=1)
    sums = exact_dot(sums, gather[...]) * 0.125
    for i in range(4):
        power[i] = sums[i * 24 : i * 24 + 24]
        if i >= 1:
            up[i - 1] = sums[i * 24 : i * 24 + 24]
        if i < 3:
            down[i] = sums[i * 24 : i * 24 + 24]


def bioheat(coord, narrow, tiles, power, before, after, injury, wave, warm_out, dose_out, wave_out, now, later, sem):
    store = pltpu.make_async_copy(wave, wave_out, sem)
    store.start()

    def flag(test):
        return jnp.where(test, 1.0, 0.0)

    x_before, x_after = flag(coord[0] > 0), flag(coord[0] < 3)
    row, col = iota((24, 256), 0), iota((24, 256), 1)
    y_ok = jnp.where(row < 16, 1.0, jnp.where(row < 20, flag(coord[1] < 15), flag(coord[1] > 0)))
    z_ok = jnp.where(col < 128, 1.0, jnp.where(col < 192, flag(coord[2] < 3), flag(coord[2] > 0)))
    inside = y_ok * z_ok
    edge = [inside * (x_before if f < 4 else x_after) if not 4 <= f < 8 else inside for f in range(TX)]

    def extended(base, f):
        at = base + f * 24
        return jnp.concatenate([narrow[pl.ds(at, 24), :], tiles[pl.ds(at - N_THETA, 24), :]], axis=1)

    for f in range(TX):
        now[f] = extended(N_THETA, f) * edge[f]
    dose = [injury[i] for i in range(4)]
    state, other = now, later
    for turn in range(4):
        for f in range(1 + turn, TX - 1 - turn):
            mid = state[f]
            beside = state[f - 1] + state[f + 1]
            beside = beside + pltpu.roll(mid, 1, 0) + pltpu.roll(mid, 23, 0)
            beside = beside + pltpu.roll(mid, 1, 1) + pltpu.roll(mid, 255, 1)
            heat = power[f - 4] if 4 <= f < 8 else before[f - 1] if f < 4 else after[f - 8]
            wash = extended(N_PERF, f - 1)
            new = mid + DIFFUSION * (beside - 6.0 * mid) - wash * mid + HEATING * heat
            other[f] = new * edge[f]
            if 4 <= f < 8:
                own = new[0:16, 0:128]
                dose[f - 4] = dose[f - 4] + jnp.exp(LN_PREFACTOR - ENERGY_BARRIER / (CORE_WARMTH + own))
                if turn == 3:
                    warm_out[f - 4] = own
        state, other = other, state
    for i in range(4):
        dose_out[i] = jnp.log(dose[i])
    store.wait()


def shaped(*shape, dtype=F32):
    return jax.ShapeDtypeStruct(shape, dtype)


def call(kernel, name, in_specs, outs, scratch=(), out_specs=None, cost=2000):
    return pl.pallas_call(
        kernel,
        name=name,
        out_shape=tuple(outs),
        in_specs=in_specs,
        out_specs=tuple(out_specs or [vmem() for _ in outs]),
        scratch_shapes=list(scratch),
        cost_estimate=pl.CostEstimate(flops=cost * 1000, bytes_accessed=cost * 1000, transcendentals=0),
        compiler_params=pltpu.CompilerParams(vmem_limit_bytes=24 * 1024 * 1024),
    )


def on_device(
    acoustic_iterate,
    coarse_update,
    class_codes_volume,
    element_location,
    element_excitation,
    class_wavespeed,
    class_damping,
    washout_fraction,
    thermal_excess,
    injury_integral,
):
    it, co, codes, theta = acoustic_iterate, coarse_update, class_codes_volume, thermal_excess
    coord = jnp.stack([lax.axis_index("gx"), lax.axis_index("gy"), lax.axis_index("gz")]).astype(jnp.int32)
    loc = element_location.T

    up, down, perf, it, co, codes, theta = call(
        pack_x, "pack_x", [hbm()] * 5,
        [
            shaped(XB, 256),
            shaped(XB, 256),
            shaped(4, 16, 128),
            shaped(2, 8, 32, 256),
            shaped(2, 4, 16, 128),
            shaped(8, 32, 256, dtype=jnp.int32),
            shaped(4, 16, 128),
        ],
        [pltpu.VMEM((2, 128, 128), F32), pltpu.SMEM((4,), F32), pltpu.SemaphoreType.DMA((5,))],
    )(*[pltpu.with_memory_space_constraint(a, pltpu.HBM) for a in (washout_fraction, it, co, codes, theta)])
    before, after = exchange(up, down, "gx")

    field, spread, gather = call(
        sources, "sources", [smem(), smem(), smem(), vmem(), vmem()],
        [shaped(2, CX, 48, 384), shaped(256, 384, dtype=BF16), shaped(384, 256, dtype=BF16)], cost=8000,
    )(coord, loc, element_excitation, loc, perf)

    up, down = call(pack_y, "pack_y", [vmem()] * 8, [shaped(YB, 256), shaped(YB, 256)])(
        it, co, codes, theta, perf, before, after, gather
    )
    below, above = exchange(up, down, "gy")

    wide, narrow, up, down = call(
        pack_z, "pack_z", [vmem()] * 9,
        [shaped(WIDE, 256), shaped(NARROW, 128), shaped(ZB, 128), shaped(ZB, 128)],
    )(it, co, codes, theta, perf, before, after, below, above)
    left, right = exchange(up, down, "gz")

    pressure, power, up, down, tiles = call(
        smooth, "smooth", [smem()] * 3 + [vmem()] * 7,
        [
            shaped(2, 8, 32, 256),
            shaped(4, 24, 256),
            shaped(3, 24, 256),
            shaped(3, 24, 256),
            shaped(NARROW - N_THETA, 128),
        ],
        [
            pltpu.VMEM((WIDE + NARROW, 128), F32),
            pltpu.VMEM((2, 2 * LX * 48, 128), F32),
            pltpu.VMEM((2 * LX * 48, 384), F32),
            pltpu.VMEM((2, FX, 48, 384), F32),
            pltpu.VMEM((2, CX, 48, 384), F32),
            pltpu.VMEM((CX, 48, 384), F32),
            pltpu.VMEM((CX, 48, 384), F32),
            pltpu.VMEM((3, 192, 128), F32),
        ],
    )(coord, class_wavespeed, class_damping, wide, narrow, left, right, field, spread, gather)
    before, after = exchange(up, down, "gx")

    warmth, dose, pressure = call(
        bioheat, "bioheat", [smem()] + [vmem()] * 7,
        [shaped(4, 16, 128), shaped(4, 16, 128), shaped(2, 8, 32, 256)],
        [pltpu.VMEM((TX, 24, 256), F32), pltpu.VMEM((TX, 24, 256), F32), pltpu.SemaphoreType.DMA],
        [vmem(), vmem(), hbm()],
    )(coord, narrow, tiles, power, before, after, injury_integral, pressure)
    return pressure, warmth, dose


def solution(mesh):
    placed = (
        P(None, "gx", "gy", "gz"),
        P(None, "gx", "gy", "gz"),
        P("gx", "gy", "gz"),
        P(),
        P(),
        P(),
        P(),
        P(),
        P("gx", "gy", "gz"),
        P("gx", "gy", "gz"),
    )
    return jax.shard_map(
        on_device,
        mesh=mesh,
        in_specs=placed,
        out_specs=(P(None, "gx", "gy", "gz"), P("gx", "gy", "gz"), P("gx", "gy", "gz")),
        check_vma=False,
    )
```

```python
import jax
import jax.numpy as jnp
from jax import lax
from jax.experimental import pallas as pl
from jax.experimental.pallas import tpu as pltpu
from jax.sharding import PartitionSpec as P

F32 = jnp.float32
BF16 = jnp.bfloat16

RELAXATION = 0.8
DAMPING_SHIFT = 0.5
DIFFUSION = 0.15
HEATING = 0.25
LN_PREFACTOR = 226.78
ENERGY_BARRIER = 75535.0
CORE_WARMTH = 310.15

FX, CX, LX, TX, QX = 12, 10, 8, 12, 10
XB_CODE, XB_COARSE, XB_THERM, XB = 128, 160, 192, 256
OWN = (128, 192, 224, 240)
FAR = (64, 80, 112, 144)
WIDE = 2 * FX * 48 + CX * 48
N_CODE = 2 * FX * 48
N_COARSE, N_THETA, N_PERF, NARROW = 0, 512, 800, 1056
GROUPS = 16
ZB = (WIDE + NARROW) // GROUPS
AXES = ("gx", "gy", "gz")


def vmem():
    return pl.BlockSpec(memory_space=pltpu.VMEM)


def hbm():
    return pl.BlockSpec(memory_space=pltpu.HBM)


def smem():
    return pl.BlockSpec(memory_space=pltpu.SMEM)


def swaps(sizes, axis, odd):
    count, targets = 1, []
    for n in sizes:
        count *= n
    for i in range(count):
        place, rest = [], i
        for n in reversed(sizes):
            place.insert(0, rest % n)
            rest //= n
        partner = list(place)
        partner[axis] = ((place[axis] + 1) ^ 1) - 1 if odd else place[axis] ^ 1
        if not 0 <= partner[axis] < sizes[axis]:
            other = 2 if axis != 2 else 0
            partner = list(place)
            partner[other] = place[other] ^ 1
        j = 0
        for n, at in zip(sizes, partner):
            j = j * n + at
        targets.append((i, j))
    return targets


def exchange(pair, axis):
    sizes = [lax.axis_size(name) for name in AXES]
    return [lax.ppermute(buffer, AXES, swaps(sizes, axis, bool(k))) for k, buffer in enumerate(pair)]


def is_even(axis):
    return lax.axis_index(AXES[axis]) % 2 == 0


class Sender:
    def __init__(self, first, second, axis):
        self.first, self.second, self.even = first, second, is_even(axis)

    def put(self, rows, lanes, up, down):
        self.first[rows, lanes] = jnp.where(self.even, up, down)
        self.second[rows, lanes] = jnp.where(self.even, down, up)


class Receiver:
    def __init__(self, first, second, axis):
        self.first, self.second, self.even = first, second, is_even(axis)

    def before(self, *at):
        return jnp.where(self.even, self.second[at], self.first[at])

    def after(self, *at):
        return jnp.where(self.even, self.first[at], self.second[at])


def exact_dot(values, weights):
    high = values.astype(BF16)
    rest = values - high.astype(F32)
    mid = rest.astype(BF16)
    low = (rest - mid.astype(F32)).astype(BF16)
    total = jnp.dot(high, weights, preferred_element_type=F32)
    total = total + jnp.dot(mid, weights, preferred_element_type=F32)
    return total + jnp.dot(low, weights, preferred_element_type=F32)


def iota(shape, dim):
    return lax.broadcasted_iota(jnp.int32, shape, dim)


def pick(codes, entries):
    value = jnp.where(codes == 0.0, entries[0], entries[1])
    value = jnp.where(codes == 2.0, entries[2], value)
    return jnp.where(codes == 3.0, entries[3], value)


def pack_x(wash_h, it_h, co_h, codes_h, theta_h, x_one, x_two, y_one, y_two, perf, it, co, codes, theta, pool, wash, sems):
    loads = [
        pltpu.make_async_copy(src, dst, sems.at[k])
        for k, (src, dst) in enumerate(
            ((codes_h, codes), (it_h, it), (wash_h, wash), (co_h, co), (theta_h, theta))
        )
    ]
    for load in loads:
        load.start()
    lane, col = iota((256, 128), 0), iota((256, 128), 1)
    pairs = jnp.where(lane // 2 == col, 1.0, 0.0).astype(BF16)
    for load in loads:
        load.wait()
    entries = [wash[k] for k in range(4)]
    for i in range(4):
        both = pick(codes[2 * i].astype(F32), entries) + pick(codes[2 * i + 1].astype(F32), entries)
        for half in range(2):
            pool[half, i * 32 : i * 32 + 32, :] = both[:, half * 128 : half * 128 + 128]
    rows = jnp.concatenate([pool[h, pl.ds(0, 64, 2), :] + pool[h, pl.ds(1, 64, 2), :] for h in range(2)], axis=1)
    washed = exact_dot(rows, pairs) * 0.125
    for i in range(4):
        perf[i] = washed[i * 16 : i * 16 + 16]
    to, every = Sender(x_one, x_two, 0), pl.ds(0, 256)
    for c in range(2):
        for k in range(2):
            to.put(pl.ds((c * 2 + k) * 32, 32), every, it[c, 6 + k], it[c, k])
    to.put(pl.ds(XB_CODE, 32), every, codes[7].astype(F32), codes[0].astype(F32))
    for k in range(2):
        for c in range(2):
            to.put(pl.ds(XB_COARSE + 16 * k, 16), pl.ds(128 * c, 128), co[c, 2 + k], co[c, k])
    for i in range(4):
        for k, value in enumerate((theta[i], washed[i * 16 : i * 16 + 16])):
            to.put(pl.ds(XB_THERM + 16 * i, 16), pl.ds(128 * k, 128), value, value)
    block = Columns(it, co, codes, theta, perf, None)
    block.send_y(Sender(y_one, y_two, 1), OWN, range(2, 10), range(1, 9), range(2, 6), range(4, 8))


class Columns:
    def __init__(self, it, co, codes, theta, perf, beside):
        self.it, self.co, self.codes, self.theta, self.perf, self.beside = it, co, codes, theta, perf, beside

    def iterate(self, c, f, at, n):
        if 2 <= f < 10:
            return self.it[c, f - 2, pl.ds(at, n), :]
        side, k = (self.beside.before, f) if f < 2 else (self.beside.after, f - 10)
        return side(pl.ds((c * 2 + k) * 32 + at, n), pl.ds(0, 256))

    def code(self, f, at, n):
        if 1 <= f < 9:
            return self.codes[f - 1, pl.ds(at, n), :].astype(F32)
        side = self.beside.before if f < 1 else self.beside.after
        return side(pl.ds(XB_CODE + at, n), pl.ds(0, 256))

    def coarse(self, c, f, at, n):
        if 2 <= f < 6:
            return self.co[c, f - 2, pl.ds(at, n), :]
        side, k = (self.beside.before, f) if f < 2 else (self.beside.after, f - 6)
        return side(pl.ds(XB_COARSE + 16 * k + at, n), pl.ds(128 * c, 128))

    def warm(self, f, at, n):
        if 4 <= f < 8:
            return self.theta[f - 4, pl.ds(at, n), :]
        side, k = (self.beside.before, f) if f < 4 else (self.beside.after, f - 8)
        return side(pl.ds(XB_THERM + 16 * k + at, n), pl.ds(0, 128))

    def wash(self, f, at, n):
        if 3 <= f < 7:
            return self.perf[f - 3, pl.ds(at, n), :]
        side, k = (self.beside.before, f + 1) if f < 3 else (self.beside.after, f - 7)
        return side(pl.ds(XB_THERM + 16 * k + at, n), pl.ds(128, 128))

    def send_y(self, to, start, iterates, codes, coarses, thermals):
        every = pl.ds(0, 256)
        for c in range(2):
            for k, f in enumerate(iterates):
                rows = pl.ds((c * len(iterates) + k) * 8, 8)
                to.put(rows, every, self.iterate(c, f, 24, 8), self.iterate(c, f, 0, 8))
        for k, f in enumerate(codes):
            to.put(pl.ds(start[0] + k * 8, 8), every, self.code(f, 24, 8), self.code(f, 0, 8))
        for k, f in enumerate(coarses):
            for c in range(2):
                rows = pl.ds(start[1] + k * 8, 8)
                to.put(rows, pl.ds(128 * c, 128), self.coarse(c, f, 8, 8), self.coarse(c, f, 0, 8))
        for k, f in enumerate(thermals):
            rows = pl.ds(start[2] + k * 4, 4)
            to.put(rows, pl.ds(0, 128), self.warm(f, 12, 4), self.warm(f, 0, 4))
            if 1 <= f < 11:
                to.put(rows, pl.ds(128, 128), self.wash(f - 1, 12, 4), self.wash(f - 1, 0, 4))
            else:
                to.put(rows, pl.ds(128, 128), jnp.zeros((4, 128), F32), jnp.zeros((4, 128), F32))


FAR_LAYERS = ((0, 1, 10, 11), (0, 9), (0, 1, 6, 7), (0, 1, 2, 3, 8, 9, 10, 11))
OWN_LAYERS = (tuple(range(2, 10)), tuple(range(1, 9)), tuple(range(2, 6)), tuple(range(4, 8)))


def pack_y(it, co, codes, theta, perf, x_one, x_two, one, two):
    block = Columns(it, co, codes, theta, perf, Receiver(x_one, x_two, 0))
    block.send_y(Sender(one, two, 1), FAR, *FAR_LAYERS)


def rows_of(wide, narrow, start, count, half):
    parts = []
    if start < WIDE:
        n = min(count, WIDE - start)
        parts.append(wide[pl.ds(start, n), pl.ds(128 * half, 128)])
        start, count = start + n, count - n
    if count:
        parts.append(narrow[pl.ds(start - WIDE, count), :])
    return parts[0] if len(parts) == 1 else jnp.concatenate(parts, axis=0)


def pack_z(it, co, codes, theta, perf, x_one, x_two, own_one, own_two, far_one, far_two, after_this, wide, narrow, one, two):
    block = Columns(it, co, codes, theta, perf, Receiver(x_one, x_two, 0))
    own, far = Receiver(own_one, own_two, 1), Receiver(far_one, far_two, 1)

    def beside(kind, f, height, lanes, part=0):
        at, layers, start = (own, OWN_LAYERS[kind], OWN) if f in OWN_LAYERS[kind] else (far, FAR_LAYERS[kind], FAR)
        row = (start[kind - 1] if kind else part * len(layers) * height) + layers.index(f) * height
        return at.after(pl.ds(row, height), lanes), at.before(pl.ds(row, height), lanes)

    every = pl.ds(0, 256)
    for c in range(2):
        for f in range(FX):
            at = (c * FX + f) * 48
            wide[pl.ds(at, 32), :] = block.iterate(c, f, 0, 32)
            wide[pl.ds(at + 32, 8), :], wide[pl.ds(at + 40, 8), :] = beside(0, f, 8, every, c)
    for f in range(CX):
        at = N_CODE + f * 48
        wide[pl.ds(at, 32), :] = block.code(f, 0, 32)
        wide[pl.ds(at + 32, 8), :], wide[pl.ds(at + 40, 8), :] = beside(1, f, 8, every)
    row = iota((8, 128), 0)
    for c in range(2):
        for f in range(LX):
            at = N_COARSE + (c * LX + f) * 32
            over, under = beside(2, f, 8, pl.ds(128 * c, 128))
            narrow[pl.ds(at, 16), :] = block.coarse(c, f, 0, 16)
            narrow[pl.ds(at + 16, 8), :] = jnp.where(row < 4, over, under)
            last = jnp.where(row == 1, jnp.broadcast_to(over[4:5], (8, 128)), 0.0)
            narrow[pl.ds(at + 24, 8), :] = jnp.where(row == 0, jnp.broadcast_to(under[3:4], (8, 128)), last)
    for f in range(TX):
        at = N_THETA + f * 24
        narrow[pl.ds(at, 16), :] = block.warm(f, 0, 16)
        narrow[pl.ds(at + 16, 4), :], narrow[pl.ds(at + 20, 4), :] = beside(3, f, 4, pl.ds(0, 128))
    for f in range(QX):
        at = N_PERF + f * 24
        narrow[pl.ds(at, 16), :] = block.wash(f, 0, 16)
        narrow[pl.ds(at + 16, 4), :], narrow[pl.ds(at + 20, 4), :] = beside(3, f + 1, 4, pl.ds(128, 128))
    narrow[pl.ds(N_PERF + QX * 24, NARROW - N_PERF - QX * 24), :] = jnp.zeros((NARROW - N_PERF - QX * 24, 128), F32)
    lane = iota((ZB, 128), 1) // 8
    ends = []
    for half, shift in ((1, 8), (0, 0)):
        packed = None
        for g in range(GROUPS):
            part = rows_of(wide, narrow, g * ZB, ZB, half)
            turn = (8 * g + shift) % 128
            part = pltpu.roll(part, turn, 1) if turn else part
            packed = part if packed is None else jnp.where(lane == g, part, packed)
        ends.append(packed)
    Sender(one, two, 2).put(pl.ds(0, ZB), pl.ds(0, 128), *ends)


def sources(loc_h, exc_h, after_this, field, spread, gather, loc_s, exc_s, loc, sems):
    loads = [
        pltpu.make_async_copy(src, dst, sems.at[k])
        for k, (src, dst) in enumerate(((loc_h, loc), (loc_h, loc_s), (exc_h, exc_s)))
    ]
    for load in loads:
        load.start()
    field[...] = jnp.zeros(field.shape, F32)
    coord = [lax.axis_index(name) for name in AXES]
    for load in loads:
        load.wait()
    first = loc[0:1, :] - coord[0] * 8
    second = loc[1:2, :] - coord[1] * 32
    third = loc[2:3, :] - coord[2] * 256
    near = (first >= -1) & (first < 9) & (second >= -7) & (second < 39) & (third >= -7) & (third < 263)
    order = iota((1, 1024), 1)
    lane = iota((1, 384), 1)

    def place(state):
        e, keys = state
        x = loc_s[0, e] - coord[0] * 8 + 1
        y = loc_s[1, e] - coord[1] * 32
        z = loc_s[2, e] - coord[2] * 256
        y = jnp.where(y < 0, y + 48, y)
        z = jnp.where(z < 0, z + 384, z)
        for c in range(2):
            field[c, x, pl.ds(y, 1), :] += jnp.where(lane == z, exc_s[c, e], 0.0)
        keys = jnp.where(order == e, 1024, keys)
        return jnp.min(keys), keys

    keys = jnp.where(near, order, 1024)
    lax.while_loop(lambda state: state[0] < 1024, place, (jnp.min(keys), keys))

    k, f = iota((256, 384), 0), iota((256, 384), 1)
    cell = jnp.where(f < 320, f, f - 384)
    centre = cell >> 1
    beside = centre + jnp.where((cell & 1) == 1, 1, -1)
    weight = jnp.where(k == (centre & 255), 0.75, jnp.where(k == (beside & 255), 0.25, 0.0))
    spread[...] = weight.astype(BF16)
    f, k = iota((384, 256), 0), iota((384, 256), 1)
    cell = jnp.where(f < 320, f, f - 384)
    gather[...] = jnp.where(k == ((cell >> 1) & 255), 1.0, 0.0).astype(BF16)


def smooth(wave_t, damp_t, wide, narrow, z_one, z_two, source, spread, gather,
           out, power, one, two, tiles, halo, grown, fine, first, second, gain_r, gain_i, pool):
    coord = [lax.axis_index(name) for name in AXES]
    lane = iota((ZB, 128), 1)
    came = Receiver(z_one, z_two, 2)
    right, left = came.after(pl.ds(0, ZB), pl.ds(0, 128)), came.before(pl.ds(0, ZB), pl.ds(0, 128))
    for g in range(GROUPS):
        turn = (128 - 8 * g) % 128
        after = pltpu.roll(right, turn, 1) if turn else right
        turn = (120 - 8 * g) % 128
        before = pltpu.roll(left, turn, 1) if turn else left
        halo[pl.ds(g * ZB, ZB), :] = jnp.where(lane < 8, after, jnp.where(lane >= 120, before, 0.0))
    tiles[...] = halo[pl.ds(WIDE + N_THETA, NARROW - N_THETA), :]

    def flag(test):
        return jnp.where(test, 1.0, 0.0)

    x_before, x_after = flag(coord[0] > 0), flag(coord[0] < 3)
    y_before, y_after = flag(coord[1] > 0), flag(coord[1] < 15)
    z_before, z_after = flag(coord[2] > 0), flag(coord[2] < 3)

    row, col = iota((32, 256), 0), iota((32, 256), 1)
    y_ok = jnp.where(row < 16, 1.0, jnp.where((row < 20) | (row == 25), y_after, y_before))
    z_ok = jnp.where(col < 128, 1.0, jnp.where(col < 192, z_after, z_before))
    inside = y_ok * z_ok
    row = iota((24, 256), 0)
    for c in range(2):
        for f in range(LX):
            at = N_COARSE + (c * LX + f) * 32
            cells = jnp.concatenate([narrow[pl.ds(at, 32), :], halo[pl.ds(WIDE + at, 32), :]], axis=1)
            x_ok = x_before if f < 2 else x_after if f >= 6 else None
            cells = cells * (inside if x_ok is None else inside * x_ok)
            centre = cells[0:24]
            lower = jnp.where(row == 20, jnp.broadcast_to(cells[24:25], (24, 256)), pltpu.roll(centre, 1, 0))
            upper = jnp.where(row == 19, jnp.broadcast_to(cells[25:26], (24, 256)), pltpu.roll(centre, 23, 0))
            even = 0.75 * centre + 0.25 * lower
            odd = 0.75 * centre + 0.25 * upper
            for half in range(2):
                to = (c * LX + f) * 48
                grown[half, pl.ds(to, 24, 2), :] = even[:, half * 128 : half * 128 + 128]
                grown[half, pl.ds(to + 1, 24, 2), :] = odd[:, half * 128 : half * 128 + 128]
    fine[...] = exact_dot(jnp.concatenate([grown[0], grown[1]], axis=1), spread[...])

    row, col = iota((48, 384), 0), iota((48, 384), 1)
    y_ok = jnp.where(row < 32, 1.0, jnp.where(row < 40, y_after, y_before))
    z_ok = jnp.where(col < 256, 1.0, jnp.where(col < 320, z_after, z_before))
    inside = y_ok * z_ok
    for c in range(2):
        for f in range(FX):
            at = (c * FX + f) * 48
            start = jnp.concatenate([wide[pl.ds(at, 48), :], halo[pl.ds(at, 48), :]], axis=1)
            near = c * LX + f // 2 + 1
            far = near + (1 if f % 2 else -1)
            grow = 0.75 * fine[pl.ds(near * 48, 48), :] + 0.25 * fine[pl.ds(far * 48, 48), :]
            x_ok = x_before if f < 2 else x_after if f >= 10 else None
            first[c, f] = (start + grow) * (inside if x_ok is None else inside * x_ok)

    gains_r, gains_i, damps = [], [], []
    for t in range(4):
        speed = jnp.full((8, 128), wave_t[t], F32)
        damp = jnp.full((8, 128), damp_t[t], F32)
        wave = 1.0 / (speed * speed)
        diag_r = 6.0 - wave
        diag_i = DAMPING_SHIFT * wave + damp
        modulus = diag_r * diag_r + diag_i * diag_i
        gains_r.append((RELAXATION * diag_r / modulus)[0:1, 0:1])
        gains_i.append((RELAXATION * diag_i / modulus)[0:1, 0:1])
        damps.append(damp_t[t])

    def step(cells, at, drive_r, drive_i, g_r, g_i):
        sums = []
        for c, drive in ((0, drive_r), (1, drive_i)):
            mid = cells[c, at]
            total = cells[c, at - 1] + cells[c, at + 1] + drive
            total = total + pltpu.roll(mid, 1, 0) + pltpu.roll(mid, 47, 0)
            sums.append((mid, total + pltpu.roll(mid, 1, 1) + pltpu.roll(mid, 383, 1)))
        (mid_r, sum_r), (mid_i, sum_i) = sums
        keep = 1.0 - RELAXATION
        return keep * mid_r + (g_r * sum_r + g_i * sum_i), keep * mid_i + (g_r * sum_i - g_i * sum_r)

    def classes(f):
        at = N_CODE + f * 48
        return jnp.concatenate([wide[pl.ds(at, 48), :], halo[pl.ds(at, 48), :]], axis=1)

    for f in range(CX):
        codes = classes(f)
        x_ok = x_before if f < 1 else x_after if f >= 9 else None
        ok = inside if x_ok is None else inside * x_ok
        g_r = pick(codes, gains_r) * ok
        g_i = pick(codes, gains_i) * ok
        gain_r[f], gain_i[f] = g_r, g_i
        second[0, f], second[1, f] = step(first, f + 1, source[0, f], source[1, f], g_r, g_i)

    for i in range(4):
        heat = None
        for f in (2 * i, 2 * i + 1):
            new_r, new_i = step(second, f + 1, source[0, f + 1], source[1, f + 1], gain_r[f + 1], gain_i[f + 1])
            out[0, f] = new_r[0:32, 0:256]
            out[1, f] = new_i[0:32, 0:256]
            layer = pick(classes(f + 1), damps) * (new_r * new_r + new_i * new_i)
            heat = layer if heat is None else heat + layer
        for third in range(3):
            pool[third, pl.ds(i * 48, 48), :] = heat[:, third * 128 : third * 128 + 128]
    sums = jnp.concatenate([pool[t, pl.ds(0, 96, 2), :] + pool[t, pl.ds(1, 96, 2), :] for t in range(3)], axis=1)
    sums = exact_dot(sums, gather[...]) * 0.125
    for i in range(4):
        power[i] = sums[i * 24 : i * 24 + 24]
    Sender(one, two, 0).put(pl.ds(0, 72), pl.ds(0, 256), sums[24:96], sums[0:72])


def bioheat(narrow, tiles, power, x_one, x_two, injury, wave, warm_out, dose_out, wave_out, now, later, sem):
    store = pltpu.make_async_copy(wave, wave_out, sem)
    store.start()
    coord = [lax.axis_index(name) for name in AXES]
    came = Receiver(x_one, x_two, 0)
    layer = [(pl.ds(24 * k, 24), pl.ds(0, 256)) for k in range(3)]
    heats = [None] + [came.before(*at) for at in layer] + [power[i] for i in range(4)] + [came.after(*at) for at in layer]

    def flag(test):
        return jnp.where(test, 1.0, 0.0)

    x_before, x_after = flag(coord[0] > 0), flag(coord[0] < 3)
    row, col = iota((24, 256), 0), iota((24, 256), 1)
    y_ok = jnp.where(row < 16, 1.0, jnp.where(row < 20, flag(coord[1] < 15), flag(coord[1] > 0)))
    z_ok = jnp.where(col < 128, 1.0, jnp.where(col < 192, flag(coord[2] < 3), flag(coord[2] > 0)))
    inside = y_ok * z_ok
    edge = [inside * (x_before if f < 4 else x_after) if not 4 <= f < 8 else inside for f in range(TX)]

    def extended(base, f):
        at = base + f * 24
        return jnp.concatenate([narrow[pl.ds(at, 24), :], tiles[pl.ds(at - N_THETA, 24), :]], axis=1)

    for f in range(TX):
        now[f] = extended(N_THETA, f) * edge[f]
    dose = [injury[i] for i in range(4)]
    state, other = now, later
    for turn in range(4):
        for f in range(1 + turn, TX - 1 - turn):
            mid = state[f]
            beside = state[f - 1] + state[f + 1]
            beside = beside + pltpu.roll(mid, 1, 0) + pltpu.roll(mid, 23, 0)
            beside = beside + pltpu.roll(mid, 1, 1) + pltpu.roll(mid, 255, 1)
            heat = heats[f]
            wash = extended(N_PERF, f - 1)
            new = mid + DIFFUSION * (beside - 6.0 * mid) - wash * mid + HEATING * heat
            other[f] = new * edge[f]
            if 4 <= f < 8:
                own = new[0:16, 0:128]
                dose[f - 4] = dose[f - 4] + jnp.exp(LN_PREFACTOR - ENERGY_BARRIER / (CORE_WARMTH + own))
                if turn == 3:
                    warm_out[f - 4] = own
        state, other = other, state
    for i in range(4):
        dose_out[i] = jnp.log(dose[i])
    store.wait()


def shaped(*shape, dtype=F32):
    return jax.ShapeDtypeStruct(shape, dtype)


def call(kernel, name, in_specs, outs, scratch=(), out_specs=None, cost=2000):
    return pl.pallas_call(
        kernel,
        name=name,
        out_shape=tuple(outs),
        in_specs=in_specs,
        out_specs=tuple(out_specs or [vmem() for _ in outs]),
        scratch_shapes=list(scratch),
        cost_estimate=pl.CostEstimate(flops=cost * 1000, bytes_accessed=cost * 1000, transcendentals=0),
        compiler_params=pltpu.CompilerParams(vmem_limit_bytes=24 * 1024 * 1024),
    )


def on_device(
    acoustic_iterate,
    coarse_update,
    class_codes_volume,
    element_location,
    element_excitation,
    class_wavespeed,
    class_damping,
    washout_fraction,
    thermal_excess,
    injury_integral,
):
    def in_hbm(*arrays):
        return [pltpu.with_memory_space_constraint(array, pltpu.HBM) for array in arrays]

    *sent, perf, it, co, codes, theta = call(
        pack_x, "pack_x", [hbm()] * 5,
        [
            shaped(XB, 256),
            shaped(XB, 256),
            shaped(OWN[3], 256),
            shaped(OWN[3], 256),
            shaped(4, 16, 128),
            shaped(2, 8, 32, 256),
            shaped(2, 4, 16, 128),
            shaped(8, 32, 256, dtype=jnp.int32),
            shaped(4, 16, 128),
        ],
        [pltpu.VMEM((2, 128, 128), F32), pltpu.SMEM((4,), F32), pltpu.SemaphoreType.DMA((5,))],
    )(*in_hbm(washout_fraction, acoustic_iterate, coarse_update, class_codes_volume, thermal_excess))
    own = (it, co, codes, theta, perf)
    x_came = exchange(sent[:2], 0)
    y_came = exchange(sent[2:], 1)

    sent = call(pack_y, "pack_y", [vmem()] * 7, [shaped(FAR[3], 256)] * 2)(*own, *x_came)
    field, spread, gather = call(
        sources, "sources", [hbm(), hbm(), vmem()],
        [shaped(2, CX, 48, 384), shaped(256, 384, dtype=BF16), shaped(384, 256, dtype=BF16)],
        [
            pltpu.SMEM((3, 1024), jnp.int32),
            pltpu.SMEM((2, 1024), F32),
            pltpu.VMEM((3, 1024), jnp.int32),
            pltpu.SemaphoreType.DMA((3,)),
        ],
        cost=8000,
    )(*in_hbm(element_location.T, element_excitation), sent[0])
    far_came = exchange(sent, 1)

    wide, narrow, *sent = call(
        pack_z, "pack_z", [vmem()] * 12,
        [shaped(WIDE, 256), shaped(NARROW, 128), shaped(ZB, 128), shaped(ZB, 128)],
    )(*own, *x_came, *y_came, *far_came, gather)
    z_came = exchange(sent, 2)

    pressure, power, *sent, tiles = call(
        smooth, "smooth", [smem()] * 2 + [vmem()] * 7,
        [
            shaped(2, 8, 32, 256),
            shaped(4, 24, 256),
            shaped(72, 256),
            shaped(72, 256),
            shaped(NARROW - N_THETA, 128),
        ],
        [
            pltpu.VMEM((WIDE + NARROW, 128), F32),
            pltpu.VMEM((2, 2 * LX * 48, 128), F32),
            pltpu.VMEM((2 * LX * 48, 384), F32),
            pltpu.VMEM((2, FX, 48, 384), F32),
            pltpu.VMEM((2, CX, 48, 384), F32),
            pltpu.VMEM((CX, 48, 384), F32),
            pltpu.VMEM((CX, 48, 384), F32),
            pltpu.VMEM((3, 192, 128), F32),
        ],
    )(class_wavespeed, class_damping, wide, narrow, *z_came, field, spread, gather)
    x_came = exchange(sent, 0)

    warmth, dose, pressure = call(
        bioheat, "bioheat", [vmem()] * 7,
        [shaped(4, 16, 128), shaped(4, 16, 128), shaped(2, 8, 32, 256)],
        [pltpu.VMEM((TX, 24, 256), F32), pltpu.VMEM((TX, 24, 256), F32), pltpu.SemaphoreType.DMA],
        [vmem(), vmem(), hbm()],
    )(narrow, tiles, power, *x_came, injury_integral, pressure)
    return pressure, warmth, dose


def solution(mesh):
    placed = (
        P(None, "gx", "gy", "gz"),
        P(None, "gx", "gy", "gz"),
        P("gx", "gy", "gz"),
        P(),
        P(),
        P(),
        P(),
        P(),
        P("gx", "gy", "gz"),
        P("gx", "gy", "gz"),
    )
    return jax.shard_map(
        on_device,
        mesh=mesh,
        in_specs=placed,
        out_specs=(P(None, "gx", "gy", "gz"), P("gx", "gy", "gz"), P("gx", "gy", "gz")),
        check_vma=False,
    )
```

```python
import jax
import jax.numpy as jnp
from jax import lax
from jax.experimental import pallas as pl
from jax.experimental.pallas import tpu as pltpu
from jax.sharding import PartitionSpec as P

F32 = jnp.float32
BF16 = jnp.bfloat16

RELAXATION = 0.8
DAMPING_SHIFT = 0.5
DIFFUSION = 0.15
HEATING = 0.25
LN_PREFACTOR = 226.78
ENERGY_BARRIER = 75535.0
CORE_WARMTH = 310.15

FX, CX, LX, TX, QX = 12, 10, 8, 12, 10
XB_CODE, XB_COARSE, XB_THERM, XB = 128, 160, 192, 256
YB_CODE, YB_COARSE, YB_THERM, YB = 128, 192, 212, 232
KB_CODE, KB_COARSE, KB_THERM, KB = 64, 80, 100, 128
WIDE = 2 * FX * 48 + CX * 48
N_CODE = 2 * FX * 48
N_COARSE, N_THETA, N_PERF, NARROW = 0, 512, 800, 1056
GROUPS = 16
ZB = (WIDE + NARROW) // GROUPS
AXES = ("gx", "gy", "gz")


def vmem():
    return pl.BlockSpec(memory_space=pltpu.VMEM)


def hbm():
    return pl.BlockSpec(memory_space=pltpu.HBM)


def smem():
    return pl.BlockSpec(memory_space=pltpu.SMEM)


def swaps(sizes, axis, odd):
    count, targets = 1, []
    for n in sizes:
        count *= n
    for i in range(count):
        place, rest = [], i
        for n in reversed(sizes):
            place.insert(0, rest % n)
            rest //= n
        partner = list(place)
        partner[axis] = ((place[axis] + 1) ^ 1) - 1 if odd else place[axis] ^ 1
        if not 0 <= partner[axis] < sizes[axis]:
            other = 2 if axis != 2 else 0
            partner = list(place)
            partner[other] = place[other] ^ 1
        j = 0
        for n, at in zip(sizes, partner):
            j = j * n + at
        targets.append((i, j))
    return targets


def exchange(pair, axis):
    sizes = [lax.axis_size(name) for name in AXES]
    return [lax.ppermute(buffer, AXES, swaps(sizes, axis, (axis == 1) != (k == 1))) for k, buffer in enumerate(pair)]


def is_even(axis):
    return lax.axis_index(AXES[axis]) % 2 == (1 if axis == 1 else 0)


class Sender:
    def __init__(self, first, second, axis):
        self.first, self.second, self.even = first, second, is_even(axis)

    def put(self, rows, lanes, up, down):
        self.first[rows, lanes] = jnp.where(self.even, up, down)
        self.second[rows, lanes] = jnp.where(self.even, down, up)


class Receiver:
    def __init__(self, first, second, axis):
        self.first, self.second, self.even = first, second, is_even(axis)

    def before(self, *at):
        return jnp.where(self.even, self.second[at], self.first[at])

    def after(self, *at):
        return jnp.where(self.even, self.first[at], self.second[at])


def exact_dot(values, weights):
    high = values.astype(BF16)
    rest = values - high.astype(F32)
    mid = rest.astype(BF16)
    low = (rest - mid.astype(F32)).astype(BF16)
    total = jnp.dot(high, weights, preferred_element_type=F32)
    total = total + jnp.dot(mid, weights, preferred_element_type=F32)
    return total + jnp.dot(low, weights, preferred_element_type=F32)


def iota(shape, dim):
    return lax.broadcasted_iota(jnp.int32, shape, dim)


def pick(codes, entries):
    value = jnp.where(codes == 0.0, entries[0], entries[1])
    value = jnp.where(codes == 2.0, entries[2], value)
    return jnp.where(codes == 3.0, entries[3], value)


def pack_x(wash_h, it_h, co_h, codes_h, theta_h, x_one, x_two, y_one, y_two, perf, it, co, codes, theta, pool, wash, sems):
    loads = [
        pltpu.make_async_copy(src, dst, sems.at[k])
        for k, (src, dst) in enumerate(
            ((codes_h, codes), (it_h, it), (wash_h, wash), (co_h, co), (theta_h, theta))
        )
    ]
    for load in loads:
        load.start()
    lane, col = iota((256, 128), 0), iota((256, 128), 1)
    pairs = jnp.where(lane // 2 == col, 1.0, 0.0).astype(BF16)
    for load in loads:
        load.wait()
    entries = [wash[k] for k in range(4)]
    for i in range(4):
        both = pick(codes[2 * i].astype(F32), entries) + pick(codes[2 * i + 1].astype(F32), entries)
        for half in range(2):
            pool[half, i * 32 : i * 32 + 32, :] = both[:, half * 128 : half * 128 + 128]
    rows = jnp.concatenate([pool[h, pl.ds(0, 64, 2), :] + pool[h, pl.ds(1, 64, 2), :] for h in range(2)], axis=1)
    washed = exact_dot(rows, pairs) * 0.125
    for i in range(4):
        perf[i] = washed[i * 16 : i * 16 + 16]
    to, every = Sender(x_one, x_two, 0), pl.ds(0, 256)
    for c in range(2):
        for k in range(2):
            to.put(pl.ds((c * 2 + k) * 32, 32), every, it[c, 6 + k], it[c, k])
    to.put(pl.ds(XB_CODE, 32), every, codes[7].astype(F32), codes[0].astype(F32))
    for k in range(2):
        for c in range(2):
            to.put(pl.ds(XB_COARSE + 16 * k, 16), pl.ds(128 * c, 128), co[c, 2 + k], co[c, k])
    for i in range(4):
        for k, value in enumerate((theta[i], washed[i * 16 : i * 16 + 16])):
            to.put(pl.ds(XB_THERM + 16 * i, 16), pl.ds(128 * k, 128), value, value)
    to = Sender(y_one, y_two, 1)
    for c in range(2):
        for k in range(8):
            to.put(pl.ds((c * 8 + k) * 8, 8), every, it[c, k, 24:32, :], it[c, k, 0:8, :])
    for k in range(8):
        to.put(pl.ds(YB_CODE + k * 8, 8), every, codes[k, 24:32, :].astype(F32), codes[k, 0:8, :].astype(F32))
    for k in range(4):
        for c in range(2):
            to.put(pl.ds(YB_COARSE + k * 5, 5), pl.ds(128 * c, 128), co[c, k, 11:16, :], co[c, k, 0:5, :])
        for c, field in enumerate((theta, perf)):
            to.put(pl.ds(YB_THERM + k * 4, 4), pl.ds(128 * c, 128), field[k, 12:16, :], field[k, 0:4, :])


class Columns:
    def __init__(self, it, co, codes, theta, perf, beside):
        self.it, self.co, self.codes, self.theta, self.perf, self.beside = it, co, codes, theta, perf, beside

    def iterate(self, c, f, at, n):
        if 2 <= f < 10:
            return self.it[c, f - 2, pl.ds(at, n), :]
        side, k = (self.beside.before, f) if f < 2 else (self.beside.after, f - 10)
        return side(pl.ds((c * 2 + k) * 32 + at, n), pl.ds(0, 256))

    def code(self, f, at, n):
        if 1 <= f < 9:
            return self.codes[f - 1, pl.ds(at, n), :].astype(F32)
        side = self.beside.before if f < 1 else self.beside.after
        return side(pl.ds(XB_CODE + at, n), pl.ds(0, 256))

    def coarse(self, c, f, at, n):
        if 2 <= f < 6:
            return self.co[c, f - 2, pl.ds(at, n), :]
        side, k = (self.beside.before, f) if f < 2 else (self.beside.after, f - 6)
        return side(pl.ds(XB_COARSE + 16 * k + at, n), pl.ds(128 * c, 128))

    def warm(self, f, at, n):
        if 4 <= f < 8:
            return self.theta[f - 4, pl.ds(at, n), :]
        side, k = (self.beside.before, f) if f < 4 else (self.beside.after, f - 8)
        return side(pl.ds(XB_THERM + 16 * k + at, n), pl.ds(0, 128))

    def wash(self, f, at, n):
        if 3 <= f < 7:
            return self.perf[f - 3, pl.ds(at, n), :]
        side, k = (self.beside.before, f + 1) if f < 3 else (self.beside.after, f - 7)
        return side(pl.ds(XB_THERM + 16 * k + at, n), pl.ds(128, 128))


def pack_corner(y_one, y_two, after_this, one, two):
    came, to = Receiver(y_one, y_two, 1), Sender(one, two, 0)

    def put(at, n, lanes, up, down):
        for k, side in enumerate((came.after, came.before)):
            to.put(pl.ds(at + k * n, n), lanes, side(pl.ds(up, n), lanes), side(pl.ds(down, n), lanes))

    every = pl.ds(0, 256)
    for c in range(2):
        for k in range(2):
            put((c * 2 + k) * 16, 8, every, (c * 8 + 6 + k) * 8, (c * 8 + k) * 8)
    put(KB_CODE, 8, every, YB_CODE + 56, YB_CODE)
    for k in range(2):
        put(KB_COARSE + k * 10, 5, every, YB_COARSE + (2 + k) * 5, YB_COARSE + k * 5)
    for k in range(3):
        put(KB_THERM + k * 8, 4, every, YB_THERM + (1 + k) * 4, YB_THERM + k * 4)


def rows_of(wide, narrow, start, count, half):
    parts = []
    if start < WIDE:
        n = min(count, WIDE - start)
        parts.append(wide[pl.ds(start, n), pl.ds(128 * half, 128)])
        start, count = start + n, count - n
    if count:
        parts.append(narrow[pl.ds(start - WIDE, count), :])
    return parts[0] if len(parts) == 1 else jnp.concatenate(parts, axis=0)


def pack_z(it, co, codes, theta, perf, x_one, x_two, y_one, y_two, k_one, k_two, wide, narrow, one, two):
    block = Columns(it, co, codes, theta, perf, Receiver(x_one, x_two, 0))
    rows, corners = Receiver(y_one, y_two, 1), Receiver(k_one, k_two, 0)

    def beside(f, first, count, height, own, corner, lanes, skip=0):
        k = f - first
        if 0 <= k < count:
            at = pl.ds(own + k * height, height)
            return rows.after(at, lanes), rows.before(at, lanes)
        side, k = (corners.before, f - skip) if k < 0 else (corners.after, k - count)
        return [side(pl.ds(corner + (2 * k + j) * height, height), lanes) for j in range(2)]

    every = pl.ds(0, 256)
    for c in range(2):
        for f in range(FX):
            at = (c * FX + f) * 48
            wide[pl.ds(at, 32), :] = block.iterate(c, f, 0, 32)
            wide[pl.ds(at + 32, 8), :], wide[pl.ds(at + 40, 8), :] = beside(f, 2, 8, 8, c * 64, c * 32, every)
    for f in range(CX):
        at = N_CODE + f * 48
        wide[pl.ds(at, 32), :] = block.code(f, 0, 32)
        wide[pl.ds(at + 32, 8), :], wide[pl.ds(at + 40, 8), :] = beside(f, 1, 8, 8, YB_CODE, KB_CODE, every)
    for c in range(2):
        for f in range(LX):
            at = N_COARSE + (c * LX + f) * 32
            over, under = beside(f, 2, 4, 5, YB_COARSE, KB_COARSE, pl.ds(128 * c, 128))
            narrow[pl.ds(at, 16), :] = block.coarse(c, f, 0, 16)
            narrow[pl.ds(at + 24, 8), :] = jnp.zeros((8, 128), F32)
            narrow[pl.ds(at + 16, 4), :] = over[0:4]
            narrow[pl.ds(at + 20, 4), :] = under[1:5]
            narrow[pl.ds(at + 24, 1), :] = under[0:1]
            narrow[pl.ds(at + 25, 1), :] = over[4:5]
    for f in range(TX):
        at = N_THETA + f * 24
        narrow[pl.ds(at, 16), :] = block.warm(f, 0, 16)
        if 0 < f < 11:
            over, under = beside(f, 4, 4, 4, YB_THERM, KB_THERM, pl.ds(0, 128), 1)
        else:
            over = under = jnp.zeros((4, 128), F32)
        narrow[pl.ds(at + 16, 4), :], narrow[pl.ds(at + 20, 4), :] = over, under
    for f in range(QX):
        at = N_PERF + f * 24
        narrow[pl.ds(at, 16), :] = block.wash(f, 0, 16)
        over, under = beside(f + 1, 4, 4, 4, YB_THERM, KB_THERM, pl.ds(128, 128), 1)
        narrow[pl.ds(at + 16, 4), :], narrow[pl.ds(at + 20, 4), :] = over, under
    narrow[pl.ds(N_PERF + QX * 24, NARROW - N_PERF - QX * 24), :] = jnp.zeros((NARROW - N_PERF - QX * 24, 128), F32)
    lane = iota((ZB, 128), 1) // 8
    ends = []
    for half, shift in ((1, 8), (0, 0)):
        packed = None
        for g in range(GROUPS):
            part = rows_of(wide, narrow, g * ZB, ZB, half)
            turn = (8 * g + shift) % 128
            part = pltpu.roll(part, turn, 1) if turn else part
            packed = part if packed is None else jnp.where(lane == g, part, packed)
        ends.append(packed)
    Sender(one, two, 2).put(pl.ds(0, ZB), pl.ds(0, 128), *ends)


def strip_cell(lane):
    return jnp.where(lane < 32, lane, jnp.where(lane < 96, lane + 192, lane - 128))


def sources(loc_h, exc_h, after_this, field, strip, spread, gather, spread_strip, gather_strip, loc_s, exc_s, loc, sems):
    loads = [
        pltpu.make_async_copy(src, dst, sems.at[k])
        for k, (src, dst) in enumerate(((loc_h, loc), (loc_h, loc_s), (exc_h, exc_s)))
    ]
    for load in loads:
        load.start()
    field[...] = jnp.zeros(field.shape, F32)
    strip[...] = jnp.zeros(strip.shape, F32)
    coord = [lax.axis_index(name) for name in AXES]
    for load in loads:
        load.wait()
    first = loc[0:1, :] - coord[0] * 8
    second = loc[1:2, :] - coord[1] * 32
    third = loc[2:3, :] - coord[2] * 256
    near = (first >= -1) & (first < 9) & (second >= -7) & (second < 39) & (third >= -7) & (third < 263)
    order = iota((1, 1024), 1)
    lane, cell = iota((1, 256), 1), strip_cell(iota((1, 128), 1))

    def place(state):
        e, keys = state
        x = loc_s[0, e] - coord[0] * 8 + 1
        y = loc_s[1, e] - coord[1] * 32
        z = loc_s[2, e] - coord[2] * 256
        y = jnp.where(y < 0, y + 48, y)
        for c in range(2):
            field[c, x, pl.ds(y, 1), :] += jnp.where(lane == z, exc_s[c, e], 0.0)
            strip[c, x, pl.ds(y, 1), :] += jnp.where(cell == z, exc_s[c, e], 0.0)
        keys = jnp.where(order == e, 1024, keys)
        return jnp.min(keys), keys

    keys = jnp.where(near, order, 1024)
    lax.while_loop(lambda state: state[0] < 1024, place, (jnp.min(keys), keys))

    def weights(cell, column, at):
        centre = cell >> 1
        beside = centre + jnp.where((cell & 1) == 1, 1, -1)
        weight = jnp.where(column == at(centre), 0.75, jnp.where(column == at(beside), 0.25, 0.0))
        return weight.astype(BF16)

    spread[...] = weights(iota((128, 256), 1), iota((128, 256), 0), lambda c: c)
    spread_strip[...] = weights(
        strip_cell(iota((256, 128), 1)),
        iota((256, 128), 0),
        lambda c: jnp.where(c < 0, c + 256, jnp.where(c < 128, c, c + 64)),
    )
    gather[...] = jnp.where(iota((256, 128), 1) == iota((256, 128), 0) >> 1, 1.0, 0.0).astype(BF16)
    centre = strip_cell(iota((128, 256), 0)) >> 1
    centre = jnp.where(centre < 0, centre + 256, centre)
    gather_strip[...] = jnp.where(iota((128, 256), 1) == centre, 1.0, 0.0).astype(BF16)


def flag(test):
    return jnp.where(test, 1.0, 0.0)


def x_flags():
    at = lax.axis_index("gx")
    return flag(at > 0), flag(at < 3)


def along_y(cells, row):
    lanes = cells.shape[1]
    centre = cells[0:24]
    lower = jnp.where(row == 20, jnp.broadcast_to(cells[24:25], (24, lanes)), pltpu.roll(centre, 1, 0))
    upper = jnp.where(row == 19, jnp.broadcast_to(cells[25:26], (24, lanes)), pltpu.roll(centre, 23, 0))
    return 0.75 * centre + 0.25 * lower, 0.75 * centre + 0.25 * upper


def coarse_rows(read, z_ok, grown):
    x_before, x_after = x_flags()
    at_y = lax.axis_index("gy")
    row = iota((32, 128), 0)
    y_ok = jnp.where(row < 16, 1.0, jnp.where((row < 20) | (row == 25), flag(at_y < 15), flag(at_y > 0)))
    inside = y_ok if z_ok is None else y_ok * z_ok
    row = iota((24, 128), 0)
    for c in range(2):
        for f in range(LX):
            x_ok = x_before if f < 2 else x_after if f >= 6 else None
            even, odd = along_y(read((c * LX + f) * 32) * (inside if x_ok is None else inside * x_ok), row)
            to = (c * LX + f) * 48
            grown[pl.ds(to, 24, 2), :] = even
            grown[pl.ds(to + 1, 24, 2), :] = odd


def relax(width, start, classes, z_ok, fine, drive, wave_t, damp_t, first, second, gain_r, gain_i, pool, emit):
    x_before, x_after = x_flags()
    at_y = lax.axis_index("gy")
    row = iota((48, width), 0)
    inside = jnp.where(row < 32, 1.0, jnp.where(row < 40, flag(at_y < 15), flag(at_y > 0)))
    if z_ok is not None:
        inside = inside * z_ok
    for c in range(2):
        for f in range(FX):
            near = c * LX + f // 2 + 1
            far = near + (1 if f % 2 else -1)
            grow = 0.75 * fine[pl.ds(near * 48, 48), :] + 0.25 * fine[pl.ds(far * 48, 48), :]
            x_ok = x_before if f < 2 else x_after if f >= 10 else None
            first[c, f] = (start((c * FX + f) * 48) + grow) * (inside if x_ok is None else inside * x_ok)

    gains_r, gains_i, damps = [], [], []
    for t in range(4):
        speed = jnp.full((8, 128), wave_t[t], F32)
        damp = jnp.full((8, 128), damp_t[t], F32)
        wave = 1.0 / (speed * speed)
        diag_r = 6.0 - wave
        diag_i = DAMPING_SHIFT * wave + damp
        modulus = diag_r * diag_r + diag_i * diag_i
        gains_r.append((RELAXATION * diag_r / modulus)[0:1, 0:1])
        gains_i.append((RELAXATION * diag_i / modulus)[0:1, 0:1])
        damps.append(damp_t[t])

    def step(cells, f, drive_f, g_r, g_i):
        sums = []
        for c in range(2):
            mid = cells[c, f]
            total = cells[c, f - 1] + cells[c, f + 1] + drive[c, drive_f]
            total = total + pltpu.roll(mid, 1, 0) + pltpu.roll(mid, 47, 0)
            sums.append((mid, total + pltpu.roll(mid, 1, 1) + pltpu.roll(mid, width - 1, 1)))
        (mid_r, sum_r), (mid_i, sum_i) = sums
        keep = 1.0 - RELAXATION
        return keep * mid_r + (g_r * sum_r + g_i * sum_i), keep * mid_i + (g_r * sum_i - g_i * sum_r)

    for f in range(CX):
        codes = classes(N_CODE + f * 48)
        x_ok = x_before if f < 1 else x_after if f >= 9 else None
        ok = inside if x_ok is None else inside * x_ok
        g_r = pick(codes, gains_r) * ok
        g_i = pick(codes, gains_i) * ok
        gain_r[f], gain_i[f] = g_r, g_i
        second[0, f], second[1, f] = step(first, f + 1, f, g_r, g_i)

    for i in range(4):
        heat = None
        for f in (2 * i, 2 * i + 1):
            new_r, new_i = step(second, f + 1, f + 1, gain_r[f + 1], gain_i[f + 1])
            emit(f, new_r, new_i)
            layer = pick(classes(N_CODE + (f + 1) * 48), damps) * (new_r * new_r + new_i * new_i)
            heat = layer if heat is None else heat + layer
        for tile in range(width // 128):
            pool[tile, pl.ds(i * 48, 48), :] = heat[:, tile * 128 : tile * 128 + 128]
    tiles = [pool[t, pl.ds(0, 96, 2), :] + pool[t, pl.ds(1, 96, 2), :] for t in range(width // 128)]
    return tiles[0] if len(tiles) == 1 else jnp.concatenate(tiles, axis=1)


def smooth_inner(wave_t, damp_t, wide, narrow, source, spread, gather, out, power, grown,
                 fine, first, second, gain_r, gain_i, pool):
    coarse_rows(lambda at: narrow[pl.ds(N_COARSE + at, 32), :], None, grown)
    fine[...] = exact_dot(grown[...], spread[...])

    def own(at):
        return wide[pl.ds(at, 48), :]

    def emit(f, new_r, new_i):
        out[0, f] = new_r[0:32]
        out[1, f] = new_i[0:32]

    sums = relax(256, own, own, None, fine, source, wave_t, damp_t, first, second, gain_r, gain_i, pool, emit)
    power[...] = exact_dot(sums, gather[...]) * 0.125


def smooth_ends(wave_t, damp_t, wide, z_one, z_two, source, spread, gather, inner, power_inner, grown,
                out, power, power_halo, one, two, tiles,
                halo, grown_halo, fine, first, second, gain_r, gain_i, pool):
    lane = iota((ZB, 128), 1)
    came, every = Receiver(z_one, z_two, 2), (pl.ds(0, ZB), pl.ds(0, 128))
    right, left = came.after(*every), came.before(*every)
    for g in range(GROUPS):
        turn = (192 - 8 * g) % 128
        after = pltpu.roll(right, turn, 1) if turn else right
        turn = (120 - 8 * g) % 128
        before = pltpu.roll(left, turn, 1) if turn else left
        halo[pl.ds(g * ZB, ZB), :] = jnp.where(lane < 96, after, before)
    beyond = halo[pl.ds(WIDE + N_THETA, NARROW - N_THETA), :]
    tiles[...] = jnp.where(iota(beyond.shape, 1) < 64, pltpu.roll(beyond, 64, 1), beyond)

    at_z = lax.axis_index("gz")
    after_ok, before_ok = flag(at_z < 3), flag(at_z > 0)
    z_ok = jnp.where(iota((32, 128), 1) < 96, after_ok, before_ok)
    coarse_rows(lambda at: halo[pl.ds(WIDE + N_COARSE + at, 32), :], z_ok, grown_halo)
    fine[...] = exact_dot(jnp.concatenate([grown[...], grown_halo[...]], axis=1), spread[...])

    lane = iota((48, 128), 1)

    def strip(at):
        ends = jnp.where(lane < 32, wide[pl.ds(at, 48), pl.ds(0, 128)], pltpu.roll(wide[pl.ds(at, 48), pl.ds(128, 128)], 64, 1))
        return jnp.where(lane < 64, ends, halo[pl.ds(at, 48), :])

    low, high = iota((32, 128), 1) < 8, iota((32, 128), 1) >= 120

    def emit(f, new_r, new_i):
        for c, new in enumerate((new_r[0:32], new_i[0:32])):
            out[c, f, :, pl.ds(0, 128)] = jnp.where(low, new, inner[c, f, :, pl.ds(0, 128)])
            out[c, f, :, pl.ds(128, 128)] = jnp.where(high, pltpu.roll(new, 64, 1), inner[c, f, :, pl.ds(128, 128)])

    z_ok = jnp.where(lane < 64, 1.0, jnp.where(lane < 96, after_ok, before_ok))
    live = jnp.where((lane < 72) | (lane >= 120), z_ok, 0.0)
    sums = relax(128, strip, strip, live, fine, source, wave_t, damp_t, first, second, gain_r, gain_i, pool, emit)
    sums = exact_dot(sums, gather[...]) * 0.125
    lane = iota((96, 128), 1)
    own = jnp.where((lane < 4) | (lane >= 124), sums[:, 0:128], power_inner[...])
    over = sums[:, 128:256]
    power[...], power_halo[...] = own, over

    def packed(first_layer):
        group, total = iota((24, 128), 1) // 16, None
        for k in range(3):
            at = (first_layer + k) * 24
            turned = pltpu.roll(over[at : at + 24], 16 * k + 8, 1)
            total = turned if total is None else jnp.where(group == k, turned, total)
        return total

    to, every = Sender(one, two, 0), pl.ds(0, 128)
    to.put(pl.ds(0, 72), every, own[24:96], own[0:72])
    to.put(pl.ds(72, 24), every, packed(1), packed(0))


def bioheat(narrow, tiles, power, power_halo, x_one, x_two, injury, wave, warm_out, dose_out, wave_out, now, later, sem):
    store = pltpu.make_async_copy(wave, wave_out, sem)
    store.start()
    coord = [lax.axis_index(name) for name in AXES]
    came = Receiver(x_one, x_two, 0)

    def sent(side, k):
        beyond = side(pl.ds(72, 24), pl.ds(0, 128))
        beyond = jnp.where(iota((24, 128), 1) // 16 == k, beyond, 0.0)
        return jnp.concatenate([side(pl.ds(24 * k, 24), pl.ds(0, 128)), pltpu.roll(beyond, 120 - 16 * k, 1)], axis=1)

    own = [jnp.concatenate([ref[pl.ds(24 * i, 24), :] for ref in (power, power_halo)], axis=1) for i in range(4)]
    heats = [None] + [sent(came.before, k) for k in range(3)] + own + [sent(came.after, k) for k in range(3)]

    x_before, x_after = flag(coord[0] > 0), flag(coord[0] < 3)
    row, col = iota((24, 256), 0), iota((24, 256), 1)
    y_ok = jnp.where(row < 16, 1.0, jnp.where(row < 20, flag(coord[1] < 15), flag(coord[1] > 0)))
    z_ok = jnp.where(col < 128, 1.0, jnp.where(col < 192, flag(coord[2] < 3), flag(coord[2] > 0)))
    inside = y_ok * z_ok
    edge = [inside * (x_before if f < 4 else x_after) if not 4 <= f < 8 else inside for f in range(TX)]

    def extended(base, f):
        at = base + f * 24
        return jnp.concatenate([narrow[pl.ds(at, 24), :], tiles[pl.ds(at - N_THETA, 24), :]], axis=1)

    for f in range(TX):
        now[f] = extended(N_THETA, f) * edge[f]
    dose = [injury[i] for i in range(4)]
    state, other = now, later
    for turn in range(4):
        for f in range(1 + turn, TX - 1 - turn):
            mid = state[f]
            beside = state[f - 1] + state[f + 1]
            beside = beside + pltpu.roll(mid, 1, 0) + pltpu.roll(mid, 23, 0)
            beside = beside + pltpu.roll(mid, 1, 1) + pltpu.roll(mid, 255, 1)
            heat = heats[f]
            wash = extended(N_PERF, f - 1)
            new = mid + DIFFUSION * (beside - 6.0 * mid) - wash * mid + HEATING * heat
            other[f] = new * edge[f]
            if 4 <= f < 8:
                own = new[0:16, 0:128]
                dose[f - 4] = dose[f - 4] + jnp.exp(LN_PREFACTOR - ENERGY_BARRIER / (CORE_WARMTH + own))
                if turn == 3:
                    warm_out[f - 4] = own
        state, other = other, state
    for i in range(4):
        dose_out[i] = jnp.log(dose[i])
    store.wait()


def shaped(*shape, dtype=F32):
    return jax.ShapeDtypeStruct(shape, dtype)


def call(kernel, name, in_specs, outs, scratch=(), out_specs=None, cost=2000):
    return pl.pallas_call(
        kernel,
        name=name,
        out_shape=tuple(outs),
        in_specs=in_specs,
        out_specs=tuple(out_specs or [vmem() for _ in outs]),
        scratch_shapes=list(scratch),
        cost_estimate=pl.CostEstimate(flops=cost * 1000, bytes_accessed=cost * 1000, transcendentals=0),
        compiler_params=pltpu.CompilerParams(vmem_limit_bytes=24 * 1024 * 1024),
    )


def on_device(
    acoustic_iterate,
    coarse_update,
    class_codes_volume,
    element_location,
    element_excitation,
    class_wavespeed,
    class_damping,
    washout_fraction,
    thermal_excess,
    injury_integral,
):
    def in_hbm(*arrays):
        return [pltpu.with_memory_space_constraint(array, pltpu.HBM) for array in arrays]

    *sent, perf, it, co, codes, theta = call(
        pack_x, "pack_x", [hbm()] * 5,
        [
            shaped(XB, 256),
            shaped(XB, 256),
            shaped(YB, 256),
            shaped(YB, 256),
            shaped(4, 16, 128),
            shaped(2, 8, 32, 256),
            shaped(2, 4, 16, 128),
            shaped(8, 32, 256, dtype=jnp.int32),
            shaped(4, 16, 128),
        ],
        [pltpu.VMEM((2, 128, 128), F32), pltpu.SMEM((4,), F32), pltpu.SemaphoreType.DMA((5,))],
    )(*in_hbm(washout_fraction, acoustic_iterate, coarse_update, class_codes_volume, thermal_excess))
    own = (it, co, codes, theta, perf)
    y_came = exchange(sent[2:], 1)
    x_came = exchange(sent[:2], 0)

    field, strip, *weights = call(
        sources, "sources", [hbm(), hbm(), vmem()],
        [
            shaped(2, CX, 48, 256),
            shaped(2, CX, 48, 128),
            shaped(128, 256, dtype=BF16),
            shaped(256, 128, dtype=BF16),
            shaped(256, 128, dtype=BF16),
            shaped(128, 256, dtype=BF16),
        ],
        [
            pltpu.SMEM((3, 1024), jnp.int32),
            pltpu.SMEM((2, 1024), F32),
            pltpu.VMEM((3, 1024), jnp.int32),
            pltpu.SemaphoreType.DMA((3,)),
        ],
        cost=8000,
    )(*in_hbm(element_location.T, element_excitation), perf)
    sent = call(pack_corner, "pack_corner", [vmem()] * 3, [shaped(KB, 256)] * 2)(*y_came, weights[0])
    corners = exchange(sent, 0)

    wide, narrow, *sent = call(
        pack_z, "pack_z", [vmem()] * 11,
        [shaped(WIDE, 256), shaped(NARROW, 128), shaped(ZB, 128), shaped(ZB, 128)],
    )(*own, *x_came, *y_came, *corners)
    z_came = exchange(sent, 2)

    def scratch(width):
        return [
            pltpu.VMEM((2 * LX * 48, width), F32),
            pltpu.VMEM((2, FX, 48, width), F32),
            pltpu.VMEM((2, CX, 48, width), F32),
            pltpu.VMEM((CX, 48, width), F32),
            pltpu.VMEM((CX, 48, width), F32),
            pltpu.VMEM((width // 128, 192, 128), F32),
        ]

    inner, power_inner, grown = call(
        smooth_inner, "smooth_inner", [smem()] * 2 + [vmem()] * 5,
        [shaped(2, 8, 32, 256), shaped(96, 128), shaped(2 * LX * 48, 128)],
        scratch(256),
    )(class_wavespeed, class_damping, wide, narrow, field, weights[0], weights[1])
    pressure, power, power_halo, *sent, tiles = call(
        smooth_ends, "smooth_ends", [smem()] * 2 + [vmem()] * 9,
        [
            shaped(2, 8, 32, 256),
            shaped(96, 128),
            shaped(96, 128),
            shaped(96, 128),
            shaped(96, 128),
            shaped(NARROW - N_THETA, 128),
        ],
        [pltpu.VMEM((WIDE + NARROW, 128), F32), pltpu.VMEM((2 * LX * 48, 128), F32)] + scratch(128),
    )(class_wavespeed, class_damping, wide, *z_came, strip, weights[2], weights[3], inner, power_inner, grown)
    x_came = exchange(sent, 0)

    warmth, dose, pressure = call(
        bioheat, "bioheat", [vmem()] * 8,
        [shaped(4, 16, 128), shaped(4, 16, 128), shaped(2, 8, 32, 256)],
        [pltpu.VMEM((TX, 24, 256), F32), pltpu.VMEM((TX, 24, 256), F32), pltpu.SemaphoreType.DMA],
        [vmem(), vmem(), hbm()],
    )(narrow, tiles, power, power_halo, *x_came, injury_integral, pressure)
    return pressure, warmth, dose


def solution(mesh):
    placed = (
        P(None, "gx", "gy", "gz"),
        P(None, "gx", "gy", "gz"),
        P("gx", "gy", "gz"),
        P(),
        P(),
        P(),
        P(),
        P(),
        P("gx", "gy", "gz"),
        P("gx", "gy", "gz"),
    )
    return jax.shard_map(
        on_device,
        mesh=mesh,
        in_specs=placed,
        out_specs=(P(None, "gx", "gy", "gz"), P("gx", "gy", "gz"), P("gx", "gy", "gz")),
        check_vma=False,
    )
```

```python
import jax
import jax.numpy as jnp
from jax import lax
from jax.experimental import pallas as pl
from jax.experimental.pallas import tpu as pltpu
from jax.sharding import PartitionSpec as P

F32 = jnp.float32
BF16 = jnp.bfloat16

RELAXATION = 0.8
DAMPING_SHIFT = 0.5
DIFFUSION = 0.15
HEATING = 0.25
LN_PREFACTOR = 226.78
ENERGY_BARRIER = 75535.0
CORE_WARMTH = 310.15

FX, CX, LX, TX, QX = 12, 10, 8, 12, 10
XB_CODE, XB_COARSE, XB_THERM, XB = 128, 160, 192, 256
YB_CODE, YB_COARSE, YB_THERM, YB = 128, 192, 212, 232
KB_CODE, KB_COARSE, KB_THERM, KB = 64, 80, 100, 128
WIDE = 2 * FX * 48 + CX * 48
N_CODE = 2 * FX * 48
N_COARSE, N_THETA, N_PERF, NARROW = 0, 512, 800, 1056
GROUPS = 16
ZB = (WIDE + NARROW) // GROUPS
AXES = ("gx", "gy", "gz")


def vmem():
    return pl.BlockSpec(memory_space=pltpu.VMEM)


def hbm():
    return pl.BlockSpec(memory_space=pltpu.HBM)


def smem():
    return pl.BlockSpec(memory_space=pltpu.SMEM)


def swaps(sizes, axis, odd):
    count, targets = 1, []
    for n in sizes:
        count *= n
    for i in range(count):
        place, rest = [], i
        for n in reversed(sizes):
            place.insert(0, rest % n)
            rest //= n
        partner = list(place)
        partner[axis] = ((place[axis] + 1) ^ 1) - 1 if odd else place[axis] ^ 1
        if not 0 <= partner[axis] < sizes[axis]:
            other = 2 if axis != 2 else 0
            partner = list(place)
            partner[other] = place[other] ^ 1
        j = 0
        for n, at in zip(sizes, partner):
            j = j * n + at
        targets.append((i, j))
    return targets


def exchange(pair, axis):
    sizes = [lax.axis_size(name) for name in AXES]
    return [lax.ppermute(buffer, AXES, swaps(sizes, axis, bool(k))) for k, buffer in enumerate(pair)]


def is_even(axis):
    return lax.axis_index(AXES[axis]) % 2 == 0


class Sender:
    def __init__(self, first, second, axis):
        self.first, self.second, self.even = first, second, is_even(axis)

    def put(self, rows, lanes, up, down):
        self.first[rows, lanes] = jnp.where(self.even, up, down)
        self.second[rows, lanes] = jnp.where(self.even, down, up)


class Receiver:
    def __init__(self, first, second, axis):
        self.first, self.second, self.even = first, second, is_even(axis)

    def before(self, *at):
        return jnp.where(self.even, self.second[at], self.first[at])

    def after(self, *at):
        return jnp.where(self.even, self.first[at], self.second[at])


def exact_dot(values, weights):
    high = values.astype(BF16)
    rest = values - high.astype(F32)
    mid = rest.astype(BF16)
    low = (rest - mid.astype(F32)).astype(BF16)
    total = jnp.dot(high, weights, preferred_element_type=F32)
    total = total + jnp.dot(mid, weights, preferred_element_type=F32)
    return total + jnp.dot(low, weights, preferred_element_type=F32)


def iota(shape, dim):
    return lax.broadcasted_iota(jnp.int32, shape, dim)


def pick(codes, entries):
    value = jnp.where(codes == 0.0, entries[0], entries[1])
    value = jnp.where(codes == 2.0, entries[2], value)
    return jnp.where(codes == 3.0, entries[3], value)


def pack_x(wash_h, it_h, co_h, codes_h, theta_h, x_one, x_two, y_one, y_two, perf, it, co, codes, theta, pool, wash, sems):
    loads = [
        pltpu.make_async_copy(src, dst, sems.at[k])
        for k, (src, dst) in enumerate(
            ((codes_h, codes), (it_h, it), (wash_h, wash), (co_h, co), (theta_h, theta))
        )
    ]
    for load in loads:
        load.start()
    lane, col = iota((256, 128), 0), iota((256, 128), 1)
    pairs = jnp.where(lane // 2 == col, 1.0, 0.0).astype(BF16)
    for load in loads:
        load.wait()
    entries = [wash[k] for k in range(4)]
    for i in range(4):
        both = pick(codes[2 * i].astype(F32), entries) + pick(codes[2 * i + 1].astype(F32), entries)
        for half in range(2):
            pool[half, i * 32 : i * 32 + 32, :] = both[:, half * 128 : half * 128 + 128]
    rows = jnp.concatenate([pool[h, pl.ds(0, 64, 2), :] + pool[h, pl.ds(1, 64, 2), :] for h in range(2)], axis=1)
    washed = exact_dot(rows, pairs) * 0.125
    for i in range(4):
        perf[i] = washed[i * 16 : i * 16 + 16]
    to, every = Sender(x_one, x_two, 0), pl.ds(0, 256)
    for c in range(2):
        for k in range(2):
            to.put(pl.ds((c * 2 + k) * 32, 32), every, it[c, 6 + k], it[c, k])
    to.put(pl.ds(XB_CODE, 32), every, codes[7].astype(F32), codes[0].astype(F32))
    for k in range(2):
        for c in range(2):
            to.put(pl.ds(XB_COARSE + 16 * k, 16), pl.ds(128 * c, 128), co[c, 2 + k], co[c, k])
    for i in range(4):
        for k, value in enumerate((theta[i], washed[i * 16 : i * 16 + 16])):
            to.put(pl.ds(XB_THERM + 16 * i, 16), pl.ds(128 * k, 128), value, value)
    to = Sender(y_one, y_two, 1)
    for c in range(2):
        for k in range(8):
            to.put(pl.ds((c * 8 + k) * 8, 8), every, it[c, k, 24:32, :], it[c, k, 0:8, :])
    for k in range(8):
        to.put(pl.ds(YB_CODE + k * 8, 8), every, codes[k, 24:32, :].astype(F32), codes[k, 0:8, :].astype(F32))
    for k in range(4):
        for c in range(2):
            to.put(pl.ds(YB_COARSE + k * 5, 5), pl.ds(128 * c, 128), co[c, k, 11:16, :], co[c, k, 0:5, :])
        for c, field in enumerate((theta, perf)):
            to.put(pl.ds(YB_THERM + k * 4, 4), pl.ds(128 * c, 128), field[k, 12:16, :], field[k, 0:4, :])


class Columns:
    def __init__(self, it, co, codes, theta, perf, beside):
        self.it, self.co, self.codes, self.theta, self.perf, self.beside = it, co, codes, theta, perf, beside

    def iterate(self, c, f, at, n):
        if 2 <= f < 10:
            return self.it[c, f - 2, pl.ds(at, n), :]
        side, k = (self.beside.before, f) if f < 2 else (self.beside.after, f - 10)
        return side(pl.ds((c * 2 + k) * 32 + at, n), pl.ds(0, 256))

    def code(self, f, at, n):
        if 1 <= f < 9:
            return self.codes[f - 1, pl.ds(at, n), :].astype(F32)
        side = self.beside.before if f < 1 else self.beside.after
        return side(pl.ds(XB_CODE + at, n), pl.ds(0, 256))

    def coarse(self, c, f, at, n):
        if 2 <= f < 6:
            return self.co[c, f - 2, pl.ds(at, n), :]
        side, k = (self.beside.before, f) if f < 2 else (self.beside.after, f - 6)
        return side(pl.ds(XB_COARSE + 16 * k + at, n), pl.ds(128 * c, 128))

    def warm(self, f, at, n):
        if 4 <= f < 8:
            return self.theta[f - 4, pl.ds(at, n), :]
        side, k = (self.beside.before, f) if f < 4 else (self.beside.after, f - 8)
        return side(pl.ds(XB_THERM + 16 * k + at, n), pl.ds(0, 128))

    def wash(self, f, at, n):
        if 3 <= f < 7:
            return self.perf[f - 3, pl.ds(at, n), :]
        side, k = (self.beside.before, f + 1) if f < 3 else (self.beside.after, f - 7)
        return side(pl.ds(XB_THERM + 16 * k + at, n), pl.ds(128, 128))


def pack_corner(y_one, y_two, after_this, one, two):
    came, to = Receiver(y_one, y_two, 1), Sender(one, two, 0)

    def put(at, n, lanes, up, down):
        for k, side in enumerate((came.after, came.before)):
            to.put(pl.ds(at + k * n, n), lanes, side(pl.ds(up, n), lanes), side(pl.ds(down, n), lanes))

    every = pl.ds(0, 256)
    for c in range(2):
        for k in range(2):
            put((c * 2 + k) * 16, 8, every, (c * 8 + 6 + k) * 8, (c * 8 + k) * 8)
    put(KB_CODE, 8, every, YB_CODE + 56, YB_CODE)
    for k in range(2):
        put(KB_COARSE + k * 10, 5, every, YB_COARSE + (2 + k) * 5, YB_COARSE + k * 5)
    for k in range(3):
        put(KB_THERM + k * 8, 4, every, YB_THERM + (1 + k) * 4, YB_THERM + k * 4)


def rows_of(wide, narrow, start, count, half):
    parts = []
    if start < WIDE:
        n = min(count, WIDE - start)
        parts.append(wide[pl.ds(start, n), pl.ds(128 * half, 128)])
        start, count = start + n, count - n
    if count:
        parts.append(narrow[pl.ds(start - WIDE, count), :])
    return parts[0] if len(parts) == 1 else jnp.concatenate(parts, axis=0)


def pack_z(it, co, codes, theta, perf, x_one, x_two, y_one, y_two, k_one, k_two, wide, narrow, one, two):
    block = Columns(it, co, codes, theta, perf, Receiver(x_one, x_two, 0))
    rows, corners = Receiver(y_one, y_two, 1), Receiver(k_one, k_two, 0)

    def beside(f, first, count, height, own, corner, lanes, skip=0):
        k = f - first
        if 0 <= k < count:
            at = pl.ds(own + k * height, height)
            return rows.after(at, lanes), rows.before(at, lanes)
        side, k = (corners.before, f - skip) if k < 0 else (corners.after, k - count)
        return [side(pl.ds(corner + (2 * k + j) * height, height), lanes) for j in range(2)]

    every = pl.ds(0, 256)
    for c in range(2):
        for f in range(FX):
            at = (c * FX + f) * 48
            wide[pl.ds(at, 32), :] = block.iterate(c, f, 0, 32)
            wide[pl.ds(at + 32, 8), :], wide[pl.ds(at + 40, 8), :] = beside(f, 2, 8, 8, c * 64, c * 32, every)
    for f in range(CX):
        at = N_CODE + f * 48
        wide[pl.ds(at, 32), :] = block.code(f, 0, 32)
        wide[pl.ds(at + 32, 8), :], wide[pl.ds(at + 40, 8), :] = beside(f, 1, 8, 8, YB_CODE, KB_CODE, every)
    for c in range(2):
        for f in range(LX):
            at = N_COARSE + (c * LX + f) * 32
            over, under = beside(f, 2, 4, 5, YB_COARSE, KB_COARSE, pl.ds(128 * c, 128))
            narrow[pl.ds(at, 16), :] = block.coarse(c, f, 0, 16)
            narrow[pl.ds(at + 24, 8), :] = jnp.zeros((8, 128), F32)
            narrow[pl.ds(at + 16, 4), :] = over[0:4]
            narrow[pl.ds(at + 20, 4), :] = under[1:5]
            narrow[pl.ds(at + 24, 1), :] = under[0:1]
            narrow[pl.ds(at + 25, 1), :] = over[4:5]
    for f in range(TX):
        at = N_THETA + f * 24
        narrow[pl.ds(at, 16), :] = block.warm(f, 0, 16)
        if 0 < f < 11:
            over, under = beside(f, 4, 4, 4, YB_THERM, KB_THERM, pl.ds(0, 128), 1)
        else:
            over = under = jnp.zeros((4, 128), F32)
        narrow[pl.ds(at + 16, 4), :], narrow[pl.ds(at + 20, 4), :] = over, under
    for f in range(QX):
        at = N_PERF + f * 24
        narrow[pl.ds(at, 16), :] = block.wash(f, 0, 16)
        over, under = beside(f + 1, 4, 4, 4, YB_THERM, KB_THERM, pl.ds(128, 128), 1)
        narrow[pl.ds(at + 16, 4), :], narrow[pl.ds(at + 20, 4), :] = over, under
    narrow[pl.ds(N_PERF + QX * 24, NARROW - N_PERF - QX * 24), :] = jnp.zeros((NARROW - N_PERF - QX * 24, 128), F32)
    lane = iota((ZB, 128), 1) // 8
    ends = []
    for half, shift in ((1, 8), (0, 0)):
        packed = None
        for g in range(GROUPS):
            part = rows_of(wide, narrow, g * ZB, ZB, half)
            turn = (8 * g + shift) % 128
            part = pltpu.roll(part, turn, 1) if turn else part
            packed = part if packed is None else jnp.where(lane == g, part, packed)
        ends.append(packed)
    Sender(one, two, 2).put(pl.ds(0, ZB), pl.ds(0, 128), *ends)


def strip_cell(lane):
    return jnp.where(lane < 32, lane, jnp.where(lane < 96, lane + 192, lane - 128))


def sources(loc_h, exc_h, after_this, field, strip, spread, gather, spread_strip, gather_strip, loc_s, exc_s, loc, sems):
    loads = [
        pltpu.make_async_copy(src, dst, sems.at[k])
        for k, (src, dst) in enumerate(((loc_h, loc), (loc_h, loc_s), (exc_h, exc_s)))
    ]
    for load in loads:
        load.start()
    field[...] = jnp.zeros(field.shape, F32)
    strip[...] = jnp.zeros(strip.shape, F32)
    coord = [lax.axis_index(name) for name in AXES]
    for load in loads:
        load.wait()
    first = loc[0:1, :] - coord[0] * 8
    second = loc[1:2, :] - coord[1] * 32
    third = loc[2:3, :] - coord[2] * 256
    near = (first >= -1) & (first < 9) & (second >= -7) & (second < 39) & (third >= -7) & (third < 263)
    order = iota((1, 1024), 1)
    lane, cell = iota((1, 256), 1), strip_cell(iota((1, 128), 1))

    def place(state):
        e, keys = state
        x = loc_s[0, e] - coord[0] * 8 + 1
        y = loc_s[1, e] - coord[1] * 32
        z = loc_s[2, e] - coord[2] * 256
        y = jnp.where(y < 0, y + 48, y)
        for c in range(2):
            field[c, x, pl.ds(y, 1), :] += jnp.where(lane == z, exc_s[c, e], 0.0)
            strip[c, x, pl.ds(y, 1), :] += jnp.where(cell == z, exc_s[c, e], 0.0)
        keys = jnp.where(order == e, 1024, keys)
        return jnp.min(keys), keys

    keys = jnp.where(near, order, 1024)
    lax.while_loop(lambda state: state[0] < 1024, place, (jnp.min(keys), keys))

    def weights(cell, column, at):
        centre = cell >> 1
        beside = centre + jnp.where((cell & 1) == 1, 1, -1)
        weight = jnp.where(column == at(centre), 0.75, jnp.where(column == at(beside), 0.25, 0.0))
        return weight.astype(BF16)

    spread[...] = weights(iota((128, 256), 1), iota((128, 256), 0), lambda c: c)
    spread_strip[...] = weights(
        strip_cell(iota((256, 128), 1)),
        iota((256, 128), 0),
        lambda c: jnp.where(c < 0, c + 256, jnp.where(c < 128, c, c + 64)),
    )
    gather[...] = jnp.where(iota((256, 128), 1) == iota((256, 128), 0) >> 1, 1.0, 0.0).astype(BF16)
    centre = strip_cell(iota((128, 256), 0)) >> 1
    centre = jnp.where(centre < 0, centre + 256, centre)
    gather_strip[...] = jnp.where(iota((128, 256), 1) == centre, 1.0, 0.0).astype(BF16)


def flag(test):
    return jnp.where(test, 1.0, 0.0)


def x_flags():
    at = lax.axis_index("gx")
    return flag(at > 0), flag(at < 3)


def along_y(cells, row):
    lanes = cells.shape[1]
    centre = cells[0:24]
    lower = jnp.where(row == 20, jnp.broadcast_to(cells[24:25], (24, lanes)), pltpu.roll(centre, 1, 0))
    upper = jnp.where(row == 19, jnp.broadcast_to(cells[25:26], (24, lanes)), pltpu.roll(centre, 23, 0))
    return 0.75 * centre + 0.25 * lower, 0.75 * centre + 0.25 * upper


def coarse_rows(read, z_ok, grown):
    x_before, x_after = x_flags()
    at_y = lax.axis_index("gy")
    row = iota((32, 128), 0)
    y_ok = jnp.where(row < 16, 1.0, jnp.where((row < 20) | (row == 25), flag(at_y < 15), flag(at_y > 0)))
    inside = y_ok if z_ok is None else y_ok * z_ok
    row = iota((24, 128), 0)
    for c in range(2):
        for f in range(LX):
            x_ok = x_before if f < 2 else x_after if f >= 6 else None
            even, odd = along_y(read((c * LX + f) * 32) * (inside if x_ok is None else inside * x_ok), row)
            to = (c * LX + f) * 48
            grown[pl.ds(to, 24, 2), :] = even
            grown[pl.ds(to + 1, 24, 2), :] = odd


def relax(width, start, classes, z_ok, fine, drive, wave_t, damp_t, first, second, gain_r, gain_i, pool, emit):
    x_before, x_after = x_flags()
    at_y = lax.axis_index("gy")
    row = iota((48, width), 0)
    inside = jnp.where(row < 32, 1.0, jnp.where(row < 40, flag(at_y < 15), flag(at_y > 0)))
    if z_ok is not None:
        inside = inside * z_ok
    for c in range(2):
        for f in range(FX):
            near = c * LX + f // 2 + 1
            far = near + (1 if f % 2 else -1)
            grow = 0.75 * fine[pl.ds(near * 48, 48), :] + 0.25 * fine[pl.ds(far * 48, 48), :]
            x_ok = x_before if f < 2 else x_after if f >= 10 else None
            first[c, f] = (start((c * FX + f) * 48) + grow) * (inside if x_ok is None else inside * x_ok)

    gains_r, gains_i, damps = [], [], []
    for t in range(4):
        speed = jnp.full((8, 128), wave_t[t], F32)
        damp = jnp.full((8, 128), damp_t[t], F32)
        wave = 1.0 / (speed * speed)
        diag_r = 6.0 - wave
        diag_i = DAMPING_SHIFT * wave + damp
        modulus = diag_r * diag_r + diag_i * diag_i
        gains_r.append((RELAXATION * diag_r / modulus)[0:1, 0:1])
        gains_i.append((RELAXATION * diag_i / modulus)[0:1, 0:1])
        damps.append(damp_t[t])

    def step(cells, f, drive_f, g_r, g_i):
        sums = []
        for c in range(2):
            mid = cells[c, f]
            total = cells[c, f - 1] + cells[c, f + 1] + drive[c, drive_f]
            total = total + pltpu.roll(mid, 1, 0) + pltpu.roll(mid, 47, 0)
            sums.append((mid, total + pltpu.roll(mid, 1, 1) + pltpu.roll(mid, width - 1, 1)))
        (mid_r, sum_r), (mid_i, sum_i) = sums
        keep = 1.0 - RELAXATION
        return keep * mid_r + (g_r * sum_r + g_i * sum_i), keep * mid_i + (g_r * sum_i - g_i * sum_r)

    for f in range(CX):
        codes = classes(N_CODE + f * 48)
        x_ok = x_before if f < 1 else x_after if f >= 9 else None
        ok = inside if x_ok is None else inside * x_ok
        g_r = pick(codes, gains_r) * ok
        g_i = pick(codes, gains_i) * ok
        gain_r[f], gain_i[f] = g_r, g_i
        second[0, f], second[1, f] = step(first, f + 1, f, g_r, g_i)

    for i in range(4):
        heat = None
        for f in (2 * i, 2 * i + 1):
            new_r, new_i = step(second, f + 1, f + 1, gain_r[f + 1], gain_i[f + 1])
            emit(f, new_r, new_i)
            layer = pick(classes(N_CODE + (f + 1) * 48), damps) * (new_r * new_r + new_i * new_i)
            heat = layer if heat is None else heat + layer
        for tile in range(width // 128):
            pool[tile, pl.ds(i * 48, 48), :] = heat[:, tile * 128 : tile * 128 + 128]
    tiles = [pool[t, pl.ds(0, 96, 2), :] + pool[t, pl.ds(1, 96, 2), :] for t in range(width // 128)]
    return tiles[0] if len(tiles) == 1 else jnp.concatenate(tiles, axis=1)


def smooth_inner(wave_t, damp_t, wide, narrow, source, spread, gather, spread_strip, out, power, ends, fine_ends,
                 grown, fine, first, second, gain_r, gain_i, pool):
    coarse_rows(lambda at: narrow[pl.ds(N_COARSE + at, 32), :], None, grown)
    fine[...] = exact_dot(grown[...], spread[...])
    fine_ends[...] = exact_dot(grown[...], spread_strip[pl.ds(0, 128), :])
    lane = iota((48, 128), 1)
    for at in range(0, WIDE, 48):
        turned = pltpu.roll(wide[pl.ds(at, 48), pl.ds(128, 128)], 64, 1)
        ends[pl.ds(at, 48), :] = jnp.where(lane < 32, wide[pl.ds(at, 48), pl.ds(0, 128)], turned)

    def own(at):
        return wide[pl.ds(at, 48), :]

    def emit(f, new_r, new_i):
        out[0, f] = new_r[0:32]
        out[1, f] = new_i[0:32]

    sums = relax(256, own, own, None, fine, source, wave_t, damp_t, first, second, gain_r, gain_i, pool, emit)
    power[...] = exact_dot(sums, gather[...]) * 0.125


def smooth_ends(wave_t, damp_t, ends, z_one, z_two, source, spread, gather, inner, power_inner, fine_ends,
                out, power, power_halo, one, two, tiles,
                halo, grown_halo, fine, first, second, gain_r, gain_i, pool):
    lane = iota((ZB, 128), 1)
    came, every = Receiver(z_one, z_two, 2), (pl.ds(0, ZB), pl.ds(0, 128))
    right, left = came.after(*every), came.before(*every)
    for g in range(GROUPS):
        turn = (192 - 8 * g) % 128
        after = pltpu.roll(right, turn, 1) if turn else right
        turn = (120 - 8 * g) % 128
        before = pltpu.roll(left, turn, 1) if turn else left
        halo[pl.ds(g * ZB, ZB), :] = jnp.where(lane < 96, after, before)
    beyond = halo[pl.ds(WIDE + N_THETA, NARROW - N_THETA), :]
    tiles[...] = jnp.where(iota(beyond.shape, 1) < 64, pltpu.roll(beyond, 64, 1), beyond)

    at_z = lax.axis_index("gz")
    after_ok, before_ok = flag(at_z < 3), flag(at_z > 0)
    z_ok = jnp.where(iota((32, 128), 1) < 96, after_ok, before_ok)
    coarse_rows(lambda at: halo[pl.ds(WIDE + N_COARSE + at, 32), :], z_ok, grown_halo)
    fine[...] = fine_ends[...] + exact_dot(grown_halo[...], spread[pl.ds(128, 128), :])

    lane = iota((48, 128), 1)

    def strip(at):
        return jnp.where(lane < 64, ends[pl.ds(at, 48), :], halo[pl.ds(at, 48), :])

    low, high = iota((32, 128), 1) < 8, iota((32, 128), 1) >= 120

    def emit(f, new_r, new_i):
        for c, new in enumerate((new_r[0:32], new_i[0:32])):
            out[c, f, :, pl.ds(0, 128)] = jnp.where(low, new, inner[c, f, :, pl.ds(0, 128)])
            out[c, f, :, pl.ds(128, 128)] = jnp.where(high, pltpu.roll(new, 64, 1), inner[c, f, :, pl.ds(128, 128)])

    z_ok = jnp.where(lane < 64, 1.0, jnp.where(lane < 96, after_ok, before_ok))
    live = jnp.where((lane < 72) | (lane >= 120), z_ok, 0.0)
    sums = relax(128, strip, strip, live, fine, source, wave_t, damp_t, first, second, gain_r, gain_i, pool, emit)
    sums = exact_dot(sums, gather[...]) * 0.125
    lane = iota((96, 128), 1)
    own = jnp.where((lane < 4) | (lane >= 124), sums[:, 0:128], power_inner[...])
    over = sums[:, 128:256]
    power[...], power_halo[...] = own, over

    def packed(first_layer):
        group, total = iota((24, 128), 1) // 16, None
        for k in range(3):
            at = (first_layer + k) * 24
            turned = pltpu.roll(over[at : at + 24], 16 * k + 8, 1)
            total = turned if total is None else jnp.where(group == k, turned, total)
        return total

    to, every = Sender(one, two, 0), pl.ds(0, 128)
    to.put(pl.ds(0, 72), every, own[24:96], own[0:72])
    to.put(pl.ds(72, 24), every, packed(1), packed(0))


class Bioheat:
    def __init__(self):
        x_before, x_after = x_flags()
        at_y, at_z = lax.axis_index("gy"), lax.axis_index("gz")
        row, col = iota((24, 256), 0), iota((24, 256), 1)
        y_ok = jnp.where(row < 16, 1.0, jnp.where(row < 20, flag(at_y < 15), flag(at_y > 0)))
        z_ok = jnp.where(col < 128, 1.0, jnp.where(col < 192, flag(at_z < 3), flag(at_z > 0)))
        inside = y_ok * z_ok
        self.edge = [inside * (x_before if f < 4 else x_after) if not 4 <= f < 8 else inside for f in range(TX)]

    def step(self, state, wash, f):
        mid = state[f]
        beside = state[f - 1] + state[f + 1]
        beside = beside + pltpu.roll(mid, 1, 0) + pltpu.roll(mid, 23, 0)
        beside = beside + pltpu.roll(mid, 1, 1) + pltpu.roll(mid, 255, 1)
        return mid + DIFFUSION * (beside - 6.0 * mid) - wash[f - 1] * mid

    def finish(self, cooled, heat, f):
        return (cooled + HEATING * heat) * self.edge[f]


def injury_of(warm):
    own = warm[0:16, 0:128]
    return jnp.exp(LN_PREFACTOR - ENERGY_BARRIER / (CORE_WARMTH + own))


def own_heat(power, power_halo, f):
    return jnp.concatenate([ref[pl.ds(24 * (f - 4), 24), :] for ref in (power, power_halo)], axis=1)


def bioheat_inner(narrow, tiles, power, power_halo, injury, wave, begun, later, wash, dose, wave_out, now, sem):
    store = pltpu.make_async_copy(wave, wave_out, sem)
    store.start()
    heat = Bioheat()

    def extended(base, f):
        at = base + f * 24
        return jnp.concatenate([narrow[pl.ds(at, 24), :], tiles[pl.ds(at - N_THETA, 24), :]], axis=1)

    for f in range(TX):
        now[f] = extended(N_THETA, f) * heat.edge[f]
    for f in range(QX):
        wash[f] = extended(N_PERF, f)
    for f in range(1, TX - 1):
        new = heat.step(now, wash, f)
        if 4 <= f < 8:
            new = heat.finish(new, own_heat(power, power_halo, f), f)
            dose[f - 4] = injury[f - 4] + injury_of(new)
        begun[f] = new
    for f in (5, 6):
        new = heat.finish(heat.step(begun, wash, f), own_heat(power, power_halo, f), f)
        later[f - 5] = new
        dose[f - 4] = dose[f - 4] + injury_of(new)
    store.wait()


def bioheat(begun, later, wash, dose_in, power, power_halo, x_one, x_two, warm_out, dose_out, one, two):
    heat = Bioheat()
    came = Receiver(x_one, x_two, 0)

    def sent(side, k):
        beyond = side(pl.ds(72, 24), pl.ds(0, 128))
        beyond = jnp.where(iota((24, 128), 1) // 16 == k, beyond, 0.0)
        return jnp.concatenate([side(pl.ds(24 * k, 24), pl.ds(0, 128)), pltpu.roll(beyond, 120 - 16 * k, 1)], axis=1)

    own = [own_heat(power, power_halo, f) for f in range(4, 8)]
    heats = [None] + [sent(came.before, k) for k in range(3)] + own + [sent(came.after, k) for k in range(3)]
    for f in range(1, TX - 1):
        one[f] = begun[f] if 4 <= f < 8 else heat.finish(begun[f], heats[f], f)
    dose = [dose_in[i] for i in range(4)]
    state, other = one, two
    for turn in range(1, 4):
        for f in range(1 + turn, TX - 1 - turn):
            if turn == 1 and f in (5, 6):
                other[f] = later[f - 5]
                continue
            new = heat.finish(heat.step(state, wash, f), heats[f], f)
            other[f] = new
            if 4 <= f < 8:
                dose[f - 4] = dose[f - 4] + injury_of(new)
                if turn == 3:
                    warm_out[f - 4] = new[0:16, 0:128]
        state, other = other, state
    for i in range(4):
        dose_out[i] = jnp.log(dose[i])


def shaped(*shape, dtype=F32):
    return jax.ShapeDtypeStruct(shape, dtype)


def call(kernel, name, in_specs, outs, scratch=(), out_specs=None, cost=2000):
    return pl.pallas_call(
        kernel,
        name=name,
        out_shape=tuple(outs),
        in_specs=in_specs,
        out_specs=tuple(out_specs or [vmem() for _ in outs]),
        scratch_shapes=list(scratch),
        cost_estimate=pl.CostEstimate(flops=cost * 1000, bytes_accessed=cost * 1000, transcendentals=0),
        compiler_params=pltpu.CompilerParams(vmem_limit_bytes=24 * 1024 * 1024),
    )


def on_device(
    acoustic_iterate,
    coarse_update,
    class_codes_volume,
    element_location,
    element_excitation,
    class_wavespeed,
    class_damping,
    washout_fraction,
    thermal_excess,
    injury_integral,
):
    def in_hbm(*arrays):
        return [pltpu.with_memory_space_constraint(array, pltpu.HBM) for array in arrays]

    *sent, perf, it, co, codes, theta = call(
        pack_x, "pack_x", [hbm()] * 5,
        [
            shaped(XB, 256),
            shaped(XB, 256),
            shaped(YB, 256),
            shaped(YB, 256),
            shaped(4, 16, 128),
            shaped(2, 8, 32, 256),
            shaped(2, 4, 16, 128),
            shaped(8, 32, 256, dtype=jnp.int32),
            shaped(4, 16, 128),
        ],
        [pltpu.VMEM((2, 128, 128), F32), pltpu.SMEM((4,), F32), pltpu.SemaphoreType.DMA((5,))],
    )(*in_hbm(washout_fraction, acoustic_iterate, coarse_update, class_codes_volume, thermal_excess))
    own = (it, co, codes, theta, perf)
    y_came = exchange(sent[2:], 1)
    x_came = exchange(sent[:2], 0)

    field, strip, *weights = call(
        sources, "sources", [hbm(), hbm(), vmem()],
        [
            shaped(2, CX, 48, 256),
            shaped(2, CX, 48, 128),
            shaped(128, 256, dtype=BF16),
            shaped(256, 128, dtype=BF16),
            shaped(256, 128, dtype=BF16),
            shaped(128, 256, dtype=BF16),
        ],
        [
            pltpu.SMEM((3, 1024), jnp.int32),
            pltpu.SMEM((2, 1024), F32),
            pltpu.VMEM((3, 1024), jnp.int32),
            pltpu.SemaphoreType.DMA((3,)),
        ],
        cost=8000,
    )(*in_hbm(element_location.T, element_excitation), perf)
    sent = call(pack_corner, "pack_corner", [vmem()] * 3, [shaped(KB, 256)] * 2)(*y_came, weights[0])
    corners = exchange(sent, 0)

    wide, narrow, *sent = call(
        pack_z, "pack_z", [vmem()] * 11,
        [shaped(WIDE, 256), shaped(NARROW, 128), shaped(ZB, 128), shaped(ZB, 128)],
    )(*own, *x_came, *y_came, *corners)
    z_came = exchange(sent, 2)

    def scratch(width):
        return [
            pltpu.VMEM((2 * LX * 48, width), F32),
            pltpu.VMEM((2, FX, 48, width), F32),
            pltpu.VMEM((2, CX, 48, width), F32),
            pltpu.VMEM((CX, 48, width), F32),
            pltpu.VMEM((CX, 48, width), F32),
            pltpu.VMEM((width // 128, 192, 128), F32),
        ]

    inner, power_inner, ends, fine_ends = call(
        smooth_inner, "smooth_inner", [smem()] * 2 + [vmem()] * 6,
        [shaped(2, 8, 32, 256), shaped(96, 128), shaped(WIDE, 128), shaped(2 * LX * 48, 128)],
        [pltpu.VMEM((2 * LX * 48, 128), F32)] + scratch(256),
    )(class_wavespeed, class_damping, wide, narrow, field, weights[0], weights[1], weights[2])
    pressure, power, power_halo, *sent, tiles = call(
        smooth_ends, "smooth_ends", [smem()] * 2 + [vmem()] * 9,
        [
            shaped(2, 8, 32, 256),
            shaped(96, 128),
            shaped(96, 128),
            shaped(96, 128),
            shaped(96, 128),
            shaped(NARROW - N_THETA, 128),
        ],
        [pltpu.VMEM((WIDE + NARROW, 128), F32), pltpu.VMEM((2 * LX * 48, 128), F32)] + scratch(128),
    )(class_wavespeed, class_damping, ends, *z_came, strip, weights[2], weights[3], inner, power_inner, fine_ends)
    x_came = exchange(sent, 0)

    block = shaped(TX, 24, 256)
    begun, later, wash, dose, pressure = call(
        bioheat_inner, "bioheat_inner", [vmem()] * 6,
        [block, shaped(2, 24, 256), shaped(QX, 24, 256), shaped(4, 16, 128), shaped(2, 8, 32, 256)],
        [pltpu.VMEM((TX, 24, 256), F32), pltpu.SemaphoreType.DMA],
        [vmem()] * 4 + [hbm()],
    )(narrow, tiles, power, power_halo, injury_integral, pressure)
    warmth, dose = call(
        bioheat, "bioheat", [vmem()] * 8,
        [shaped(4, 16, 128), shaped(4, 16, 128)],
        [pltpu.VMEM((TX, 24, 256), F32), pltpu.VMEM((TX, 24, 256), F32)],
    )(begun, later, wash, dose, power, power_halo, *x_came)
    return pressure, warmth, dose


def solution(mesh):
    placed = (
        P(None, "gx", "gy", "gz"),
        P(None, "gx", "gy", "gz"),
        P("gx", "gy", "gz"),
        P(),
        P(),
        P(),
        P(),
        P(),
        P("gx", "gy", "gz"),
        P("gx", "gy", "gz"),
    )
    return jax.shard_map(
        on_device,
        mesh=mesh,
        in_specs=placed,
        out_specs=(P(None, "gx", "gy", "gz"), P("gx", "gy", "gz"), P("gx", "gy", "gz")),
        check_vma=False,
    )
```

```python
import jax
import jax.numpy as jnp
from jax import lax
from jax.experimental import pallas as pl
from jax.experimental.pallas import tpu as pltpu
from jax.sharding import PartitionSpec as P

F32 = jnp.float32
BF16 = jnp.bfloat16

RELAXATION = 0.8
DAMPING_SHIFT = 0.5
DIFFUSION = 0.15
HEATING = 0.25
LN_PREFACTOR = 226.78
ENERGY_BARRIER = 75535.0
CORE_WARMTH = 310.15

FX, CX, LX, TX, QX = 12, 10, 8, 12, 10
XB_CODE, XB_COARSE, XB_THERM, XB = 128, 160, 192, 256
YB_CODE, YB_COARSE, YB_THERM, YB = 128, 184, 204, 224
KB_CODE, KB_COARSE, KB_THERM, KB = 64, 78, 98, 128
WIDE = 2 * FX * 48 + CX * 48
N_CODE = 2 * FX * 48
N_COARSE, N_THETA, N_PERF, NARROW = 0, 512, 800, 1056
GROUPS = 16
ZB = (WIDE + NARROW) // GROUPS
WARM = (WIDE + N_THETA) // ZB
AXES = ("gx", "gy", "gz")


def vmem():
    return pl.BlockSpec(memory_space=pltpu.VMEM)


def hbm():
    return pl.BlockSpec(memory_space=pltpu.HBM)


def smem():
    return pl.BlockSpec(memory_space=pltpu.SMEM)


def swaps(sizes, axis, odd):
    count, targets = 1, []
    for n in sizes:
        count *= n
    for i in range(count):
        place, rest = [], i
        for n in reversed(sizes):
            place.insert(0, rest % n)
            rest //= n
        partner = list(place)
        partner[axis] = ((place[axis] + 1) ^ 1) - 1 if odd else place[axis] ^ 1
        if not 0 <= partner[axis] < sizes[axis]:
            other = 2 if axis != 2 else 0
            partner = list(place)
            partner[other] = place[other] ^ 1
        j = 0
        for n, at in zip(sizes, partner):
            j = j * n + at
        targets.append((i, j))
    return targets


def exchange(pair, axis):
    sizes = [lax.axis_size(name) for name in AXES]
    return [lax.ppermute(buffer, AXES, swaps(sizes, axis, bool(k))) for k, buffer in enumerate(pair)]


def is_even(axis):
    return lax.axis_index(AXES[axis]) % 2 == 0


class Sender:
    def __init__(self, first, second, axis):
        self.first, self.second, self.even = first, second, is_even(axis)

    def put(self, rows, lanes, up, down):
        self.first[rows, lanes] = jnp.where(self.even, up, down)
        self.second[rows, lanes] = jnp.where(self.even, down, up)


class Receiver:
    def __init__(self, first, second, axis):
        self.first, self.second, self.even = first, second, is_even(axis)

    def before(self, *at):
        return jnp.where(self.even, self.second[at], self.first[at])

    def after(self, *at):
        return jnp.where(self.even, self.first[at], self.second[at])


def exact_dot(values, weights):
    high = values.astype(BF16)
    rest = values - high.astype(F32)
    mid = rest.astype(BF16)
    low = (rest - mid.astype(F32)).astype(BF16)
    total = jnp.dot(high, weights, preferred_element_type=F32)
    total = total + jnp.dot(mid, weights, preferred_element_type=F32)
    return total + jnp.dot(low, weights, preferred_element_type=F32)


def iota(shape, dim):
    return lax.broadcasted_iota(jnp.int32, shape, dim)


def pick(codes, entries):
    value = jnp.where(codes == 0.0, entries[0], entries[1])
    value = jnp.where(codes == 2.0, entries[2], value)
    return jnp.where(codes == 3.0, entries[3], value)


def pack_x(wash_h, it_h, co_h, codes_h, theta_h, x_one, x_two, y_one, y_two, perf, it, co, codes, theta, pool, wash, sems):
    loads = [
        pltpu.make_async_copy(src, dst, sems.at[k])
        for k, (src, dst) in enumerate(
            ((codes_h, codes), (it_h, it), (wash_h, wash), (co_h, co), (theta_h, theta))
        )
    ]
    for load in loads:
        load.start()
    lane, col = iota((256, 128), 0), iota((256, 128), 1)
    pairs = jnp.where(lane // 2 == col, 1.0, 0.0).astype(BF16)
    loads[0].wait()
    loads[2].wait()
    entries = [wash[k] for k in range(4)]
    for i in range(4):
        both = pick(codes[2 * i].astype(F32), entries) + pick(codes[2 * i + 1].astype(F32), entries)
        for half in range(2):
            pool[half, i * 32 : i * 32 + 32, :] = both[:, half * 128 : half * 128 + 128]
    rows = jnp.concatenate([pool[h, pl.ds(0, 64, 2), :] + pool[h, pl.ds(1, 64, 2), :] for h in range(2)], axis=1)
    washed = exact_dot(rows, pairs) * 0.125
    for k in (1, 3, 4):
        loads[k].wait()
    for i in range(4):
        perf[i] = washed[i * 16 : i * 16 + 16]
    to, every = Sender(x_one, x_two, 0), pl.ds(0, 256)
    for c in range(2):
        for k in range(2):
            to.put(pl.ds((c * 2 + k) * 32, 32), every, it[c, 6 + k], it[c, k])
    to.put(pl.ds(XB_CODE, 32), every, codes[7].astype(F32), codes[0].astype(F32))
    for k in range(2):
        for c in range(2):
            to.put(pl.ds(XB_COARSE + 16 * k, 16), pl.ds(128 * c, 128), co[c, 2 + k], co[c, k])
    for i in range(4):
        for k, value in enumerate((theta[i], washed[i * 16 : i * 16 + 16])):
            to.put(pl.ds(XB_THERM + 16 * i, 16), pl.ds(128 * k, 128), value, value)
    to = Sender(y_one, y_two, 1)
    for c in range(2):
        for k in range(8):
            to.put(pl.ds((c * 8 + k) * 8, 8), every, it[c, k, 24:32, :], it[c, k, 0:8, :])
    for k in range(8):
        to.put(pl.ds(YB_CODE + k * 7, 7), every, codes[k, 25:32, :].astype(F32), codes[k, 0:7, :].astype(F32))
    for k in range(4):
        for c in range(2):
            to.put(pl.ds(YB_COARSE + k * 5, 5), pl.ds(128 * c, 128), co[c, k, 11:16, :], co[c, k, 0:5, :])
        for c, field in enumerate((theta, perf)):
            to.put(pl.ds(YB_THERM + k * 4, 4), pl.ds(128 * c, 128), field[k, 12:16, :], field[k, 0:4, :])


class Columns:
    def __init__(self, it, co, codes, theta, perf, beside):
        self.it, self.co, self.codes, self.theta, self.perf, self.beside = it, co, codes, theta, perf, beside

    def iterate(self, c, f, at, n):
        if 2 <= f < 10:
            return self.it[c, f - 2, pl.ds(at, n), :]
        side, k = (self.beside.before, f) if f < 2 else (self.beside.after, f - 10)
        return side(pl.ds((c * 2 + k) * 32 + at, n), pl.ds(0, 256))

    def code(self, f, at, n):
        if 1 <= f < 9:
            return self.codes[f - 1, pl.ds(at, n), :].astype(F32)
        side = self.beside.before if f < 1 else self.beside.after
        return side(pl.ds(XB_CODE + at, n), pl.ds(0, 256))

    def coarse(self, c, f, at, n):
        if 2 <= f < 6:
            return self.co[c, f - 2, pl.ds(at, n), :]
        side, k = (self.beside.before, f) if f < 2 else (self.beside.after, f - 6)
        return side(pl.ds(XB_COARSE + 16 * k + at, n), pl.ds(128 * c, 128))

    def warm(self, f, at, n):
        if 4 <= f < 8:
            return self.theta[f - 4, pl.ds(at, n), :]
        side, k = (self.beside.before, f) if f < 4 else (self.beside.after, f - 8)
        return side(pl.ds(XB_THERM + 16 * k + at, n), pl.ds(0, 128))

    def wash(self, f, at, n):
        if 3 <= f < 7:
            return self.perf[f - 3, pl.ds(at, n), :]
        side, k = (self.beside.before, f + 1) if f < 3 else (self.beside.after, f - 7)
        return side(pl.ds(XB_THERM + 16 * k + at, n), pl.ds(128, 128))


def pack_corner(y_one, y_two, after_this, one, two):
    came, to = Receiver(y_one, y_two, 1), Sender(one, two, 0)

    def put(at, n, lanes, up, down):
        for k, side in enumerate((came.after, came.before)):
            to.put(pl.ds(at + k * n, n), lanes, side(pl.ds(up, n), lanes), side(pl.ds(down, n), lanes))

    every = pl.ds(0, 256)
    for c in range(2):
        for k in range(2):
            put((c * 2 + k) * 16, 8, every, (c * 8 + 6 + k) * 8, (c * 8 + k) * 8)
    put(KB_CODE, 7, every, YB_CODE + 49, YB_CODE)
    for k in range(2):
        put(KB_COARSE + k * 10, 5, every, YB_COARSE + (2 + k) * 5, YB_COARSE + k * 5)
    for k in range(3):
        put(KB_THERM + k * 8, 4, every, YB_THERM + (1 + k) * 4, YB_THERM + k * 4)


def rows_of(wide, narrow, start, count, half):
    parts = []
    if start < WIDE:
        n = min(count, WIDE - start)
        parts.append(wide[pl.ds(start, n), pl.ds(128 * half, 128)])
        start, count = start + n, count - n
    if count:
        parts.append(narrow[pl.ds(start - WIDE, count), :])
    return parts[0] if len(parts) == 1 else jnp.concatenate(parts, axis=0)


def pack_z(it, co, codes, theta, perf, x_one, x_two, y_one, y_two, k_one, k_two, wide, narrow, one, two):
    block = Columns(it, co, codes, theta, perf, Receiver(x_one, x_two, 0))
    rows, corners = Receiver(y_one, y_two, 1), Receiver(k_one, k_two, 0)

    def beside(f, first, count, height, own, corner, lanes, skip=0):
        k = f - first
        if 0 <= k < count:
            at = pl.ds(own + k * height, height)
            return rows.after(at, lanes), rows.before(at, lanes)
        side, k = (corners.before, f - skip) if k < 0 else (corners.after, k - count)
        return [side(pl.ds(corner + (2 * k + j) * height, height), lanes) for j in range(2)]

    every = pl.ds(0, 256)
    for c in range(2):
        for f in range(FX):
            at = (c * FX + f) * 48
            wide[pl.ds(at, 32), :] = block.iterate(c, f, 0, 32)
            wide[pl.ds(at + 32, 8), :], wide[pl.ds(at + 40, 8), :] = beside(f, 2, 8, 8, c * 64, c * 32, every)
    for f in range(CX):
        at = N_CODE + f * 48
        wide[pl.ds(at, 32), :] = block.code(f, 0, 32)
        wide[pl.ds(at + 32, 16), :] = jnp.zeros((16, 256), F32)
        wide[pl.ds(at + 32, 7), :], wide[pl.ds(at + 41, 7), :] = beside(f, 1, 8, 7, YB_CODE, KB_CODE, every)
    for c in range(2):
        for f in range(LX):
            at = N_COARSE + (c * LX + f) * 32
            over, under = beside(f, 2, 4, 5, YB_COARSE, KB_COARSE, pl.ds(128 * c, 128))
            narrow[pl.ds(at, 16), :] = block.coarse(c, f, 0, 16)
            narrow[pl.ds(at + 24, 8), :] = jnp.zeros((8, 128), F32)
            narrow[pl.ds(at + 16, 4), :] = over[0:4]
            narrow[pl.ds(at + 20, 4), :] = under[1:5]
            narrow[pl.ds(at + 24, 1), :] = under[0:1]
            narrow[pl.ds(at + 25, 1), :] = over[4:5]
    for f in range(TX):
        at = N_THETA + f * 24
        narrow[pl.ds(at, 16), :] = block.warm(f, 0, 16)
        if 0 < f < 11:
            over, under = beside(f, 4, 4, 4, YB_THERM, KB_THERM, pl.ds(0, 128), 1)
        else:
            over = under = jnp.zeros((4, 128), F32)
        narrow[pl.ds(at + 16, 4), :], narrow[pl.ds(at + 20, 4), :] = over, under
    for f in range(QX):
        at = N_PERF + f * 24
        narrow[pl.ds(at, 16), :] = block.wash(f, 0, 16)
        over, under = beside(f + 1, 4, 4, 4, YB_THERM, KB_THERM, pl.ds(128, 128), 1)
        narrow[pl.ds(at + 16, 4), :], narrow[pl.ds(at + 20, 4), :] = over, under
    narrow[pl.ds(N_PERF + QX * 24, NARROW - N_PERF - QX * 24), :] = jnp.zeros((NARROW - N_PERF - QX * 24, 128), F32)
    lane, ends = iota((ZB, 128), 1) // 8, []
    for half, shift in ((1, 8), (0, 0)):
        packed = None
        for g in range(GROUPS):
            part = rows_of(wide, narrow, g * ZB, ZB, half)
            turn = (8 * g + shift) % 128
            part = pltpu.roll(part, turn, 1) if turn else part
            packed = part if packed is None else jnp.where(lane == g, part, packed)
        ends.append(packed)
    Sender(one, two, 2).put(pl.ds(0, ZB), pl.ds(0, 128), *ends)


def unpack_z(one, two, groups, lane_after, halo):
    lane = iota((ZB, 128), 1)
    came, every = Receiver(one, two, 2), (pl.ds(0, ZB), pl.ds(0, 128))
    right, left = came.after(*every), came.before(*every)
    for k, g in enumerate(groups):
        turn = (128 + lane_after - 8 * g) % 128
        after = pltpu.roll(right, turn, 1) if turn else right
        turn = (120 - 8 * g) % 128
        before = pltpu.roll(left, turn, 1) if turn else left
        halo[pl.ds(k * ZB, ZB), :] = jnp.where(lane < 96, after, before)


def strip_cell(lane):
    return jnp.where(lane < 32, lane, jnp.where(lane < 96, lane + 192, lane - 128))


def sources(loc_h, exc_h, after_this, field, strip, spread, gather, spread_strip, gather_strip, loc_s, exc_s, loc, sems):
    loads = [
        pltpu.make_async_copy(src, dst, sems.at[k])
        for k, (src, dst) in enumerate(((loc_h, loc), (loc_h, loc_s), (exc_h, exc_s)))
    ]
    for load in loads:
        load.start()
    field[...] = jnp.zeros(field.shape, F32)
    strip[...] = jnp.zeros(strip.shape, F32)
    coord = [lax.axis_index(name) for name in AXES]
    for load in loads:
        load.wait()
    first = loc[0:1, :] - coord[0] * 8
    second = loc[1:2, :] - coord[1] * 32
    third = loc[2:3, :] - coord[2] * 256
    near = (first >= -1) & (first < 9) & (second >= -7) & (second < 39) & (third >= -7) & (third < 263)
    order = iota((1, 1024), 1)
    lane, cell = iota((1, 256), 1), strip_cell(iota((1, 128), 1))

    def place(state):
        e, keys = state
        x = loc_s[0, e] - coord[0] * 8 + 1
        y = loc_s[1, e] - coord[1] * 32
        z = loc_s[2, e] - coord[2] * 256
        y = jnp.where(y < 0, y + 48, y)
        for c in range(2):
            field[c, x, pl.ds(y, 1), :] += jnp.where(lane == z, exc_s[c, e], 0.0)
            strip[c, x, pl.ds(y, 1), :] += jnp.where(cell == z, exc_s[c, e], 0.0)
        keys = jnp.where(order == e, 1024, keys)
        return jnp.min(keys), keys

    keys = jnp.where(near, order, 1024)
    lax.while_loop(lambda state: state[0] < 1024, place, (jnp.min(keys), keys))

    def weights(cell, column, at):
        centre = cell >> 1
        beside = centre + jnp.where((cell & 1) == 1, 1, -1)
        weight = jnp.where(column == at(centre), 0.75, jnp.where(column == at(beside), 0.25, 0.0))
        return weight.astype(BF16)

    spread[...] = weights(iota((128, 256), 1), iota((128, 256), 0), lambda c: c)
    spread_strip[...] = weights(
        strip_cell(iota((256, 128), 1)),
        iota((256, 128), 0),
        lambda c: jnp.where(c < 0, c + 256, jnp.where(c < 128, c, c + 64)),
    )
    gather[...] = jnp.where(iota((256, 128), 1) == iota((256, 128), 0) >> 1, 1.0, 0.0).astype(BF16)
    centre = strip_cell(iota((128, 256), 0)) >> 1
    centre = jnp.where(centre < 0, centre + 256, centre)
    gather_strip[...] = jnp.where(iota((128, 256), 1) == centre, 1.0, 0.0).astype(BF16)


def flag(test):
    return jnp.where(test, 1.0, 0.0)


def x_flags():
    at = lax.axis_index("gx")
    return flag(at > 0), flag(at < 3)


def along_y(cells, row):
    lanes = cells.shape[1]
    centre = cells[0:24]
    lower = jnp.where(row == 20, jnp.broadcast_to(cells[24:25], (24, lanes)), pltpu.roll(centre, 1, 0))
    upper = jnp.where(row == 19, jnp.broadcast_to(cells[25:26], (24, lanes)), pltpu.roll(centre, 23, 0))
    return 0.75 * centre + 0.25 * lower, 0.75 * centre + 0.25 * upper


def coarse_rows(read, z_ok, grown):
    x_before, x_after = x_flags()
    at_y = lax.axis_index("gy")
    row = iota((32, 128), 0)
    y_ok = jnp.where(row < 16, 1.0, jnp.where((row < 20) | (row == 25), flag(at_y < 15), flag(at_y > 0)))
    inside = y_ok if z_ok is None else y_ok * z_ok
    row = iota((24, 128), 0)
    for c in range(2):
        for f in range(LX):
            x_ok = x_before if f < 2 else x_after if f >= 6 else None
            even, odd = along_y(read((c * LX + f) * 32) * (inside if x_ok is None else inside * x_ok), row)
            to = (c * LX + f) * 48
            grown[pl.ds(to, 24, 2), :] = even
            grown[pl.ds(to + 1, 24, 2), :] = odd


def relax(width, start, classes, z_ok, fine, drive, wave_t, damp_t, first, second, gain_r, gain_i, pool, emit):
    x_before, x_after = x_flags()
    at_y = lax.axis_index("gy")
    row = iota((48, width), 0)
    inside = jnp.where(row < 32, 1.0, jnp.where(row < 40, flag(at_y < 15), flag(at_y > 0)))
    if z_ok is not None:
        inside = inside * z_ok
    for c in range(2):
        for f in range(FX):
            near = c * LX + f // 2 + 1
            far = near + (1 if f % 2 else -1)
            grow = 0.75 * fine[pl.ds(near * 48, 48), :] + 0.25 * fine[pl.ds(far * 48, 48), :]
            x_ok = x_before if f < 2 else x_after if f >= 10 else None
            first[c, f] = (start((c * FX + f) * 48) + grow) * (inside if x_ok is None else inside * x_ok)

    gains_r, gains_i, damps = [], [], []
    for t in range(4):
        speed = jnp.full((8, 128), wave_t[t], F32)
        damp = jnp.full((8, 128), damp_t[t], F32)
        wave = 1.0 / (speed * speed)
        diag_r = 6.0 - wave
        diag_i = DAMPING_SHIFT * wave + damp
        modulus = diag_r * diag_r + diag_i * diag_i
        gains_r.append((RELAXATION * diag_r / modulus)[0:1, 0:1])
        gains_i.append((RELAXATION * diag_i / modulus)[0:1, 0:1])
        damps.append(damp_t[t])

    def step(cells, f, drive_f, g_r, g_i):
        sums = []
        for c in range(2):
            mid = cells[c, f]
            total = cells[c, f - 1] + cells[c, f + 1] + drive[c, drive_f]
            total = total + pltpu.roll(mid, 1, 0) + pltpu.roll(mid, 47, 0)
            sums.append((mid, total + pltpu.roll(mid, 1, 1) + pltpu.roll(mid, width - 1, 1)))
        (mid_r, sum_r), (mid_i, sum_i) = sums
        keep = 1.0 - RELAXATION
        return keep * mid_r + (g_r * sum_r + g_i * sum_i), keep * mid_i + (g_r * sum_i - g_i * sum_r)

    for f in range(CX):
        codes = classes(N_CODE + f * 48)
        x_ok = x_before if f < 1 else x_after if f >= 9 else None
        ok = inside if x_ok is None else inside * x_ok
        g_r = pick(codes, gains_r) * ok
        g_i = pick(codes, gains_i) * ok
        gain_r[f], gain_i[f] = g_r, g_i
        second[0, f], second[1, f] = step(first, f + 1, f, g_r, g_i)

    for i in range(4):
        heat = None
        for f in (2 * i, 2 * i + 1):
            new_r, new_i = step(second, f + 1, f + 1, gain_r[f + 1], gain_i[f + 1])
            emit(f, new_r, new_i)
            layer = pick(classes(N_CODE + (f + 1) * 48), damps) * (new_r * new_r + new_i * new_i)
            heat = layer if heat is None else heat + layer
        for tile in range(width // 128):
            pool[tile, pl.ds(i * 48, 48), :] = heat[:, tile * 128 : tile * 128 + 128]
    tiles = [pool[t, pl.ds(0, 96, 2), :] + pool[t, pl.ds(1, 96, 2), :] for t in range(width // 128)]
    return tiles[0] if len(tiles) == 1 else jnp.concatenate(tiles, axis=1)


def smooth_inner(wave_t, damp_t, wide, narrow, source, spread, gather, spread_strip, out, power, ends, fine_ends,
                 grown, fine, first, second, gain_r, gain_i, pool):
    coarse_rows(lambda at: narrow[pl.ds(N_COARSE + at, 32), :], None, grown)
    fine[...] = exact_dot(grown[...], spread[...])
    fine_ends[...] = exact_dot(grown[...], spread_strip[pl.ds(0, 128), :])
    lane = iota((48, 128), 1)
    for at in range(0, WIDE, 48):
        turned = pltpu.roll(wide[pl.ds(at, 48), pl.ds(128, 128)], 64, 1)
        ends[pl.ds(at, 48), :] = jnp.where(lane < 32, wide[pl.ds(at, 48), pl.ds(0, 128)], turned)

    def own(at):
        return wide[pl.ds(at, 48), :]

    def emit(f, new_r, new_i):
        out[0, f] = new_r[0:32]
        out[1, f] = new_i[0:32]

    sums = relax(256, own, own, None, fine, source, wave_t, damp_t, first, second, gain_r, gain_i, pool, emit)
    power[...] = exact_dot(sums, gather[...]) * 0.125


def smooth_ends(wave_t, damp_t, ends, z_one, z_two, source, spread, gather, power_inner, fine_ends,
                out, power, power_halo, one, two,
                halo, grown_halo, fine, first, second, gain_r, gain_i, pool):
    unpack_z(z_one, z_two, range(WARM + 1), 64, halo)
    at_z = lax.axis_index("gz")
    after_ok, before_ok = flag(at_z < 3), flag(at_z > 0)
    z_ok = jnp.where(iota((32, 128), 1) < 96, after_ok, before_ok)
    coarse_rows(lambda at: halo[pl.ds(WIDE + N_COARSE + at, 32), :], z_ok, grown_halo)
    fine[...] = fine_ends[...] + exact_dot(grown_halo[...], spread[pl.ds(128, 128), :])

    lane = iota((48, 128), 1)

    def strip(at):
        return jnp.where(lane < 64, ends[pl.ds(at, 48), :], halo[pl.ds(at, 48), :])

    def emit(f, new_r, new_i):
        out[0, f] = new_r[0:32]
        out[1, f] = new_i[0:32]

    z_ok = jnp.where(lane < 64, 1.0, jnp.where(lane < 96, after_ok, before_ok))
    live = jnp.where((lane < 72) | (lane >= 120), z_ok, 0.0)
    sums = relax(128, strip, strip, live, fine, source, wave_t, damp_t, first, second, gain_r, gain_i, pool, emit)
    sums = exact_dot(sums, gather[...]) * 0.125
    lane = iota((96, 128), 1)
    own = jnp.where((lane < 4) | (lane >= 124), sums[:, 0:128], power_inner[...])
    over = sums[:, 128:256]
    power[...], power_halo[...] = own, over

    def packed(first_layer):
        group, total = iota((24, 128), 1) // 16, None
        for k in range(3):
            at = (first_layer + k) * 24
            turned = pltpu.roll(over[at : at + 24], 16 * k + 8, 1)
            total = turned if total is None else jnp.where(group == k, turned, total)
        return total

    to, every = Sender(one, two, 0), pl.ds(0, 128)
    to.put(pl.ds(0, 72), every, own[24:96], own[0:72])
    to.put(pl.ds(72, 24), every, packed(1), packed(0))


class Bioheat:
    def __init__(self):
        x_before, x_after = x_flags()
        at_y, at_z = lax.axis_index("gy"), lax.axis_index("gz")
        row, col = iota((24, 256), 0), iota((24, 256), 1)
        y_ok = jnp.where(row < 16, 1.0, jnp.where(row < 20, flag(at_y < 15), flag(at_y > 0)))
        z_ok = jnp.where(col < 128, 1.0, jnp.where(col < 192, flag(at_z < 3), flag(at_z > 0)))
        inside = y_ok * z_ok
        self.edge = [inside * (x_before if f < 4 else x_after) if not 4 <= f < 8 else inside for f in range(TX)]

    def step(self, state, wash, f):
        mid = state[f]
        beside = state[f - 1] + state[f + 1]
        beside = beside + pltpu.roll(mid, 1, 0) + pltpu.roll(mid, 23, 0)
        beside = beside + pltpu.roll(mid, 1, 1) + pltpu.roll(mid, 255, 1)
        return mid + DIFFUSION * (beside - 6.0 * mid) - wash[f - 1] * mid

    def finish(self, cooled, heat, f):
        return (cooled + HEATING * heat) * self.edge[f]


def injury_of(warm):
    own = warm[0:16, 0:128]
    return jnp.exp(LN_PREFACTOR - ENERGY_BARRIER / (CORE_WARMTH + own))


def own_heat(power, power_halo, f):
    return jnp.concatenate([ref[pl.ds(24 * (f - 4), 24), :] for ref in (power, power_halo)], axis=1)


def bioheat_inner(narrow, z_one, z_two, power, power_halo, injury, inner, ends, begun, later, wash, dose, wave_out,
                  now, tiles, wave, sem):
    low, high = iota((32, 128), 1) < 8, iota((32, 128), 1) >= 120
    for c in range(2):
        for f in range(8):
            new = ends[c, f]
            wave[c, f, :, pl.ds(0, 128)] = jnp.where(low, new, inner[c, f, :, pl.ds(0, 128)])
            turned = pltpu.roll(new, 64, 1)
            wave[c, f, :, pl.ds(128, 128)] = jnp.where(high, turned, inner[c, f, :, pl.ds(128, 128)])
    store = pltpu.make_async_copy(wave, wave_out, sem)
    store.start()
    unpack_z(z_one, z_two, range(WARM, GROUPS), 0, tiles)
    heat = Bioheat()

    def extended(base, f):
        at = base + f * 24
        return jnp.concatenate([narrow[pl.ds(at, 24), :], tiles[pl.ds(WIDE + at - WARM * ZB, 24), :]], axis=1)

    for f in range(TX):
        now[f] = extended(N_THETA, f) * heat.edge[f]
    for f in range(QX):
        wash[f] = extended(N_PERF, f)
    for f in range(1, TX - 1):
        new = heat.step(now, wash, f)
        if 4 <= f < 8:
            new = heat.finish(new, own_heat(power, power_halo, f), f)
            dose[f - 4] = injury[f - 4] + injury_of(new)
        begun[f] = new
    for f in (5, 6):
        new = heat.finish(heat.step(begun, wash, f), own_heat(power, power_halo, f), f)
        later[f - 5] = new
        dose[f - 4] = dose[f - 4] + injury_of(new)
    store.wait()


def bioheat(begun, later, wash, dose_in, power, power_halo, x_one, x_two, warm_out, dose_out, one, two):
    heat = Bioheat()
    came = Receiver(x_one, x_two, 0)

    def sent(side, k):
        beyond = side(pl.ds(72, 24), pl.ds(0, 128))
        beyond = jnp.where(iota((24, 128), 1) // 16 == k, beyond, 0.0)
        return jnp.concatenate([side(pl.ds(24 * k, 24), pl.ds(0, 128)), pltpu.roll(beyond, 120 - 16 * k, 1)], axis=1)

    own = [own_heat(power, power_halo, f) for f in range(4, 8)]
    heats = [None] + [sent(came.before, k) for k in range(3)] + own + [sent(came.after, k) for k in range(3)]
    for f in range(1, TX - 1):
        one[f] = begun[f] if 4 <= f < 8 else heat.finish(begun[f], heats[f], f)
    dose = [dose_in[i] for i in range(4)]
    state, other = one, two
    for turn in range(1, 4):
        for f in range(1 + turn, TX - 1 - turn):
            if turn == 1 and f in (5, 6):
                other[f] = later[f - 5]
                continue
            new = heat.finish(heat.step(state, wash, f), heats[f], f)
            if turn < 3:
                other[f] = new
            if 4 <= f < 8:
                dose[f - 4] = dose[f - 4] + injury_of(new)
                if turn == 3:
                    warm_out[f - 4] = new[0:16, 0:128]
        state, other = other, state
    for i in range(4):
        dose_out[i] = jnp.log(dose[i])


def shaped(*shape, dtype=F32):
    return jax.ShapeDtypeStruct(shape, dtype)


def call(kernel, name, in_specs, outs, scratch=(), out_specs=None, cost=2000):
    return pl.pallas_call(
        kernel,
        name=name,
        out_shape=tuple(outs),
        in_specs=in_specs,
        out_specs=tuple(out_specs or [vmem() for _ in outs]),
        scratch_shapes=list(scratch),
        cost_estimate=pl.CostEstimate(flops=cost * 1000, bytes_accessed=cost * 1000, transcendentals=0),
        compiler_params=pltpu.CompilerParams(vmem_limit_bytes=24 * 1024 * 1024),
    )


def on_device(
    acoustic_iterate,
    coarse_update,
    class_codes_volume,
    element_location,
    element_excitation,
    class_wavespeed,
    class_damping,
    washout_fraction,
    thermal_excess,
    injury_integral,
):
    def in_hbm(*arrays):
        return [pltpu.with_memory_space_constraint(array, pltpu.HBM) for array in arrays]

    *sent, perf, it, co, codes, theta = call(
        pack_x, "pack_x", [hbm()] * 5,
        [
            shaped(XB, 256),
            shaped(XB, 256),
            shaped(YB, 256),
            shaped(YB, 256),
            shaped(4, 16, 128),
            shaped(2, 8, 32, 256),
            shaped(2, 4, 16, 128),
            shaped(8, 32, 256, dtype=jnp.int32),
            shaped(4, 16, 128),
        ],
        [pltpu.VMEM((2, 128, 128), F32), pltpu.SMEM((4,), F32), pltpu.SemaphoreType.DMA((5,))],
    )(*in_hbm(washout_fraction, acoustic_iterate, coarse_update, class_codes_volume, thermal_excess))
    own = (it, co, codes, theta, perf)
    y_came = exchange(sent[2:], 1)
    x_came = exchange(sent[:2], 0)

    field, strip, *weights = call(
        sources, "sources", [hbm(), hbm(), vmem()],
        [
            shaped(2, CX, 48, 256),
            shaped(2, CX, 48, 128),
            shaped(128, 256, dtype=BF16),
            shaped(256, 128, dtype=BF16),
            shaped(256, 128, dtype=BF16),
            shaped(128, 256, dtype=BF16),
        ],
        [
            pltpu.SMEM((3, 1024), jnp.int32),
            pltpu.SMEM((2, 1024), F32),
            pltpu.VMEM((3, 1024), jnp.int32),
            pltpu.SemaphoreType.DMA((3,)),
        ],
        cost=8000,
    )(*in_hbm(element_location.T, element_excitation), perf)
    sent = call(pack_corner, "pack_corner", [vmem()] * 3, [shaped(KB, 256)] * 2)(*y_came, weights[0])
    corners = exchange(sent, 0)

    wide, narrow, *sent = call(
        pack_z, "pack_z", [vmem()] * 11,
        [shaped(WIDE, 256), shaped(NARROW, 128)] + [shaped(ZB, 128)] * 2,
    )(*own, *x_came, *y_came, *corners)
    z_came = exchange(sent, 2)

    def scratch(width):
        return [
            pltpu.VMEM((2 * LX * 48, width), F32),
            pltpu.VMEM((2, FX, 48, width), F32),
            pltpu.VMEM((2, CX, 48, width), F32),
            pltpu.VMEM((CX, 48, width), F32),
            pltpu.VMEM((CX, 48, width), F32),
            pltpu.VMEM((width // 128, 192, 128), F32),
        ]

    inner, power_inner, ends, fine_ends = call(
        smooth_inner, "smooth_inner", [smem()] * 2 + [vmem()] * 6,
        [shaped(2, 8, 32, 256), shaped(96, 128), shaped(WIDE, 128), shaped(2 * LX * 48, 128)],
        [pltpu.VMEM((2 * LX * 48, 128), F32)] + scratch(256),
    )(class_wavespeed, class_damping, wide, narrow, field, weights[0], weights[1], weights[2])
    ends, power, power_halo, *sent = call(
        smooth_ends, "smooth_ends", [smem()] * 2 + [vmem()] * 8,
        [shaped(2, 8, 32, 128)] + [shaped(96, 128)] * 4,
        [pltpu.VMEM(((WARM + 1) * ZB, 128), F32), pltpu.VMEM((2 * LX * 48, 128), F32)] + scratch(128),
    )(class_wavespeed, class_damping, ends, *z_came, strip, weights[2], weights[3], power_inner, fine_ends)
    x_came = exchange(sent, 0)

    block = shaped(TX, 24, 256)
    begun, later, wash, dose, pressure = call(
        bioheat_inner, "bioheat_inner", [vmem()] * 8,
        [block, shaped(2, 24, 256), shaped(QX, 24, 256), shaped(4, 16, 128), shaped(2, 8, 32, 256)],
        [
            pltpu.VMEM((TX, 24, 256), F32),
            pltpu.VMEM(((GROUPS - WARM) * ZB, 128), F32),
            pltpu.VMEM((2, 8, 32, 256), F32),
            pltpu.SemaphoreType.DMA,
        ],
        [vmem()] * 4 + [hbm()],
    )(narrow, *z_came, power, power_halo, injury_integral, inner, ends)
    warmth, dose = call(
        bioheat, "bioheat", [vmem()] * 8,
        [shaped(4, 16, 128), shaped(4, 16, 128)],
        [pltpu.VMEM((TX, 24, 256), F32), pltpu.VMEM((TX, 24, 256), F32)],
    )(begun, later, wash, dose, power, power_halo, *x_came)
    return pressure, warmth, dose


def solution(mesh):
    placed = (
        P(None, "gx", "gy", "gz"),
        P(None, "gx", "gy", "gz"),
        P("gx", "gy", "gz"),
        P(),
        P(),
        P(),
        P(),
        P(),
        P("gx", "gy", "gz"),
        P("gx", "gy", "gz"),
    )
    return jax.shard_map(
        on_device,
        mesh=mesh,
        in_specs=placed,
        out_specs=(P(None, "gx", "gy", "gz"), P("gx", "gy", "gz"), P("gx", "gy", "gz")),
        check_vma=False,
    )
```

```python
import jax
import jax.numpy as jnp
from jax import lax
from jax.experimental import pallas as pl
from jax.experimental.pallas import tpu as pltpu
from jax.sharding import PartitionSpec as P

F32 = jnp.float32
BF16 = jnp.bfloat16

RELAXATION = 0.8
DAMPING_SHIFT = 0.5
DIFFUSION = 0.15
HEATING = 0.25
LN_PREFACTOR = 226.78
ENERGY_BARRIER = 75535.0
CORE_WARMTH = 310.15

FX, CX, LX, TX, QX = 12, 10, 8, 12, 10
XB_CODE, XB_COARSE, XB_THERM, XB = 128, 160, 192, 256
YB_CODE, YB_COARSE, YB_THERM, YB = 128, 184, 204, 224
KB_CODE, KB_COARSE, KB_THERM, KB = 64, 78, 98, 128
WIDE = 2 * FX * 48 + CX * 48
N_CODE = 2 * FX * 48
N_COARSE, N_THETA, N_PERF, NARROW = 0, 512, 800, 1056
GROUPS = 16
ZB = (WIDE + NARROW) // GROUPS
WARM = (WIDE + N_THETA) // ZB
AXES = ("gx", "gy", "gz")


def vmem():
    return pl.BlockSpec(memory_space=pltpu.VMEM)


def hbm():
    return pl.BlockSpec(memory_space=pltpu.HBM)


def smem():
    return pl.BlockSpec(memory_space=pltpu.SMEM)


def swaps(sizes, axis, odd):
    count, targets = 1, []
    for n in sizes:
        count *= n
    for i in range(count):
        place, rest = [], i
        for n in reversed(sizes):
            place.insert(0, rest % n)
            rest //= n
        partner = list(place)
        partner[axis] = ((place[axis] + 1) ^ 1) - 1 if odd else place[axis] ^ 1
        if not 0 <= partner[axis] < sizes[axis]:
            other = 2 if axis != 2 else 0
            partner = list(place)
            partner[other] = place[other] ^ 1
        j = 0
        for n, at in zip(sizes, partner):
            j = j * n + at
        targets.append((i, j))
    return targets


def exchange(pair, axis):
    sizes = [lax.axis_size(name) for name in AXES]
    return [lax.ppermute(buffer, AXES, swaps(sizes, axis, bool(k))) for k, buffer in enumerate(pair)]


def is_even(axis):
    return lax.axis_index(AXES[axis]) % 2 == 0


class Sender:
    def __init__(self, first, second, axis):
        self.first, self.second, self.even = first, second, is_even(axis)

    def put(self, rows, lanes, up, down):
        self.first[rows, lanes] = jnp.where(self.even, up, down)
        self.second[rows, lanes] = jnp.where(self.even, down, up)


class Receiver:
    def __init__(self, first, second, axis):
        self.first, self.second, self.even = first, second, is_even(axis)

    def before(self, *at):
        return jnp.where(self.even, self.second[at], self.first[at])

    def after(self, *at):
        return jnp.where(self.even, self.first[at], self.second[at])


def exact_dot(values, weights):
    high = values.astype(BF16)
    rest = values - high.astype(F32)
    mid = rest.astype(BF16)
    low = (rest - mid.astype(F32)).astype(BF16)
    total = jnp.dot(high, weights, preferred_element_type=F32)
    total = total + jnp.dot(mid, weights, preferred_element_type=F32)
    return total + jnp.dot(low, weights, preferred_element_type=F32)


def iota(shape, dim):
    return lax.broadcasted_iota(jnp.int32, shape, dim)


def pick(codes, entries):
    value = jnp.where(codes == 0.0, entries[0], entries[1])
    value = jnp.where(codes == 2.0, entries[2], value)
    return jnp.where(codes == 3.0, entries[3], value)


def pack_x(wash_h, it_h, co_h, codes_h, theta_h, x_one, x_two, y_one, y_two, perf, it, co, codes, theta, pool, wash, sems):
    loads = [
        pltpu.make_async_copy(src, dst, sems.at[k])
        for k, (src, dst) in enumerate(
            ((codes_h, codes), (it_h, it), (wash_h, wash), (co_h, co), (theta_h, theta))
        )
    ]
    for load in loads:
        load.start()
    lane, col = iota((256, 128), 0), iota((256, 128), 1)
    pairs = jnp.where(lane // 2 == col, 1.0, 0.0).astype(BF16)
    loads[0].wait()
    loads[2].wait()
    entries = [wash[k] for k in range(4)]
    for i in range(4):
        both = pick(codes[2 * i].astype(F32), entries) + pick(codes[2 * i + 1].astype(F32), entries)
        for half in range(2):
            pool[half, i * 32 : i * 32 + 32, :] = both[:, half * 128 : half * 128 + 128]
    rows = jnp.concatenate([pool[h, pl.ds(0, 64, 2), :] + pool[h, pl.ds(1, 64, 2), :] for h in range(2)], axis=1)
    washed = exact_dot(rows, pairs) * 0.125
    for k in (1, 3, 4):
        loads[k].wait()
    for i in range(4):
        perf[i] = washed[i * 16 : i * 16 + 16]
    to, every = Sender(x_one, x_two, 0), pl.ds(0, 256)
    for c in range(2):
        for k in range(2):
            to.put(pl.ds((c * 2 + k) * 32, 32), every, it[c, 6 + k], it[c, k])
    to.put(pl.ds(XB_CODE, 32), every, codes[7].astype(F32), codes[0].astype(F32))
    for k in range(2):
        for c in range(2):
            to.put(pl.ds(XB_COARSE + 16 * k, 16), pl.ds(128 * c, 128), co[c, 2 + k], co[c, k])
    for i in range(4):
        for k, value in enumerate((theta[i], washed[i * 16 : i * 16 + 16])):
            to.put(pl.ds(XB_THERM + 16 * i, 16), pl.ds(128 * k, 128), value, value)
    to = Sender(y_one, y_two, 1)
    for c in range(2):
        for k in range(8):
            to.put(pl.ds((c * 8 + k) * 8, 8), every, it[c, k, 24:32, :], it[c, k, 0:8, :])
    for k in range(8):
        to.put(pl.ds(YB_CODE + k * 7, 7), every, codes[k, 25:32, :].astype(F32), codes[k, 0:7, :].astype(F32))
    for k in range(4):
        for c in range(2):
            to.put(pl.ds(YB_COARSE + k * 5, 5), pl.ds(128 * c, 128), co[c, k, 11:16, :], co[c, k, 0:5, :])
        for c, field in enumerate((theta, perf)):
            to.put(pl.ds(YB_THERM + k * 4, 4), pl.ds(128 * c, 128), field[k, 12:16, :], field[k, 0:4, :])


class Columns:
    def __init__(self, it, co, codes, theta, perf, beside):
        self.it, self.co, self.codes, self.theta, self.perf, self.beside = it, co, codes, theta, perf, beside

    def iterate(self, c, f, at, n):
        if 2 <= f < 10:
            return self.it[c, f - 2, pl.ds(at, n), :]
        side, k = (self.beside.before, f) if f < 2 else (self.beside.after, f - 10)
        return side(pl.ds((c * 2 + k) * 32 + at, n), pl.ds(0, 256))

    def code(self, f, at, n):
        if 1 <= f < 9:
            return self.codes[f - 1, pl.ds(at, n), :].astype(F32)
        side = self.beside.before if f < 1 else self.beside.after
        return side(pl.ds(XB_CODE + at, n), pl.ds(0, 256))

    def coarse(self, c, f, at, n):
        if 2 <= f < 6:
            return self.co[c, f - 2, pl.ds(at, n), :]
        side, k = (self.beside.before, f) if f < 2 else (self.beside.after, f - 6)
        return side(pl.ds(XB_COARSE + 16 * k + at, n), pl.ds(128 * c, 128))

    def warm(self, f, at, n):
        if 4 <= f < 8:
            return self.theta[f - 4, pl.ds(at, n), :]
        side, k = (self.beside.before, f) if f < 4 else (self.beside.after, f - 8)
        return side(pl.ds(XB_THERM + 16 * k + at, n), pl.ds(0, 128))

    def wash(self, f, at, n):
        if 3 <= f < 7:
            return self.perf[f - 3, pl.ds(at, n), :]
        side, k = (self.beside.before, f + 1) if f < 3 else (self.beside.after, f - 7)
        return side(pl.ds(XB_THERM + 16 * k + at, n), pl.ds(128, 128))


def pack_corner(y_one, y_two, after_this, one, two):
    came, to = Receiver(y_one, y_two, 1), Sender(one, two, 0)

    def put(at, n, lanes, up, down):
        for k, side in enumerate((came.after, came.before)):
            to.put(pl.ds(at + k * n, n), lanes, side(pl.ds(up, n), lanes), side(pl.ds(down, n), lanes))

    every = pl.ds(0, 256)
    for c in range(2):
        for k in range(2):
            put((c * 2 + k) * 16, 8, every, (c * 8 + 6 + k) * 8, (c * 8 + k) * 8)
    put(KB_CODE, 7, every, YB_CODE + 49, YB_CODE)
    for k in range(2):
        put(KB_COARSE + k * 10, 5, every, YB_COARSE + (2 + k) * 5, YB_COARSE + k * 5)
    for k in range(3):
        put(KB_THERM + k * 8, 4, every, YB_THERM + (1 + k) * 4, YB_THERM + k * 4)


def rows_of(wide, narrow, start, count, half):
    parts = []
    if start < WIDE:
        n = min(count, WIDE - start)
        parts.append(wide[pl.ds(start, n), pl.ds(128 * half, 128)])
        start, count = start + n, count - n
    if count:
        parts.append(narrow[pl.ds(start - WIDE, count), :])
    return parts[0] if len(parts) == 1 else jnp.concatenate(parts, axis=0)


def pack_z(it, co, codes, theta, perf, x_one, x_two, y_one, y_two, k_one, k_two, wide, narrow, one, two):
    block = Columns(it, co, codes, theta, perf, Receiver(x_one, x_two, 0))
    rows, corners = Receiver(y_one, y_two, 1), Receiver(k_one, k_two, 0)

    def beside(f, first, count, height, own, corner, lanes, skip=0):
        k = f - first
        if 0 <= k < count:
            at = pl.ds(own + k * height, height)
            return rows.after(at, lanes), rows.before(at, lanes)
        side, k = (corners.before, f - skip) if k < 0 else (corners.after, k - count)
        return [side(pl.ds(corner + (2 * k + j) * height, height), lanes) for j in range(2)]

    every = pl.ds(0, 256)
    for c in range(2):
        for f in range(FX):
            at = (c * FX + f) * 48
            wide[pl.ds(at, 32), :] = block.iterate(c, f, 0, 32)
            wide[pl.ds(at + 32, 8), :], wide[pl.ds(at + 40, 8), :] = beside(f, 2, 8, 8, c * 64, c * 32, every)
    for f in range(CX):
        at = N_CODE + f * 48
        wide[pl.ds(at, 32), :] = block.code(f, 0, 32)
        wide[pl.ds(at + 32, 16), :] = jnp.zeros((16, 256), F32)
        wide[pl.ds(at + 32, 7), :], wide[pl.ds(at + 41, 7), :] = beside(f, 1, 8, 7, YB_CODE, KB_CODE, every)
    for c in range(2):
        for f in range(LX):
            at = N_COARSE + (c * LX + f) * 32
            over, under = beside(f, 2, 4, 5, YB_COARSE, KB_COARSE, pl.ds(128 * c, 128))
            narrow[pl.ds(at, 16), :] = block.coarse(c, f, 0, 16)
            narrow[pl.ds(at + 24, 8), :] = jnp.zeros((8, 128), F32)
            narrow[pl.ds(at + 16, 4), :] = over[0:4]
            narrow[pl.ds(at + 20, 4), :] = under[1:5]
            narrow[pl.ds(at + 24, 1), :] = under[0:1]
            narrow[pl.ds(at + 25, 1), :] = over[4:5]
    for f in range(TX):
        at = N_THETA + f * 24
        narrow[pl.ds(at, 16), :] = block.warm(f, 0, 16)
        if 0 < f < 11:
            over, under = beside(f, 4, 4, 4, YB_THERM, KB_THERM, pl.ds(0, 128), 1)
        else:
            over = under = jnp.zeros((4, 128), F32)
        narrow[pl.ds(at + 16, 4), :], narrow[pl.ds(at + 20, 4), :] = over, under
    for f in range(QX):
        at = N_PERF + f * 24
        narrow[pl.ds(at, 16), :] = block.wash(f, 0, 16)
        over, under = beside(f + 1, 4, 4, 4, YB_THERM, KB_THERM, pl.ds(128, 128), 1)
        narrow[pl.ds(at + 16, 4), :], narrow[pl.ds(at + 20, 4), :] = over, under
    narrow[pl.ds(N_PERF + QX * 24, NARROW - N_PERF - QX * 24), :] = jnp.zeros((NARROW - N_PERF - QX * 24, 128), F32)
    lane, ends = iota((ZB, 128), 1) // 8, []
    for half, shift in ((1, 8), (0, 0)):
        packed = None
        for g in range(GROUPS):
            part = rows_of(wide, narrow, g * ZB, ZB, half)
            turn = (8 * g + shift) % 128
            part = pltpu.roll(part, turn, 1) if turn else part
            packed = part if packed is None else jnp.where(lane == g, part, packed)
        ends.append(packed)
    Sender(one, two, 2).put(pl.ds(0, ZB), pl.ds(0, 128), *ends)


def unpack_z(one, two, groups, lane_after, halo):
    lane = iota((ZB, 128), 1)
    came, every = Receiver(one, two, 2), (pl.ds(0, ZB), pl.ds(0, 128))
    right, left = came.after(*every), came.before(*every)
    for k, g in enumerate(groups):
        turn = (128 + lane_after - 8 * g) % 128
        after = pltpu.roll(right, turn, 1) if turn else right
        turn = (120 - 8 * g) % 128
        before = pltpu.roll(left, turn, 1) if turn else left
        halo[pl.ds(k * ZB, ZB), :] = jnp.where(lane < 96, after, before)


def strip_cell(lane):
    return jnp.where(lane < 32, lane, jnp.where(lane < 96, lane + 192, lane - 128))


def sources(loc_h, exc_h, after_this, field, strip, spread, gather, spread_strip, gather_strip, loc_s, exc_s, loc, sems):
    loads = [
        pltpu.make_async_copy(src, dst, sems.at[k])
        for k, (src, dst) in enumerate(((loc_h, loc), (loc_h, loc_s), (exc_h, exc_s)))
    ]
    for load in loads:
        load.start()
    field[...] = jnp.zeros(field.shape, F32)
    strip[...] = jnp.zeros(strip.shape, F32)
    coord = [lax.axis_index(name) for name in AXES]
    for load in loads:
        load.wait()
    first = loc[0:1, :] - coord[0] * 8
    second = loc[1:2, :] - coord[1] * 32
    third = loc[2:3, :] - coord[2] * 256
    near = (first >= -1) & (first < 9) & (second >= -7) & (second < 39) & (third >= -7) & (third < 263)
    order = iota((1, 1024), 1)
    lane, cell = iota((1, 256), 1), strip_cell(iota((1, 128), 1))

    def place(state):
        e, keys = state
        x = loc_s[0, e] - coord[0] * 8 + 1
        y = loc_s[1, e] - coord[1] * 32
        z = loc_s[2, e] - coord[2] * 256
        y = jnp.where(y < 0, y + 48, y)
        for c in range(2):
            field[c, x, pl.ds(y, 1), :] += jnp.where(lane == z, exc_s[c, e], 0.0)
            strip[c, x, pl.ds(y, 1), :] += jnp.where(cell == z, exc_s[c, e], 0.0)
        keys = jnp.where(order == e, 1024, keys)
        return jnp.min(keys), keys

    keys = jnp.where(near, order, 1024)
    lax.while_loop(lambda state: state[0] < 1024, place, (jnp.min(keys), keys))

    def weights(cell, column, at):
        centre = cell >> 1
        beside = centre + jnp.where((cell & 1) == 1, 1, -1)
        weight = jnp.where(column == at(centre), 0.75, jnp.where(column == at(beside), 0.25, 0.0))
        return weight.astype(BF16)

    spread[...] = weights(iota((128, 256), 1), iota((128, 256), 0), lambda c: c)
    spread_strip[...] = weights(
        strip_cell(iota((256, 128), 1)),
        iota((256, 128), 0),
        lambda c: jnp.where(c < 0, c + 256, jnp.where(c < 128, c, c + 64)),
    )
    gather[...] = jnp.where(iota((256, 128), 1) == iota((256, 128), 0) >> 1, 1.0, 0.0).astype(BF16)
    centre = strip_cell(iota((128, 256), 0)) >> 1
    centre = jnp.where(centre < 0, centre + 256, centre)
    gather_strip[...] = jnp.where(iota((128, 256), 1) == centre, 1.0, 0.0).astype(BF16)


def flag(test):
    return jnp.where(test, 1.0, 0.0)


def x_flags():
    at = lax.axis_index("gx")
    return flag(at > 0), flag(at < 3)


def along_y(cells, row):
    lanes = cells.shape[1]
    centre = cells[0:24]
    lower = jnp.where(row == 20, jnp.broadcast_to(cells[24:25], (24, lanes)), pltpu.roll(centre, 1, 0))
    upper = jnp.where(row == 19, jnp.broadcast_to(cells[25:26], (24, lanes)), pltpu.roll(centre, 23, 0))
    return 0.75 * centre + 0.25 * lower, 0.75 * centre + 0.25 * upper


def coarse_rows(read, z_ok, grown):
    x_before, x_after = x_flags()
    at_y = lax.axis_index("gy")
    row = iota((32, 128), 0)
    y_ok = jnp.where(row < 16, 1.0, jnp.where((row < 20) | (row == 25), flag(at_y < 15), flag(at_y > 0)))
    inside = y_ok if z_ok is None else y_ok * z_ok
    row = iota((24, 128), 0)
    for c in range(2):
        for f in range(LX):
            x_ok = x_before if f < 2 else x_after if f >= 6 else None
            even, odd = along_y(read((c * LX + f) * 32) * (inside if x_ok is None else inside * x_ok), row)
            to = (c * LX + f) * 48
            grown[pl.ds(to, 24, 2), :] = even
            grown[pl.ds(to + 1, 24, 2), :] = odd


def relax(width, start, classes, z_ok, fine, drive, wave_t, damp_t, first, second, gain_r, gain_i, pool, emit):
    x_before, x_after = x_flags()
    at_y = lax.axis_index("gy")
    row = iota((48, width), 0)
    inside = jnp.where(row < 32, 1.0, jnp.where(row < 40, flag(at_y < 15), flag(at_y > 0)))
    if z_ok is not None:
        inside = inside * z_ok
    for c in range(2):
        for f in range(FX):
            near = c * LX + f // 2 + 1
            far = near + (1 if f % 2 else -1)
            grow = 0.75 * fine[pl.ds(near * 48, 48), :] + 0.25 * fine[pl.ds(far * 48, 48), :]
            x_ok = x_before if f < 2 else x_after if f >= 10 else None
            first[c, f] = (start((c * FX + f) * 48) + grow) * (inside if x_ok is None else inside * x_ok)

    gains_r, gains_i, damps = [], [], []
    for t in range(4):
        speed = jnp.full((8, 128), wave_t[t], F32)
        damp = jnp.full((8, 128), damp_t[t], F32)
        wave = 1.0 / (speed * speed)
        diag_r = 6.0 - wave
        diag_i = DAMPING_SHIFT * wave + damp
        modulus = diag_r * diag_r + diag_i * diag_i
        gains_r.append((RELAXATION * diag_r / modulus)[0:1, 0:1])
        gains_i.append((RELAXATION * diag_i / modulus)[0:1, 0:1])
        damps.append(damp_t[t])

    def step(cells, f, drive_f, g_r, g_i):
        sums = []
        for c in range(2):
            mid = cells[c, f]
            total = cells[c, f - 1] + cells[c, f + 1] + drive[c, drive_f]
            total = total + pltpu.roll(mid, 1, 0) + pltpu.roll(mid, 47, 0)
            sums.append((mid, total + pltpu.roll(mid, 1, 1) + pltpu.roll(mid, width - 1, 1)))
        (mid_r, sum_r), (mid_i, sum_i) = sums
        keep = 1.0 - RELAXATION
        return keep * mid_r + (g_r * sum_r + g_i * sum_i), keep * mid_i + (g_r * sum_i - g_i * sum_r)

    for f in range(CX):
        codes = classes(N_CODE + f * 48)
        x_ok = x_before if f < 1 else x_after if f >= 9 else None
        ok = inside if x_ok is None else inside * x_ok
        g_r = pick(codes, gains_r) * ok
        g_i = pick(codes, gains_i) * ok
        gain_r[f], gain_i[f] = g_r, g_i
        second[0, f], second[1, f] = step(first, f + 1, f, g_r, g_i)

    for i in range(4):
        heat = None
        for f in (2 * i, 2 * i + 1):
            new_r, new_i = step(second, f + 1, f + 1, gain_r[f + 1], gain_i[f + 1])
            emit(f, new_r, new_i)
            layer = pick(classes(N_CODE + (f + 1) * 48), damps) * (new_r * new_r + new_i * new_i)
            heat = layer if heat is None else heat + layer
        for tile in range(width // 128):
            pool[tile, pl.ds(i * 48, 48), :] = heat[:, tile * 128 : tile * 128 + 128]
    tiles = [pool[t, pl.ds(0, 96, 2), :] + pool[t, pl.ds(1, 96, 2), :] for t in range(width // 128)]
    return tiles[0] if len(tiles) == 1 else jnp.concatenate(tiles, axis=1)


def smooth_inner(wave_t, damp_t, wide, narrow, source, spread, gather, spread_strip, out, power, ends, fine_ends,
                 grown, fine, first, second, gain_r, gain_i, pool):
    coarse_rows(lambda at: narrow[pl.ds(N_COARSE + at, 32), :], None, grown)
    fine[...] = exact_dot(grown[pl.ds(0, 2 * LX * 48), :], spread[...])
    fine_ends[...] = exact_dot(grown[pl.ds(0, 2 * LX * 48), :], spread_strip[pl.ds(0, 128), :])
    lane = iota((48, 128), 1)
    for at in range(0, WIDE, 48):
        turned = pltpu.roll(wide[pl.ds(at, 48), pl.ds(128, 128)], 64, 1)
        ends[pl.ds(at, 48), :] = jnp.where(lane < 32, wide[pl.ds(at, 48), pl.ds(0, 128)], turned)

    def own(at):
        return wide[pl.ds(at, 48), :]

    def emit(f, new_r, new_i):
        out[0, f] = new_r[0:32]
        out[1, f] = new_i[0:32]

    sums = relax(256, own, own, None, fine, source, wave_t, damp_t, first, second, gain_r, gain_i, pool, emit)
    power[...] = exact_dot(sums, gather[...]) * 0.125


def smooth_ends(wave_t, damp_t, ends, z_one, z_two, source, spread, gather, power_inner, fine_ends,
                out, power, power_halo, one, two,
                halo, grown_halo, fine, first, second, gain_r, gain_i, pool):
    unpack_z(z_one, z_two, range(WARM + 1), 64, halo)
    at_z = lax.axis_index("gz")
    after_ok, before_ok = flag(at_z < 3), flag(at_z > 0)
    z_ok = jnp.where(iota((32, 128), 1) < 96, after_ok, before_ok)
    coarse_rows(lambda at: halo[pl.ds(WIDE + N_COARSE + at, 32), :], z_ok, grown_halo)
    fine[...] = fine_ends[...] + exact_dot(grown_halo[pl.ds(0, 2 * LX * 48), :], spread[pl.ds(128, 128), :])

    lane = iota((48, 128), 1)

    def strip(at):
        return jnp.where(lane < 64, ends[pl.ds(at, 48), :], halo[pl.ds(at, 48), :])

    def emit(f, new_r, new_i):
        out[0, f] = new_r[0:32]
        out[1, f] = new_i[0:32]

    z_ok = jnp.where(lane < 64, 1.0, jnp.where(lane < 96, after_ok, before_ok))
    live = jnp.where((lane < 72) | (lane >= 120), z_ok, 0.0)
    sums = relax(128, strip, strip, live, fine, source, wave_t, damp_t, first, second, gain_r, gain_i, pool, emit)
    sums = exact_dot(sums, gather[...]) * 0.125
    lane = iota((96, 128), 1)
    own = jnp.where((lane < 4) | (lane >= 124), sums[:, 0:128], power_inner[...])
    over = sums[:, 128:256]
    power[...], power_halo[...] = own, over

    def packed(first_layer):
        group, total = iota((24, 128), 1) // 16, None
        for k in range(3):
            at = (first_layer + k) * 24
            turned = pltpu.roll(over[at : at + 24], 16 * k + 8, 1)
            total = turned if total is None else jnp.where(group == k, turned, total)
        return total

    to, every = Sender(one, two, 0), pl.ds(0, 128)
    to.put(pl.ds(0, 72), every, own[24:96], own[0:72])
    to.put(pl.ds(72, 24), every, packed(1), packed(0))


class Bioheat:
    def __init__(self):
        x_before, x_after = x_flags()
        at_y, at_z = lax.axis_index("gy"), lax.axis_index("gz")
        row, col = iota((24, 256), 0), iota((24, 256), 1)
        y_ok = jnp.where(row < 16, 1.0, jnp.where(row < 20, flag(at_y < 15), flag(at_y > 0)))
        z_ok = jnp.where(col < 128, 1.0, jnp.where(col < 192, flag(at_z < 3), flag(at_z > 0)))
        inside = y_ok * z_ok
        self.edge = [inside * (x_before if f < 4 else x_after) if not 4 <= f < 8 else inside for f in range(TX)]

    def step(self, state, wash, f):
        mid = state[f]
        beside = state[f - 1] + state[f + 1]
        beside = beside + pltpu.roll(mid, 1, 0) + pltpu.roll(mid, 23, 0)
        beside = beside + pltpu.roll(mid, 1, 1) + pltpu.roll(mid, 255, 1)
        return mid + DIFFUSION * (beside - 6.0 * mid) - wash[f - 1] * mid

    def finish(self, cooled, heat, f):
        return (cooled + HEATING * heat) * self.edge[f]


def injury_of(warm):
    own = warm[0:16, 0:128]
    return jnp.exp(LN_PREFACTOR - ENERGY_BARRIER / (CORE_WARMTH + own))


def own_heat(power, power_halo, f):
    return jnp.concatenate([ref[pl.ds(24 * (f - 4), 24), :] for ref in (power, power_halo)], axis=1)


def bioheat_inner(narrow, z_one, z_two, power, power_halo, injury, inner, ends, begun, later, wash, dose, wave_out,
                  now, tiles, wave, sem):
    low, high = iota((32, 128), 1) < 8, iota((32, 128), 1) >= 120
    for c in range(2):
        for f in range(8):
            new = ends[c, f]
            wave[c, f, :, pl.ds(0, 128)] = jnp.where(low, new, inner[c, f, :, pl.ds(0, 128)])
            turned = pltpu.roll(new, 64, 1)
            wave[c, f, :, pl.ds(128, 128)] = jnp.where(high, turned, inner[c, f, :, pl.ds(128, 128)])
    store = pltpu.make_async_copy(wave, wave_out, sem)
    store.start()
    unpack_z(z_one, z_two, range(WARM, GROUPS), 0, tiles)
    heat = Bioheat()

    def extended(base, f):
        at = base + f * 24
        return jnp.concatenate([narrow[pl.ds(at, 24), :], tiles[pl.ds(WIDE + at - WARM * ZB, 24), :]], axis=1)

    for f in range(TX):
        now[f] = extended(N_THETA, f) * heat.edge[f]
    for f in range(QX):
        wash[f] = extended(N_PERF, f)
    for f in range(1, TX - 1):
        new = heat.step(now, wash, f)
        if 4 <= f < 8:
            new = heat.finish(new, own_heat(power, power_halo, f), f)
            dose[f - 4] = injury[f - 4] + injury_of(new)
        begun[f] = new
    for f in (5, 6):
        new = heat.finish(heat.step(begun, wash, f), own_heat(power, power_halo, f), f)
        later[f - 5] = new
        dose[f - 4] = dose[f - 4] + injury_of(new)
    store.wait()


def bioheat(begun, later, wash, dose_in, power, power_halo, x_one, x_two, warm_out, dose_out, one, two):
    heat = Bioheat()
    came = Receiver(x_one, x_two, 0)

    def sent(side, k):
        beyond = side(pl.ds(72, 24), pl.ds(0, 128))
        beyond = jnp.where(iota((24, 128), 1) // 16 == k, beyond, 0.0)
        return jnp.concatenate([side(pl.ds(24 * k, 24), pl.ds(0, 128)), pltpu.roll(beyond, 120 - 16 * k, 1)], axis=1)

    own = [own_heat(power, power_halo, f) for f in range(4, 8)]
    heats = [None] + [sent(came.before, k) for k in range(3)] + own + [sent(came.after, k) for k in range(3)]
    for f in range(1, TX - 1):
        one[f] = begun[f] if 4 <= f < 8 else heat.finish(begun[f], heats[f], f)
    dose = [dose_in[i] for i in range(4)]
    state, other = one, two
    for turn in range(1, 4):
        for f in range(1 + turn, TX - 1 - turn):
            if turn == 1 and f in (5, 6):
                other[f] = later[f - 5]
                continue
            new = heat.finish(heat.step(state, wash, f), heats[f], f)
            if turn < 3:
                other[f] = new
            if 4 <= f < 8:
                dose[f - 4] = dose[f - 4] + injury_of(new)
                if turn == 3:
                    warm_out[f - 4] = new[0:16, 0:128]
        state, other = other, state
    for i in range(4):
        dose_out[i] = jnp.log(dose[i])


def shaped(*shape, dtype=F32):
    return jax.ShapeDtypeStruct(shape, dtype)


def call(kernel, name, in_specs, outs, scratch=(), out_specs=None, cost=2000):
    return pl.pallas_call(
        kernel,
        name=name,
        out_shape=tuple(outs),
        in_specs=in_specs,
        out_specs=tuple(out_specs or [vmem() for _ in outs]),
        scratch_shapes=list(scratch),
        cost_estimate=pl.CostEstimate(flops=cost * 1000, bytes_accessed=cost * 1000, transcendentals=0),
        compiler_params=pltpu.CompilerParams(vmem_limit_bytes=24 * 1024 * 1024),
    )


def on_device(
    acoustic_iterate,
    coarse_update,
    class_codes_volume,
    element_location,
    element_excitation,
    class_wavespeed,
    class_damping,
    washout_fraction,
    thermal_excess,
    injury_integral,
):
    def in_hbm(*arrays):
        return [pltpu.with_memory_space_constraint(array, pltpu.HBM) for array in arrays]

    *sent, perf, it, co, codes, theta = call(
        pack_x, "pack_x", [hbm()] * 5,
        [
            shaped(XB, 256),
            shaped(XB, 256),
            shaped(YB, 256),
            shaped(YB, 256),
            shaped(4, 16, 128),
            shaped(2, 8, 32, 256),
            shaped(2, 4, 16, 128),
            shaped(8, 32, 256, dtype=jnp.int32),
            shaped(4, 16, 128),
        ],
        [pltpu.VMEM((2, 128 + 8, 128), F32), pltpu.SMEM((4,), F32), pltpu.SemaphoreType.DMA((5,))],
    )(*in_hbm(washout_fraction, acoustic_iterate, coarse_update, class_codes_volume, thermal_excess))
    own = (it, co, codes, theta, perf)
    y_came = exchange(sent[2:], 1)
    x_came = exchange(sent[:2], 0)

    field, strip, *weights = call(
        sources, "sources", [hbm(), hbm(), vmem()],
        [
            shaped(2, CX, 48, 256),
            shaped(2, CX, 48, 128),
            shaped(128, 256, dtype=BF16),
            shaped(256, 128, dtype=BF16),
            shaped(256, 128, dtype=BF16),
            shaped(128, 256, dtype=BF16),
        ],
        [
            pltpu.SMEM((3, 1024), jnp.int32),
            pltpu.SMEM((2, 1024), F32),
            pltpu.VMEM((3, 1024), jnp.int32),
            pltpu.SemaphoreType.DMA((3,)),
        ],
        cost=8000,
    )(*in_hbm(element_location.T, element_excitation), perf)
    sent = call(pack_corner, "pack_corner", [vmem()] * 3, [shaped(KB, 256)] * 2)(*y_came, weights[0])
    corners = exchange(sent, 0)

    wide, narrow, *sent = call(
        pack_z, "pack_z", [vmem()] * 11,
        [shaped(WIDE, 256), shaped(NARROW, 128)] + [shaped(ZB, 128)] * 2,
    )(*own, *x_came, *y_came, *corners)
    z_came = exchange(sent, 2)

    def scratch(width):
        return [
            pltpu.VMEM((2 * LX * 48, width), F32),
            pltpu.VMEM((2, FX, 48, width), F32),
            pltpu.VMEM((2, CX, 48, width), F32),
            pltpu.VMEM((CX, 48, width), F32),
            pltpu.VMEM((CX, 48, width), F32),
            pltpu.VMEM((width // 128, 192 + 8, 128), F32),
        ]

    inner, power_inner, ends, fine_ends = call(
        smooth_inner, "smooth_inner", [smem()] * 2 + [vmem()] * 6,
        [shaped(2, 8, 32, 256), shaped(96, 128), shaped(WIDE, 128), shaped(2 * LX * 48, 128)],
        [pltpu.VMEM((2 * LX * 48 + 8, 128), F32)] + scratch(256),
    )(class_wavespeed, class_damping, wide, narrow, field, weights[0], weights[1], weights[2])
    ends, power, power_halo, *sent = call(
        smooth_ends, "smooth_ends", [smem()] * 2 + [vmem()] * 8,
        [shaped(2, 8, 32, 128)] + [shaped(96, 128)] * 4,
        [pltpu.VMEM(((WARM + 1) * ZB, 128), F32), pltpu.VMEM((2 * LX * 48 + 8, 128), F32)] + scratch(128),
    )(class_wavespeed, class_damping, ends, *z_came, strip, weights[2], weights[3], power_inner, fine_ends)
    x_came = exchange(sent, 0)

    block = shaped(TX, 24, 256)
    begun, later, wash, dose, pressure = call(
        bioheat_inner, "bioheat_inner", [vmem()] * 8,
        [block, shaped(2, 24, 256), shaped(QX, 24, 256), shaped(4, 16, 128), shaped(2, 8, 32, 256)],
        [
            pltpu.VMEM((TX, 24, 256), F32),
            pltpu.VMEM(((GROUPS - WARM) * ZB, 128), F32),
            pltpu.VMEM((2, 8, 32, 256), F32),
            pltpu.SemaphoreType.DMA,
        ],
        [vmem()] * 4 + [hbm()],
    )(narrow, *z_came, power, power_halo, injury_integral, inner, ends)
    warmth, dose = call(
        bioheat, "bioheat", [vmem()] * 8,
        [shaped(4, 16, 128), shaped(4, 16, 128)],
        [pltpu.VMEM((TX, 24, 256), F32), pltpu.VMEM((TX, 24, 256), F32)],
    )(begun, later, wash, dose, power, power_halo, *x_came)
    return pressure, warmth, dose


def solution(mesh):
    placed = (
        P(None, "gx", "gy", "gz"),
        P(None, "gx", "gy", "gz"),
        P("gx", "gy", "gz"),
        P(),
        P(),
        P(),
        P(),
        P(),
        P("gx", "gy", "gz"),
        P("gx", "gy", "gz"),
    )
    return jax.shard_map(
        on_device,
        mesh=mesh,
        in_specs=placed,
        out_specs=(P(None, "gx", "gy", "gz"), P("gx", "gy", "gz"), P("gx", "gy", "gz")),
        check_vma=False,
    )
```

```python
import jax
import jax.numpy as jnp
from jax import lax
from jax.experimental import pallas as pl
from jax.experimental.pallas import tpu as pltpu
from jax.sharding import PartitionSpec as P

F32 = jnp.float32
BF16 = jnp.bfloat16

RELAXATION = 0.8
DAMPING_SHIFT = 0.5
DIFFUSION = 0.15
HEATING = 0.25
LN_PREFACTOR = 226.78
ENERGY_BARRIER = 75535.0
CORE_WARMTH = 310.15

FX, CX, LX, TX, QX = 12, 10, 8, 12, 10
XB_CODE, XB_COARSE, XB_THERM, XB = 128, 160, 192, 256
YB_CODE, YB_COARSE, YB_THERM, YB = 128, 184, 204, 224
KB_CODE, KB_COARSE, KB_THERM, KB = 64, 78, 98, 128
WIDE = 2 * FX * 48 + CX * 48
N_CODE = 2 * FX * 48
N_COARSE, N_THETA, N_PERF, NARROW = 0, 512, 800, 1056
GROUPS = 16
ZB = (WIDE + NARROW) // GROUPS
WARM = (WIDE + N_THETA) // ZB
AXES = ("gx", "gy", "gz")


def vmem():
    return pl.BlockSpec(memory_space=pltpu.VMEM)


def hbm():
    return pl.BlockSpec(memory_space=pltpu.HBM)


def smem():
    return pl.BlockSpec(memory_space=pltpu.SMEM)


def swaps(sizes, axis, odd):
    count, targets = 1, []
    for n in sizes:
        count *= n
    for i in range(count):
        place, rest = [], i
        for n in reversed(sizes):
            place.insert(0, rest % n)
            rest //= n
        partner = list(place)
        partner[axis] = ((place[axis] + 1) ^ 1) - 1 if odd else place[axis] ^ 1
        if not 0 <= partner[axis] < sizes[axis]:
            other = 2 if axis != 2 else 0
            partner = list(place)
            partner[other] = place[other] ^ 1
        j = 0
        for n, at in zip(sizes, partner):
            j = j * n + at
        targets.append((i, j))
    return targets


def exchange(pair, axis):
    sizes = [lax.axis_size(name) for name in AXES]
    return [lax.ppermute(buffer, AXES, swaps(sizes, axis, bool(k))) for k, buffer in enumerate(pair)]


def is_even(axis):
    return lax.axis_index(AXES[axis]) % 2 == 0


class Sender:
    def __init__(self, first, second, axis):
        self.first, self.second, self.even = first, second, is_even(axis)

    def put(self, rows, lanes, up, down):
        self.first[rows, lanes] = jnp.where(self.even, up, down)
        self.second[rows, lanes] = jnp.where(self.even, down, up)


class Receiver:
    def __init__(self, first, second, axis):
        self.first, self.second, self.even = first, second, is_even(axis)

    def before(self, *at):
        return jnp.where(self.even, self.second[at], self.first[at])

    def after(self, *at):
        return jnp.where(self.even, self.first[at], self.second[at])


def exact_dot(values, weights):
    high = values.astype(BF16)
    rest = values - high.astype(F32)
    mid = rest.astype(BF16)
    low = (rest - mid.astype(F32)).astype(BF16)
    total = jnp.dot(high, weights, preferred_element_type=F32)
    total = total + jnp.dot(mid, weights, preferred_element_type=F32)
    return total + jnp.dot(low, weights, preferred_element_type=F32)


def iota(shape, dim):
    return lax.broadcasted_iota(jnp.int32, shape, dim)


def pick(codes, entries):
    value = jnp.where(codes == 0.0, entries[0], entries[1])
    value = jnp.where(codes == 2.0, entries[2], value)
    return jnp.where(codes == 3.0, entries[3], value)


def pack_x(wash_h, it_h, co_h, codes_h, theta_h, x_one, x_two, y_one, y_two, perf, it, co, codes, theta, pool, wash, sems):
    loads = [
        pltpu.make_async_copy(src, dst, sems.at[k])
        for k, (src, dst) in enumerate(
            ((codes_h, codes), (it_h, it), (wash_h, wash), (co_h, co), (theta_h, theta))
        )
    ]
    for load in loads:
        load.start()
    lane, col = iota((256, 128), 0), iota((256, 128), 1)
    pairs = jnp.where(lane // 2 == col, 1.0, 0.0).astype(BF16)
    loads[0].wait()
    loads[2].wait()
    entries = [wash[k] for k in range(4)]
    for i in range(4):
        both = pick(codes[2 * i].astype(F32), entries) + pick(codes[2 * i + 1].astype(F32), entries)
        for half in range(2):
            pool[half, i * 32 : i * 32 + 32, :] = both[:, half * 128 : half * 128 + 128]
    rows = jnp.concatenate([pool[h, pl.ds(0, 64, 2), :] + pool[h, pl.ds(1, 64, 2), :] for h in range(2)], axis=1)
    washed = exact_dot(rows, pairs) * 0.125
    for k in (1, 3, 4):
        loads[k].wait()
    for i in range(4):
        perf[i] = washed[i * 16 : i * 16 + 16]
    to, every = Sender(x_one, x_two, 0), pl.ds(0, 256)
    for c in range(2):
        for k in range(2):
            to.put(pl.ds((c * 2 + k) * 32, 32), every, it[c, 6 + k], it[c, k])
    to.put(pl.ds(XB_CODE, 32), every, codes[7].astype(F32), codes[0].astype(F32))
    for k in range(2):
        for c in range(2):
            to.put(pl.ds(XB_COARSE + 16 * k, 16), pl.ds(128 * c, 128), co[c, 2 + k], co[c, k])
    for i in range(4):
        for k, value in enumerate((theta[i], washed[i * 16 : i * 16 + 16])):
            to.put(pl.ds(XB_THERM + 16 * i, 16), pl.ds(128 * k, 128), value, value)
    to = Sender(y_one, y_two, 1)
    for c in range(2):
        for k in range(8):
            to.put(pl.ds((c * 8 + k) * 8, 8), every, it[c, k, 24:32, :], it[c, k, 0:8, :])
    for k in range(8):
        to.put(pl.ds(YB_CODE + k * 7, 7), every, codes[k, 25:32, :].astype(F32), codes[k, 0:7, :].astype(F32))
    for k in range(4):
        for c in range(2):
            to.put(pl.ds(YB_COARSE + k * 5, 5), pl.ds(128 * c, 128), co[c, k, 11:16, :], co[c, k, 0:5, :])
        for c, field in enumerate((theta, perf)):
            to.put(pl.ds(YB_THERM + k * 4, 4), pl.ds(128 * c, 128), field[k, 12:16, :], field[k, 0:4, :])


class Columns:
    def __init__(self, it, co, codes, theta, perf, beside):
        self.it, self.co, self.codes, self.theta, self.perf, self.beside = it, co, codes, theta, perf, beside

    def iterate(self, c, f, at, n):
        if 2 <= f < 10:
            return self.it[c, f - 2, pl.ds(at, n), :]
        side, k = (self.beside.before, f) if f < 2 else (self.beside.after, f - 10)
        return side(pl.ds((c * 2 + k) * 32 + at, n), pl.ds(0, 256))

    def code(self, f, at, n):
        if 1 <= f < 9:
            return self.codes[f - 1, pl.ds(at, n), :].astype(F32)
        side = self.beside.before if f < 1 else self.beside.after
        return side(pl.ds(XB_CODE + at, n), pl.ds(0, 256))

    def coarse(self, c, f, at, n):
        if 2 <= f < 6:
            return self.co[c, f - 2, pl.ds(at, n), :]
        side, k = (self.beside.before, f) if f < 2 else (self.beside.after, f - 6)
        return side(pl.ds(XB_COARSE + 16 * k + at, n), pl.ds(128 * c, 128))

    def warm(self, f, at, n):
        if 4 <= f < 8:
            return self.theta[f - 4, pl.ds(at, n), :]
        side, k = (self.beside.before, f) if f < 4 else (self.beside.after, f - 8)
        return side(pl.ds(XB_THERM + 16 * k + at, n), pl.ds(0, 128))

    def wash(self, f, at, n):
        if 3 <= f < 7:
            return self.perf[f - 3, pl.ds(at, n), :]
        side, k = (self.beside.before, f + 1) if f < 3 else (self.beside.after, f - 7)
        return side(pl.ds(XB_THERM + 16 * k + at, n), pl.ds(128, 128))


def pack_corner(y_one, y_two, after_this, one, two):
    came, to = Receiver(y_one, y_two, 1), Sender(one, two, 0)

    def put(at, n, lanes, up, down):
        for k, side in enumerate((came.after, came.before)):
            to.put(pl.ds(at + k * n, n), lanes, side(pl.ds(up, n), lanes), side(pl.ds(down, n), lanes))

    every = pl.ds(0, 256)
    for c in range(2):
        for k in range(2):
            put((c * 2 + k) * 16, 8, every, (c * 8 + 6 + k) * 8, (c * 8 + k) * 8)
    put(KB_CODE, 7, every, YB_CODE + 49, YB_CODE)
    for k in range(2):
        put(KB_COARSE + k * 10, 5, every, YB_COARSE + (2 + k) * 5, YB_COARSE + k * 5)
    for k in range(3):
        put(KB_THERM + k * 8, 4, every, YB_THERM + (1 + k) * 4, YB_THERM + k * 4)


def rows_of(wide, narrow, start, count, half):
    parts = []
    if start < WIDE:
        n = min(count, WIDE - start)
        parts.append(wide[pl.ds(start, n), pl.ds(128 * half, 128)])
        start, count = start + n, count - n
    if count:
        parts.append(narrow[pl.ds(start - WIDE, count), :])
    return parts[0] if len(parts) == 1 else jnp.concatenate(parts, axis=0)


def pack_z(it, co, codes, theta, perf, x_one, x_two, y_one, y_two, k_one, k_two, wide, narrow, one, two):
    block = Columns(it, co, codes, theta, perf, Receiver(x_one, x_two, 0))
    rows, corners = Receiver(y_one, y_two, 1), Receiver(k_one, k_two, 0)

    def beside(f, first, count, height, own, corner, lanes, skip=0):
        k = f - first
        if 0 <= k < count:
            at = pl.ds(own + k * height, height)
            return rows.after(at, lanes), rows.before(at, lanes)
        side, k = (corners.before, f - skip) if k < 0 else (corners.after, k - count)
        return [side(pl.ds(corner + (2 * k + j) * height, height), lanes) for j in range(2)]

    every = pl.ds(0, 256)
    for c in range(2):
        for f in range(FX):
            at = (c * FX + f) * 48
            wide[pl.ds(at, 32), :] = block.iterate(c, f, 0, 32)
            wide[pl.ds(at + 32, 8), :], wide[pl.ds(at + 40, 8), :] = beside(f, 2, 8, 8, c * 64, c * 32, every)
    for f in range(CX):
        at = N_CODE + f * 48
        wide[pl.ds(at, 32), :] = block.code(f, 0, 32)
        wide[pl.ds(at + 32, 16), :] = jnp.zeros((16, 256), F32)
        wide[pl.ds(at + 32, 7), :], wide[pl.ds(at + 41, 7), :] = beside(f, 1, 8, 7, YB_CODE, KB_CODE, every)
    for c in range(2):
        for f in range(LX):
            at = N_COARSE + (c * LX + f) * 32
            over, under = beside(f, 2, 4, 5, YB_COARSE, KB_COARSE, pl.ds(128 * c, 128))
            narrow[pl.ds(at, 16), :] = block.coarse(c, f, 0, 16)
            narrow[pl.ds(at + 24, 8), :] = jnp.zeros((8, 128), F32)
            narrow[pl.ds(at + 16, 4), :] = over[0:4]
            narrow[pl.ds(at + 20, 4), :] = under[1:5]
            narrow[pl.ds(at + 24, 1), :] = under[0:1]
            narrow[pl.ds(at + 25, 1), :] = over[4:5]
    for f in range(TX):
        at = N_THETA + f * 24
        narrow[pl.ds(at, 16), :] = block.warm(f, 0, 16)
        if 0 < f < 11:
            over, under = beside(f, 4, 4, 4, YB_THERM, KB_THERM, pl.ds(0, 128), 1)
        else:
            over = under = jnp.zeros((4, 128), F32)
        narrow[pl.ds(at + 16, 4), :], narrow[pl.ds(at + 20, 4), :] = over, under
    for f in range(QX):
        at = N_PERF + f * 24
        narrow[pl.ds(at, 16), :] = block.wash(f, 0, 16)
        over, under = beside(f + 1, 4, 4, 4, YB_THERM, KB_THERM, pl.ds(128, 128), 1)
        narrow[pl.ds(at + 16, 4), :], narrow[pl.ds(at + 20, 4), :] = over, under
    narrow[pl.ds(N_PERF + QX * 24, NARROW - N_PERF - QX * 24), :] = jnp.zeros((NARROW - N_PERF - QX * 24, 128), F32)
    lane, ends = iota((ZB, 128), 1) // 8, []
    for half, shift in ((1, 8), (0, 0)):
        packed = None
        for g in range(GROUPS):
            part = rows_of(wide, narrow, g * ZB, ZB, half)
            turn = (8 * g + shift) % 128
            part = pltpu.roll(part, turn, 1) if turn else part
            packed = part if packed is None else jnp.where(lane == g, part, packed)
        ends.append(packed)
    Sender(one, two, 2).put(pl.ds(0, ZB), pl.ds(0, 128), *ends)


def unpack_z(one, two, groups, lane_after, halo):
    lane = iota((ZB, 128), 1)
    came, every = Receiver(one, two, 2), (pl.ds(0, ZB), pl.ds(0, 128))
    right, left = came.after(*every), came.before(*every)
    for k, g in enumerate(groups):
        turn = (128 + lane_after - 8 * g) % 128
        after = pltpu.roll(right, turn, 1) if turn else right
        turn = (120 - 8 * g) % 128
        before = pltpu.roll(left, turn, 1) if turn else left
        halo[pl.ds(k * ZB, ZB), :] = jnp.where(lane < 96, after, before)


def strip_cell(lane):
    return jnp.where(lane < 32, lane, jnp.where(lane < 96, lane + 192, lane - 128))


def sources(loc_h, exc_h, after_this, field, strip, spread, gather, spread_strip, gather_strip, loc_s, exc_s, loc, sems):
    loads = [
        pltpu.make_async_copy(src, dst, sems.at[k])
        for k, (src, dst) in enumerate(((loc_h, loc), (loc_h, loc_s), (exc_h, exc_s)))
    ]
    for load in loads:
        load.start()
    field[...] = jnp.zeros(field.shape, F32)
    strip[...] = jnp.zeros(strip.shape, F32)
    coord = [lax.axis_index(name) for name in AXES]
    for load in loads:
        load.wait()
    first = loc[0:1, :] - coord[0] * 8
    second = loc[1:2, :] - coord[1] * 32
    third = loc[2:3, :] - coord[2] * 256
    near = (first >= -1) & (first < 9) & (second >= -7) & (second < 39) & (third >= -7) & (third < 263)
    order = iota((1, 1024), 1)
    lane, cell = iota((1, 256), 1), strip_cell(iota((1, 128), 1))

    def place(state):
        e, keys = state
        x = loc_s[0, e] - coord[0] * 8 + 1
        y = loc_s[1, e] - coord[1] * 32
        z = loc_s[2, e] - coord[2] * 256
        y = jnp.where(y < 0, y + 48, y)
        for c in range(2):
            field[c, x, pl.ds(y, 1), :] += jnp.where(lane == z, exc_s[c, e], 0.0)
            strip[c, x, pl.ds(y, 1), :] += jnp.where(cell == z, exc_s[c, e], 0.0)
        keys = jnp.where(order == e, 1024, keys)
        return jnp.min(keys), keys

    keys = jnp.where(near, order, 1024)
    lax.while_loop(lambda state: state[0] < 1024, place, (jnp.min(keys), keys))

    def weights(cell, column, at):
        centre = cell >> 1
        beside = centre + jnp.where((cell & 1) == 1, 1, -1)
        weight = jnp.where(column == at(centre), 0.75, jnp.where(column == at(beside), 0.25, 0.0))
        return weight.astype(BF16)

    spread[...] = weights(iota((128, 256), 1), iota((128, 256), 0), lambda c: c)
    spread_strip[...] = weights(
        strip_cell(iota((256, 128), 1)),
        iota((256, 128), 0),
        lambda c: jnp.where(c < 0, c + 256, jnp.where(c < 128, c, c + 64)),
    )
    gather[...] = jnp.where(iota((256, 128), 1) == iota((256, 128), 0) >> 1, 1.0, 0.0).astype(BF16)
    centre = strip_cell(iota((128, 256), 0)) >> 1
    centre = jnp.where(centre < 0, centre + 256, centre)
    gather_strip[...] = jnp.where(iota((128, 256), 1) == centre, 1.0, 0.0).astype(BF16)


def flag(test):
    return jnp.where(test, 1.0, 0.0)


def x_flags():
    at = lax.axis_index("gx")
    return flag(at > 0), flag(at < 3)


def along_y(cells, row):
    lanes = cells.shape[1]
    centre = cells[0:24]
    lower = jnp.where(row == 20, jnp.broadcast_to(cells[24:25], (24, lanes)), pltpu.roll(centre, 1, 0))
    upper = jnp.where(row == 19, jnp.broadcast_to(cells[25:26], (24, lanes)), pltpu.roll(centre, 23, 0))
    return 0.75 * centre + 0.25 * lower, 0.75 * centre + 0.25 * upper


def coarse_rows(read, z_ok, grown):
    x_before, x_after = x_flags()
    at_y = lax.axis_index("gy")
    row = iota((32, 128), 0)
    y_ok = jnp.where(row < 16, 1.0, jnp.where((row < 20) | (row == 25), flag(at_y < 15), flag(at_y > 0)))
    inside = y_ok if z_ok is None else y_ok * z_ok
    row = iota((24, 128), 0)
    for c in range(2):
        for f in range(LX):
            x_ok = x_before if f < 2 else x_after if f >= 6 else None
            even, odd = along_y(read((c * LX + f) * 32) * (inside if x_ok is None else inside * x_ok), row)
            to = (c * LX + f) * 48
            grown[pl.ds(to, 24, 2), :] = even
            grown[pl.ds(to + 1, 24, 2), :] = odd


def relax(width, start, classes, z_ok, fine, drive, wave_t, damp_t, first, second, gain_r, gain_i, pool, emit):
    x_before, x_after = x_flags()
    at_y = lax.axis_index("gy")
    row = iota((48, width), 0)
    inside = jnp.where(row < 32, 1.0, jnp.where(row < 40, flag(at_y < 15), flag(at_y > 0)))
    if z_ok is not None:
        inside = inside * z_ok
    for c in range(2):
        for f in range(FX):
            near = c * LX + f // 2 + 1
            far = near + (1 if f % 2 else -1)
            grow = 0.75 * fine[pl.ds(near * 48, 48), :] + 0.25 * fine[pl.ds(far * 48, 48), :]
            x_ok = x_before if f < 2 else x_after if f >= 10 else None
            first[c, f] = (start((c * FX + f) * 48) + grow) * (inside if x_ok is None else inside * x_ok)

    gains_r, gains_i, damps = [], [], []
    for t in range(4):
        speed = jnp.full((8, 128), wave_t[t], F32)
        damp = jnp.full((8, 128), damp_t[t], F32)
        wave = 1.0 / (speed * speed)
        diag_r = 6.0 - wave
        diag_i = DAMPING_SHIFT * wave + damp
        modulus = diag_r * diag_r + diag_i * diag_i
        gains_r.append((RELAXATION * diag_r / modulus)[0:1, 0:1])
        gains_i.append((RELAXATION * diag_i / modulus)[0:1, 0:1])
        damps.append(damp_t[t])

    def step(cells, f, drive_f, g_r, g_i):
        sums = []
        for c in range(2):
            mid = cells[c, f]
            total = cells[c, f - 1] + cells[c, f + 1] + drive[c, drive_f]
            total = total + pltpu.roll(mid, 1, 0) + pltpu.roll(mid, 47, 0)
            sums.append((mid, total + pltpu.roll(mid, 1, 1) + pltpu.roll(mid, width - 1, 1)))
        (mid_r, sum_r), (mid_i, sum_i) = sums
        keep = 1.0 - RELAXATION
        return keep * mid_r + (g_r * sum_r + g_i * sum_i), keep * mid_i + (g_r * sum_i - g_i * sum_r)

    for f in range(CX):
        codes = classes(N_CODE + f * 48)
        x_ok = x_before if f < 1 else x_after if f >= 9 else None
        ok = inside if x_ok is None else inside * x_ok
        g_r = pick(codes, gains_r) * ok
        g_i = pick(codes, gains_i) * ok
        gain_r[f], gain_i[f] = g_r, g_i
        second[0, f], second[1, f] = step(first, f + 1, f, g_r, g_i)

    for i in range(4):
        heat = None
        for f in (2 * i, 2 * i + 1):
            new_r, new_i = step(second, f + 1, f + 1, gain_r[f + 1], gain_i[f + 1])
            emit(f, new_r, new_i)
            layer = pick(classes(N_CODE + (f + 1) * 48), damps) * (new_r * new_r + new_i * new_i)
            heat = layer if heat is None else heat + layer
        for tile in range(width // 128):
            pool[tile, pl.ds(i * 48, 48), :] = heat[:, tile * 128 : tile * 128 + 128]
    tiles = [pool[t, pl.ds(0, 96, 2), :] + pool[t, pl.ds(1, 96, 2), :] for t in range(width // 128)]
    return tiles[0] if len(tiles) == 1 else jnp.concatenate(tiles, axis=1)


def smooth_inner(wave_t, damp_t, wide, narrow, source, spread, gather, spread_strip, out, power, ends, fine_ends,
                 grown, fine, first, second, gain_r, gain_i, pool):
    coarse_rows(lambda at: narrow[pl.ds(N_COARSE + at, 32), :], None, grown)
    fine[...] = exact_dot(grown[pl.ds(0, 2 * LX * 48), :], spread[...])
    fine_ends[...] = exact_dot(grown[pl.ds(0, 2 * LX * 48), :], spread_strip[pl.ds(0, 128), :])
    lane = iota((48, 128), 1)
    for at in range(0, WIDE, 48):
        turned = pltpu.roll(wide[pl.ds(at, 48), pl.ds(128, 128)], 64, 1)
        ends[pl.ds(at, 48), :] = jnp.where(lane < 32, wide[pl.ds(at, 48), pl.ds(0, 128)], turned)

    def own(at):
        return wide[pl.ds(at, 48), :]

    def emit(f, new_r, new_i):
        out[0, f] = new_r[0:32]
        out[1, f] = new_i[0:32]

    sums = relax(256, own, own, None, fine, source, wave_t, damp_t, first, second, gain_r, gain_i, pool, emit)
    power[...] = exact_dot(sums, gather[...]) * 0.125


def smooth_ends(wave_t, damp_t, ends, z_one, z_two, source, spread, gather, power_inner, fine_ends,
                out, power, power_halo, one, two,
                halo, grown_halo, fine, first, second, gain_r, gain_i, pool):
    unpack_z(z_one, z_two, range(WARM + 1), 64, halo)
    at_z = lax.axis_index("gz")
    after_ok, before_ok = flag(at_z < 3), flag(at_z > 0)
    z_ok = jnp.where(iota((32, 128), 1) < 96, after_ok, before_ok)
    coarse_rows(lambda at: halo[pl.ds(WIDE + N_COARSE + at, 32), :], z_ok, grown_halo)
    fine[...] = fine_ends[...] + exact_dot(grown_halo[pl.ds(0, 2 * LX * 48), :], spread[pl.ds(128, 128), :])

    lane = iota((48, 128), 1)

    def strip(at):
        return jnp.where(lane < 64, ends[pl.ds(at, 48), :], halo[pl.ds(at, 48), :])

    def emit(f, new_r, new_i):
        out[0, f] = new_r[0:32]
        out[1, f] = new_i[0:32]

    z_ok = jnp.where(lane < 64, 1.0, jnp.where(lane < 96, after_ok, before_ok))
    live = jnp.where((lane < 72) | (lane >= 120), z_ok, 0.0)
    sums = relax(128, strip, strip, live, fine, source, wave_t, damp_t, first, second, gain_r, gain_i, pool, emit)
    sums = exact_dot(sums, gather[...]) * 0.125
    lane = iota((96, 128), 1)
    own = jnp.where((lane < 4) | (lane >= 124), sums[:, 0:128], power_inner[...])
    over = sums[:, 128:256]
    power[...], power_halo[...] = own, over

    def packed(first_layer):
        group, total = iota((24, 128), 1) // 16, None
        for k in range(3):
            at = (first_layer + k) * 24
            turned = pltpu.roll(over[at : at + 24], 16 * k + 8, 1)
            total = turned if total is None else jnp.where(group == k, turned, total)
        return total

    to, every = Sender(one, two, 0), pl.ds(0, 128)
    to.put(pl.ds(0, 72), every, own[24:96], own[0:72])
    to.put(pl.ds(72, 24), every, packed(1), packed(0))


class Bioheat:
    def __init__(self):
        x_before, x_after = x_flags()
        at_y, at_z = lax.axis_index("gy"), lax.axis_index("gz")
        row, col = iota((24, 256), 0), iota((24, 256), 1)
        y_ok = jnp.where(row < 16, 1.0, jnp.where(row < 20, flag(at_y < 15), flag(at_y > 0)))
        z_ok = jnp.where(col < 128, 1.0, jnp.where(col < 192, flag(at_z < 3), flag(at_z > 0)))
        inside = y_ok * z_ok
        self.edge = [inside * (x_before if f < 4 else x_after) if not 4 <= f < 8 else inside for f in range(TX)]

    def step(self, state, wash, f):
        mid = state[f]
        beside = state[f - 1] + state[f + 1]
        beside = beside + pltpu.roll(mid, 1, 0) + pltpu.roll(mid, 23, 0)
        beside = beside + pltpu.roll(mid, 1, 1) + pltpu.roll(mid, 255, 1)
        return wash[f - 1] * mid + DIFFUSION * beside

    def finish(self, cooled, heat, f):
        return (cooled + HEATING * heat) * self.edge[f]


def injury_of(warm):
    own = warm[0:16, 0:128]
    return jnp.exp(LN_PREFACTOR - ENERGY_BARRIER / (CORE_WARMTH + own))


def own_heat(power, power_halo, f):
    return jnp.concatenate([ref[pl.ds(24 * (f - 4), 24), :] for ref in (power, power_halo)], axis=1)


def bioheat_inner(narrow, z_one, z_two, power, power_halo, injury, inner, ends, begun, later, wash, dose, wave_out,
                  now, tiles, wave, sem):
    low, high = iota((32, 128), 1) < 8, iota((32, 128), 1) >= 120
    for c in range(2):
        for f in range(8):
            new = ends[c, f]
            wave[c, f, :, pl.ds(0, 128)] = jnp.where(low, new, inner[c, f, :, pl.ds(0, 128)])
            turned = pltpu.roll(new, 64, 1)
            wave[c, f, :, pl.ds(128, 128)] = jnp.where(high, turned, inner[c, f, :, pl.ds(128, 128)])
    store = pltpu.make_async_copy(wave, wave_out, sem)
    store.start()
    unpack_z(z_one, z_two, range(WARM, GROUPS), 0, tiles)
    heat = Bioheat()

    def extended(base, f):
        at = base + f * 24
        return jnp.concatenate([narrow[pl.ds(at, 24), :], tiles[pl.ds(WIDE + at - WARM * ZB, 24), :]], axis=1)

    for f in range(TX):
        now[f] = extended(N_THETA, f) * heat.edge[f]
    for f in range(QX):
        wash[f] = (1.0 - 6.0 * DIFFUSION) - extended(N_PERF, f)
    for f in range(1, TX - 1):
        new = heat.step(now, wash, f)
        if 4 <= f < 8:
            new = heat.finish(new, own_heat(power, power_halo, f), f)
            dose[f - 4] = injury[f - 4] + injury_of(new)
        begun[f] = new
    for f in (5, 6):
        new = heat.finish(heat.step(begun, wash, f), own_heat(power, power_halo, f), f)
        later[f - 5] = new
        dose[f - 4] = dose[f - 4] + injury_of(new)
    store.wait()


def bioheat(begun, later, wash, dose_in, power, power_halo, x_one, x_two, warm_out, dose_out, one, two):
    heat = Bioheat()
    came = Receiver(x_one, x_two, 0)

    def sent(side, k):
        beyond = side(pl.ds(72, 24), pl.ds(0, 128))
        beyond = jnp.where(iota((24, 128), 1) // 16 == k, beyond, 0.0)
        return jnp.concatenate([side(pl.ds(24 * k, 24), pl.ds(0, 128)), pltpu.roll(beyond, 120 - 16 * k, 1)], axis=1)

    own = [own_heat(power, power_halo, f) for f in range(4, 8)]
    heats = [None] + [sent(came.before, k) for k in range(3)] + own + [sent(came.after, k) for k in range(3)]
    for f in range(1, TX - 1):
        one[f] = begun[f] if 4 <= f < 8 else heat.finish(begun[f], heats[f], f)
    dose = [dose_in[i] for i in range(4)]
    state, other = one, two
    for turn in range(1, 4):
        for f in range(1 + turn, TX - 1 - turn):
            if turn == 1 and f in (5, 6):
                other[f] = later[f - 5]
                continue
            new = heat.finish(heat.step(state, wash, f), heats[f], f)
            if turn < 3:
                other[f] = new
            if 4 <= f < 8:
                dose[f - 4] = dose[f - 4] + injury_of(new)
                if turn == 3:
                    warm_out[f - 4] = new[0:16, 0:128]
        state, other = other, state
    for i in range(4):
        dose_out[i] = jnp.log(dose[i])


def shaped(*shape, dtype=F32):
    return jax.ShapeDtypeStruct(shape, dtype)


def call(kernel, name, in_specs, outs, scratch=(), out_specs=None, cost=2000):
    return pl.pallas_call(
        kernel,
        name=name,
        out_shape=tuple(outs),
        in_specs=in_specs,
        out_specs=tuple(out_specs or [vmem() for _ in outs]),
        scratch_shapes=list(scratch),
        cost_estimate=pl.CostEstimate(flops=cost * 1000, bytes_accessed=cost * 1000, transcendentals=0),
        compiler_params=pltpu.CompilerParams(vmem_limit_bytes=24 * 1024 * 1024),
    )


def on_device(
    acoustic_iterate,
    coarse_update,
    class_codes_volume,
    element_location,
    element_excitation,
    class_wavespeed,
    class_damping,
    washout_fraction,
    thermal_excess,
    injury_integral,
):
    def in_hbm(*arrays):
        return [pltpu.with_memory_space_constraint(array, pltpu.HBM) for array in arrays]

    *sent, perf, it, co, codes, theta = call(
        pack_x, "pack_x", [hbm()] * 5,
        [
            shaped(XB, 256),
            shaped(XB, 256),
            shaped(YB, 256),
            shaped(YB, 256),
            shaped(4, 16, 128),
            shaped(2, 8, 32, 256),
            shaped(2, 4, 16, 128),
            shaped(8, 32, 256, dtype=jnp.int32),
            shaped(4, 16, 128),
        ],
        [pltpu.VMEM((2, 128 + 8, 128), F32), pltpu.SMEM((4,), F32), pltpu.SemaphoreType.DMA((5,))],
    )(*in_hbm(washout_fraction, acoustic_iterate, coarse_update, class_codes_volume, thermal_excess))
    own = (it, co, codes, theta, perf)
    y_came = exchange(sent[2:], 1)
    x_came = exchange(sent[:2], 0)

    field, strip, *weights = call(
        sources, "sources", [hbm(), hbm(), vmem()],
        [
            shaped(2, CX, 48, 256),
            shaped(2, CX, 48, 128),
            shaped(128, 256, dtype=BF16),
            shaped(256, 128, dtype=BF16),
            shaped(256, 128, dtype=BF16),
            shaped(128, 256, dtype=BF16),
        ],
        [
            pltpu.SMEM((3, 1024), jnp.int32),
            pltpu.SMEM((2, 1024), F32),
            pltpu.VMEM((3, 1024), jnp.int32),
            pltpu.SemaphoreType.DMA((3,)),
        ],
        cost=8000,
    )(*in_hbm(element_location.T, element_excitation), perf)
    sent = call(pack_corner, "pack_corner", [vmem()] * 3, [shaped(KB, 256)] * 2)(*y_came, weights[0])
    corners = exchange(sent, 0)

    wide, narrow, *sent = call(
        pack_z, "pack_z", [vmem()] * 11,
        [shaped(WIDE, 256), shaped(NARROW, 128)] + [shaped(ZB, 128)] * 2,
    )(*own, *x_came, *y_came, *corners)
    z_came = exchange(sent, 2)

    def scratch(width):
        return [
            pltpu.VMEM((2 * LX * 48, width), F32),
            pltpu.VMEM((2, FX, 48, width), F32),
            pltpu.VMEM((2, CX, 48, width), F32),
            pltpu.VMEM((CX, 48, width), F32),
            pltpu.VMEM((CX, 48, width), F32),
            pltpu.VMEM((width // 128, 192 + 8, 128), F32),
        ]

    inner, power_inner, ends, fine_ends = call(
        smooth_inner, "smooth_inner", [smem()] * 2 + [vmem()] * 6,
        [shaped(2, 8, 32, 256), shaped(96, 128), shaped(WIDE, 128), shaped(2 * LX * 48, 128)],
        [pltpu.VMEM((2 * LX * 48 + 8, 128), F32)] + scratch(256),
    )(class_wavespeed, class_damping, wide, narrow, field, weights[0], weights[1], weights[2])
    ends, power, power_halo, *sent = call(
        smooth_ends, "smooth_ends", [smem()] * 2 + [vmem()] * 8,
        [shaped(2, 8, 32, 128)] + [shaped(96, 128)] * 4,
        [pltpu.VMEM(((WARM + 1) * ZB, 128), F32), pltpu.VMEM((2 * LX * 48 + 8, 128), F32)] + scratch(128),
    )(class_wavespeed, class_damping, ends, *z_came, strip, weights[2], weights[3], power_inner, fine_ends)
    x_came = exchange(sent, 0)

    block = shaped(TX, 24, 256)
    begun, later, wash, dose, pressure = call(
        bioheat_inner, "bioheat_inner", [vmem()] * 8,
        [block, shaped(2, 24, 256), shaped(QX, 24, 256), shaped(4, 16, 128), shaped(2, 8, 32, 256)],
        [
            pltpu.VMEM((TX, 24, 256), F32),
            pltpu.VMEM(((GROUPS - WARM) * ZB, 128), F32),
            pltpu.VMEM((2, 8, 32, 256), F32),
            pltpu.SemaphoreType.DMA,
        ],
        [vmem()] * 4 + [hbm()],
    )(narrow, *z_came, power, power_halo, injury_integral, inner, ends)
    warmth, dose = call(
        bioheat, "bioheat", [vmem()] * 8,
        [shaped(4, 16, 128), shaped(4, 16, 128)],
        [pltpu.VMEM((TX, 24, 256), F32), pltpu.VMEM((TX, 24, 256), F32)],
    )(begun, later, wash, dose, power, power_halo, *x_came)
    return pressure, warmth, dose


def solution(mesh):
    placed = (
        P(None, "gx", "gy", "gz"),
        P(None, "gx", "gy", "gz"),
        P("gx", "gy", "gz"),
        P(),
        P(),
        P(),
        P(),
        P(),
        P("gx", "gy", "gz"),
        P("gx", "gy", "gz"),
    )
    return jax.shard_map(
        on_device,
        mesh=mesh,
        in_specs=placed,
        out_specs=(P(None, "gx", "gy", "gz"), P("gx", "gy", "gz"), P("gx", "gy", "gz")),
        check_vma=False,
    )
```
